32 devices in a mesh: ctx: 4 (over y, x), fsdp: 8 (over z, core).
Axes of the slice: x: 2, y: 2, z: 4, core: 2. Of those that a mesh axis runs over, the one named last changes fastest.
Arguments:
- hidden_in: bfloat16 [3, 8, 1024, 768], P(None, 'fsdp', 'ctx'), may hold values from -6 to 6
- doc_starts: int32 [3, 8, 4], P(None, 'fsdp'), may hold values from 0 to 1023, as said below
- w_qkv: bfloat16 [768, 2304], P('fsdp'), may hold values from -0.21875 to 0.21875
- w_attn_out: bfloat16 [768, 768], P('fsdp'), may hold values from -1.75 to 1.75
- w_ff_in: bfloat16 [768, 3072], P('fsdp'), may hold values from -0.21875 to 0.21875
- w_ff_out: bfloat16 [3072, 768], P('fsdp'), may hold values from -0.109375 to 0.109375
- proj_bias: bfloat16 [4, 768], P(None, 'fsdp'), may hold values from -3 to 3
- ff_in_bias: bfloat16 [3072], P('fsdp'), may hold values from -3 to 3
- ln_gain: bfloat16 [2, 768], P(None, 'fsdp'), may hold values from 0.5 to 1.5
- ln_shift: bfloat16 [2, 768], P(None, 'fsdp'), may hold values from -2 to 2
- out_grad: bfloat16 [3, 8, 1024, 768], P(None, 'fsdp', 'ctx'), may hold values from -6 to 6
Outputs:
- layer_out: bfloat16 [3, 8, 1024, 768], P(None, 'fsdp', 'ctx')
- in_grad: bfloat16 [3, 8, 1024, 768], P(None, 'fsdp', 'ctx')
- g_w_qkv: float32 [768, 2304], P('fsdp')
- g_w_attn_out: float32 [768, 768], P('fsdp')
- g_w_ff_in: float32 [768, 3072], P('fsdp')
- g_w_ff_out: float32 [3072, 768], P('fsdp')
- g_proj_bias: float32 [4, 768], P(None, 'fsdp')
- g_ff_in_bias: float32 [3072], P('fsdp')
- g_ln_gain: float32 [2, 768], P(None, 'fsdp')
- g_ln_shift: float32 [2, 768], P(None, 'fsdp')
The draws below stay inside these ranges and needn't reach their ends.
Inputs may be any that keep to these rules, and one draw needn't show every extreme that they name: Each row doc_starts[m, s] lists the starts of the 4 documents of sequence s of micro-batch m: strictly increasing offsets, the first 0. In the first sequence of micro-batch 0 the last document holds one token.
All inputs are finite; a program needn't handle non-finite values.
Results may differ from the reference program's by a relative error of at most 0.02.
Values may be sent and summed in bfloat16 or wider, within the bound.
No kernel may reach another device: no remote copies, remote signals or barrier semaphores. Data moves between devices by JAX's collectives and lax.ppermute only.
A program may use at most 320 MiB of HBM per device.

```python
import jax
import jax.numpy as jnp
from jax import lax

D = 768
HEADS = 12
HEAD_DIM = 64
FF = 3072
MICRO = 3
NDOC = 4
SEQ = 1024
STREAMS = 8


def draw_doc_starts(key, part):
    row_total = MICRO * STREAMS
    upper = max(2 ** 30 // SEQ, 2)
    ranked = jax.random.randint(key, (row_total, SEQ - 1), 0, upper, dtype=jnp.int32) * SEQ
    ranked = ranked + jnp.arange(SEQ - 1, dtype=jnp.int32)[None, :]
    unused, picked = lax.top_k(ranked, NDOC - 1)
    picked = jnp.sort(picked.astype(jnp.int32) + 1, axis=-1)
    starts = jnp.concatenate([jnp.zeros((row_total, 1), jnp.int32), picked], axis=1)
    starts = starts.at[0, NDOC - 1].set(jnp.int32(SEQ - 1))
    return starts.reshape(MICRO, STREAMS, NDOC).astype(jnp.int32)


def level_of(stream_key, shape, split, smallest, high):
    def one(axis_at, shards_of):
        draws = jax.random.uniform(jax.random.fold_in(jax.random.fold_in(stream_key, 6), axis_at), (shards_of,), jnp.float32, smallest / len(split), high / len(split))
        return jnp.repeat(jnp.exp(draws), shape[axis_at] // shards_of).reshape((-1,) + (1,) * (len(shape) - axis_at - 1))

    gain = one(*split[0])
    for cut in split[1:]:
        gain = gain * one(*cut)
    return gain


def noise(stream_key, extent, width, most, pieces=(), held_as=jnp.bfloat16):
    result = jax.random.normal(stream_key, extent, jnp.float32) * width
    if len(pieces) > 0:
        result = level_of(stream_key, extent, pieces, -0.22, 0.18) * result
    return jnp.clip(result, min=-most, max=most).astype(held_as)


def setup_inputs(seed: int = 0) -> dict:
    seeds = jax.random.split(jax.random.key(seed), 12)
    return {
        "hidden_in": noise(seeds[0], (MICRO, STREAMS, SEQ, D), 1.0, 6.0, ((1, 8), (2, 4))),
        "doc_starts": draw_doc_starts(jax.random.fold_in(seeds[11], 71), 0),
        "w_qkv": noise(seeds[2], (D, 3 * D), D ** -0.5, 0.21875, ((0, 8),)),
        "w_attn_out": noise(seeds[3], (D, D), (D // 64) ** -0.5, 1.75, ((0, 8),)),
        "w_ff_in": noise(seeds[4], (D, FF), D ** -0.5, 0.21875, ((0, 8),)),
        "w_ff_out": noise(seeds[5], (FF, D), FF ** -0.5, 0.109375, ((0, 8),)),
        "proj_bias": noise(seeds[6], (4, D), 0.5, 3.0, ((1, 8),)),
        "ff_in_bias": noise(seeds[7], (FF,), 0.5, 3.0, ((0, 8),)),
        "ln_gain": jnp.clip(1.0 + 0.1 * jax.random.normal(seeds[8], (2, D), jnp.float32), 0.5, 1.5).astype(jnp.bfloat16),
        "ln_shift": noise(seeds[9], (2, D), 0.3, 2.0, ((1, 8),)),
        "out_grad": noise(seeds[10], (MICRO, STREAMS, SEQ, D), 1.0, 6.0, ((1, 8), (2, 4))),
    }


@jax.custom_vjp
def low(v):
    return lax.optimization_barrier(v.astype(jnp.bfloat16)).astype(jnp.float32)

@jax.custom_vjp
def low_back(v):
    return v

def low_keep(v):
    return (low(v), None)

def low_pass(kept, grad):
    return (grad,)

def back_keep(v):
    return (v, None)

def back_low(kept, grad):
    return (low(grad),)
low.defvjp(low_keep, low_pass)
low_back.defvjp(back_keep, back_low)
highest = lax.Precision.HIGHEST
norm_epsilon = 1e-12
masked_score = -1e+30

def layer_norm(values, gain_row, shift_row):
    centre = values - lax.optimization_barrier(jnp.mean(values, axis=-1, keepdims=True))
    spread = lax.optimization_barrier(jnp.mean(centre * centre, axis=-1, keepdims=True))
    return centre * lax.rsqrt(spread + norm_epsilon) * gain_row + shift_row

def segment_ids(positions, starts):
    return lax.optimization_barrier(jnp.sum((positions[:, None] >= starts[None, :]).astype(jnp.int32), axis=1))

def one_sequence(params, stream, starts):
    w_qkv, w_attn_out, w_ff_in, w_ff_out, proj_bias, ff_in_bias, ln_gain, ln_shift = params
    length = stream.shape[0]
    model_width = stream.shape[1]
    qkv_bias = jnp.concatenate([proj_bias[0], jnp.zeros_like(proj_bias[0]), proj_bias[1]])
    packed = low(low_back(jnp.dot(stream, w_qkv, precision=highest) + qkv_bias))
    query_heads = packed[:, :model_width].reshape(length, HEADS, HEAD_DIM)
    key_heads = packed[:, model_width:2 * model_width].reshape(length, HEADS, HEAD_DIM)
    value_heads = packed[:, 2 * model_width:].reshape(length, HEADS, HEAD_DIM)
    scores = low_back(jnp.einsum('qhd,khd->hqk', query_heads, key_heads, precision=highest) * HEAD_DIM ** (-0.5))
    segment = segment_ids(jnp.arange(length, dtype=jnp.int32), starts)
    same_doc = segment[:, None] == segment[None, :]
    weights = jax.nn.softmax(jnp.where(same_doc[None], scores, masked_score), axis=-1)
    mixed_heads = jnp.einsum('hqk,khd->qhd', low(weights), value_heads, precision=highest).reshape(length, model_width)
    heads_out = low(low_back(mixed_heads))
    branch = low_back(jnp.dot(heads_out, w_attn_out, precision=highest) + proj_bias[2])
    normed = layer_norm(stream + branch, ln_gain[0], ln_shift[0])
    inner_act = low_back(jnp.dot(low(normed), w_ff_in, precision=highest) + ff_in_bias)
    activated = low(jax.nn.gelu(inner_act, approximate=False))
    ff_branch = low_back(jnp.dot(activated, w_ff_out, precision=highest) + proj_bias[3])
    return layer_norm(normed + ff_branch, ln_gain[1], ln_shift[1])

def reference(hidden_in, doc_starts, w_qkv, w_attn_out, w_ff_in, w_ff_out, proj_bias, ff_in_bias, ln_gain, ln_shift, out_grad):
    params = (w_qkv.astype(jnp.float32), w_attn_out.astype(jnp.float32), w_ff_in.astype(jnp.float32), w_ff_out.astype(jnp.float32), proj_bias.astype(jnp.float32), ff_in_bias.astype(jnp.float32), ln_gain.astype(jnp.float32), ln_shift.astype(jnp.float32))
    streams = hidden_in.astype(jnp.float32).reshape(MICRO * STREAMS, SEQ, D)
    all_starts = doc_starts.reshape(MICRO * STREAMS, NDOC)
    checked = jax.checkpoint(one_sequence)

    def run_all(weights_in, stream_in):

        def apply_one(stream_pair):
            return checked(weights_in, stream_pair[0], stream_pair[1])
        return lax.map(apply_one, (stream_in, all_starts))
    outputs, pullback = jax.vjp(run_all, params, streams)
    weight_grads, stream_grad = pullback(out_grad.astype(jnp.float32).reshape(MICRO * STREAMS, SEQ, D))
    full_shape = hidden_in.shape
    return (outputs.reshape(full_shape).astype(jnp.bfloat16), stream_grad.reshape(full_shape).astype(jnp.bfloat16), weight_grads[0], weight_grads[1], weight_grads[2], weight_grads[3], weight_grads[4], weight_grads[5], weight_grads[6], weight_grads[7])
```

```python
import jax
import jax.numpy as jnp
from jax import lax
from jax.experimental import pallas as pl
from jax.experimental.pallas import tpu as pltpu
from jax.sharding import PartitionSpec as P

HEADS = 12
HEAD_DIM = 64


norm_epsilon = 1e-12
masked_score = -1e30
inv_root_two = 0.7071067811865476
inv_root_tau = 0.3989422804014327
log2_e = 1.4426950408889634

def for_sending(value):

    def short(part):
        return part.astype(jnp.bfloat16) if part.dtype == jnp.float32 else part

    return jax.tree.map(short, value)


def layer_norm_parts(values, gain_row, shift_row):
    centre = values - jnp.mean(values, axis=-1, keepdims=True)
    inverse = lax.rsqrt(jnp.mean(centre * centre, axis=-1, keepdims=True) + norm_epsilon)
    normal = centre * inverse
    return (normal * gain_row + shift_row, normal, inverse)


def norm_backward(grad_rows, normal, inverse, gain_row):
    scaled = grad_rows * gain_row
    return inverse * (
        scaled
        - jnp.mean(scaled, axis=-1, keepdims=True)
        - normal * jnp.mean(scaled * normal, axis=-1, keepdims=True)
    )


def gelu_slope(inner_act):
    return (
        0.5 * (1.0 + jax.scipy.special.erf(inner_act * inv_root_two))
        + inner_act * jnp.exp(-0.5 * inner_act * inner_act) * inv_root_tau
    )


def segment_ids(positions, starts):
    return jnp.sum((positions[:, None] >= starts[None, :]).astype(jnp.int32), axis=1)


def gather_weights(shards):
    return (
        lax.all_gather(shards[0], "fsdp", axis=0, tiled=True),
        lax.all_gather(shards[1], "fsdp", axis=0, tiled=True),
        lax.all_gather(shards[2], "fsdp", axis=0, tiled=True),
        lax.all_gather(shards[3], "fsdp", axis=0, tiled=True),
        lax.all_gather(shards[4], "fsdp", axis=1, tiled=True),
        lax.all_gather(shards[5], "fsdp", axis=0, tiled=True),
        lax.all_gather(shards[6], "fsdp", axis=1, tiled=True),
        lax.all_gather(shards[7], "fsdp", axis=1, tiled=True),
    )


def reduce_weights(terms):
    return (
        lax.psum_scatter(
            terms[0].astype(jnp.bfloat16), "fsdp", scatter_dimension=0, tiled=True
        ).astype(jnp.float32),
        lax.psum_scatter(
            terms[1].astype(jnp.bfloat16), "fsdp", scatter_dimension=0, tiled=True
        ).astype(jnp.float32),
        lax.psum_scatter(
            terms[2].astype(jnp.bfloat16), "fsdp", scatter_dimension=0, tiled=True
        ).astype(jnp.float32),
        lax.psum_scatter(
            terms[3].astype(jnp.bfloat16), "fsdp", scatter_dimension=0, tiled=True
        ).astype(jnp.float32),
        lax.psum_scatter(
            terms[4].astype(jnp.bfloat16), "fsdp", scatter_dimension=1, tiled=True
        ).astype(jnp.float32),
        lax.psum_scatter(
            terms[5].astype(jnp.bfloat16), "fsdp", scatter_dimension=0, tiled=True
        ).astype(jnp.float32),
        lax.psum_scatter(
            terms[6].astype(jnp.bfloat16), "fsdp", scatter_dimension=1, tiled=True
        ).astype(jnp.float32),
        lax.psum_scatter(
            terms[7].astype(jnp.bfloat16), "fsdp", scatter_dimension=1, tiled=True
        ).astype(jnp.float32),
    )


def forward_pass(stream, starts, whole, rank_ctx):
    w_qkv, w_attn_out, w_ff_in, w_ff_out, proj_bias, ff_in_bias, ln_gain, ln_shift = whole
    row_count = stream.shape[0]
    model_width = stream.shape[1]
    bias_float = proj_bias.astype(jnp.float32)
    qkv_bias = jnp.concatenate([bias_float[0], jnp.zeros_like(bias_float[0]), bias_float[1]])
    packed = (jnp.dot(stream, w_qkv, preferred_element_type=jnp.float32) + qkv_bias).astype(
        jnp.bfloat16
    )
    query_part = packed[:, :model_width]
    key_part = packed[:, model_width : 2 * model_width]
    value_part = packed[:, 2 * model_width :]
    key_all, value_all = (
        lax.all_gather(key_part, "ctx", axis=0, tiled=True),
        lax.all_gather(value_part, "ctx", axis=0, tiled=True),
    )
    seq_len = key_all.shape[0]
    query_seg = segment_ids(rank_ctx * row_count + jnp.arange(row_count, dtype=jnp.int32), starts)
    key_seg = segment_ids(jnp.arange(seq_len, dtype=jnp.int32), starts)
    same_doc = query_seg[:, None] == key_seg[None, :]
    query_heads = query_part.reshape(row_count, HEADS, HEAD_DIM)
    key_heads = key_all.reshape(seq_len, HEADS, HEAD_DIM)
    value_heads = value_all.reshape(seq_len, HEADS, HEAD_DIM)
    scores = jnp.einsum(
        "qhd,khd->hqk", query_heads, key_heads, preferred_element_type=jnp.float32
    ) * HEAD_DIM ** (-0.5)
    scores = jnp.where(same_doc[None], scores, masked_score)
    row_peak = jnp.max(scores, axis=-1, keepdims=True)
    exp_scores = jnp.exp(scores - row_peak)
    row_total = jnp.sum(exp_scores, axis=-1, keepdims=True)
    attn_probs = exp_scores / row_total
    log_total = row_peak + jnp.log(row_total)
    mixed = jnp.einsum(
        "hqk,khd->qhd",
        attn_probs.astype(jnp.bfloat16),
        value_heads,
        preferred_element_type=jnp.float32,
    ).reshape(row_count, model_width)
    heads_out = mixed.astype(jnp.bfloat16)
    first_sum = (
        stream.astype(jnp.float32)
        + jnp.dot(heads_out, w_attn_out, preferred_element_type=jnp.float32)
        + bias_float[2]
    )
    normed, normal_one, inverse_one = layer_norm_parts(
        first_sum, ln_gain[0].astype(jnp.float32), ln_shift[0].astype(jnp.float32)
    )
    normed_low = normed.astype(jnp.bfloat16)
    inner_act = jnp.dot(
        normed_low, w_ff_in, preferred_element_type=jnp.float32
    ) + ff_in_bias.astype(jnp.float32)
    activated = jax.nn.gelu(inner_act, approximate=False).astype(jnp.bfloat16)
    second_sum = (
        normed + jnp.dot(activated, w_ff_out, preferred_element_type=jnp.float32) + bias_float[3]
    )
    result, normal_two, inverse_two = layer_norm_parts(
        second_sum, ln_gain[1].astype(jnp.float32), ln_shift[1].astype(jnp.float32)
    )
    kept = (
        query_heads,
        key_all,
        value_all,
        same_doc,
        log_total,
        mixed,
        heads_out,
        normal_one,
        inverse_one,
        normed_low,
        inner_act,
        activated,
        normal_two,
        inverse_two,
    )
    return (result, kept)


def backward_pass(grad_rows, stream, kept, whole):
    w_qkv, w_attn_out, w_ff_in, w_ff_out, proj_bias, ff_in_bias, ln_gain, ln_shift = whole
    (
        query_heads,
        key_all,
        value_all,
        same_doc,
        log_total,
        mixed,
        heads_out,
        normal_one,
        inverse_one,
        normed_low,
        inner_act,
        activated,
        normal_two,
        inverse_two,
    ) = kept
    row_count = stream.shape[0]
    model_width = stream.shape[1]
    seq_len = key_all.shape[0]
    scale = HEAD_DIM ** (-0.5)
    d_second = norm_backward(grad_rows, normal_two, inverse_two, ln_gain[1].astype(jnp.float32))
    g_gain_two = jnp.sum(grad_rows * normal_two, axis=0)
    g_shift_two = jnp.sum(grad_rows, axis=0)
    d_ff_out = d_second.astype(jnp.bfloat16)
    g_bias_out = jnp.sum(d_ff_out.astype(jnp.float32), axis=0)
    g_w_ff_out = jnp.einsum("tf,td->fd", activated, d_ff_out, preferred_element_type=jnp.float32)
    d_activated = jnp.einsum("td,fd->tf", d_ff_out, w_ff_out, preferred_element_type=jnp.float32)
    d_inner = (d_activated * gelu_slope(inner_act)).astype(jnp.bfloat16)
    g_ff_in_bias = jnp.sum(d_inner.astype(jnp.float32), axis=0)
    g_w_ff_in = jnp.einsum("td,tf->df", normed_low, d_inner, preferred_element_type=jnp.float32)
    d_normed = d_second + jnp.einsum(
        "tf,df->td", d_inner, w_ff_in, preferred_element_type=jnp.float32
    )
    d_first = norm_backward(d_normed, normal_one, inverse_one, ln_gain[0].astype(jnp.float32))
    g_gain_one = jnp.sum(d_normed * normal_one, axis=0)
    g_shift_one = jnp.sum(d_normed, axis=0)
    d_branch = d_first.astype(jnp.bfloat16)
    g_bias_attn = jnp.sum(d_branch.astype(jnp.float32), axis=0)
    g_w_attn_out = jnp.einsum("tc,td->cd", heads_out, d_branch, preferred_element_type=jnp.float32)
    d_heads = jnp.einsum(
        "td,cd->tc", d_branch, w_attn_out, preferred_element_type=jnp.float32
    ).astype(jnp.bfloat16)
    d_heads_split = d_heads.reshape(row_count, HEADS, HEAD_DIM)
    key_heads = key_all.reshape(seq_len, HEADS, HEAD_DIM)
    value_heads = value_all.reshape(seq_len, HEADS, HEAD_DIM)
    scores = (
        jnp.einsum("qhd,khd->hqk", query_heads, key_heads, preferred_element_type=jnp.float32)
        * scale
    )
    scores = jnp.where(same_doc[None], scores, masked_score)
    attn_probs = jnp.exp(scores - log_total)
    d_probs = jnp.einsum(
        "qhd,khd->hqk", d_heads_split, value_heads, preferred_element_type=jnp.float32
    )
    row_dot = jnp.sum(attn_probs * d_probs, axis=-1)
    d_scores = (attn_probs * (d_probs - row_dot[:, :, None])).astype(jnp.bfloat16)
    d_query = (
        (
            jnp.einsum("hqk,khd->qhd", d_scores, key_heads, preferred_element_type=jnp.float32)
            * scale
        )
        .reshape(row_count, model_width)
        .astype(jnp.bfloat16)
    )
    probs_low = attn_probs.astype(jnp.bfloat16)
    d_key_rows = (
        jnp.einsum("hqk,qhd->khd", d_scores, query_heads, preferred_element_type=jnp.float32)
        * scale
    )
    d_value_rows = jnp.einsum(
        "hqk,qhd->khd", probs_low, d_heads_split, preferred_element_type=jnp.float32
    )
    d_key_value = lax.psum_scatter(
        jnp.concatenate(
            [
                d_key_rows.reshape(lax.axis_size("ctx") * row_count, model_width),
                d_value_rows.reshape(lax.axis_size("ctx") * row_count, model_width),
            ],
            axis=1,
        ).astype(jnp.bfloat16),
        "ctx",
        scatter_dimension=0,
        tiled=True,
    )
    d_packed = jnp.concatenate([d_query, d_key_value], axis=1)
    g_bias_query = jnp.sum(d_query.astype(jnp.float32), axis=0)
    g_bias_value = jnp.sum(d_key_value[:, model_width:].astype(jnp.float32), axis=0)
    g_w_qkv = jnp.einsum("td,te->de", stream, d_packed, preferred_element_type=jnp.float32)
    d_stream = d_first + jnp.einsum(
        "te,de->td", d_packed, w_qkv, preferred_element_type=jnp.float32
    )
    terms = (
        g_w_qkv,
        g_w_attn_out,
        g_w_ff_in,
        g_w_ff_out,
        jnp.stack([g_bias_query, g_bias_value, g_bias_attn, g_bias_out]),
        g_ff_in_bias,
        jnp.stack([g_gain_one, g_gain_two]),
        jnp.stack([g_shift_one, g_shift_two]),
    )
    return (d_stream.astype(jnp.bfloat16), terms)


def on_device(
    hidden_in,
    doc_starts,
    w_qkv,
    w_attn_out,
    w_ff_in,
    w_ff_out,
    proj_bias,
    ff_in_bias,
    ln_gain,
    ln_shift,
    out_grad,
):
    rank_ctx = lax.axis_index("ctx")
    shards = (w_qkv, w_attn_out, w_ff_in, w_ff_out, proj_bias, ff_in_bias, ln_gain, ln_shift)
    output_list = []
    grad_list = []
    running = None
    for micro_step in range(hidden_in.shape[0]):
        stream = hidden_in[micro_step, 0]
        starts = doc_starts[micro_step, 0]
        forward_weights = gather_weights(shards)
        result, kept = forward_pass(stream, starts, forward_weights, rank_ctx)
        backward_weights = gather_weights(shards)
        d_stream, terms = backward_pass(
            out_grad[micro_step, 0].astype(jnp.float32), stream, kept, backward_weights
        )
        if micro_step == 0:
            running = terms
        else:
            running = jax.tree.map(jnp.add, running, terms)
        output_list.append(result.astype(jnp.bfloat16)[None, None])
        grad_list.append(d_stream[None, None])
    running = reduce_weights(running)
    summed = jax.tree.map(
        lambda part: part.astype(jnp.float32), lax.psum(for_sending(running), "ctx")
    )
    return (
        jnp.concatenate(output_list, axis=0),
        jnp.concatenate(grad_list, axis=0),
        summed[0],
        summed[1],
        summed[2],
        summed[3],
        summed[4],
        summed[5],
        summed[6],
        summed[7],
    )

f32 = jnp.float32
bf16 = jnp.bfloat16


def mm(a, b, dims=((1,), (0,))):
    return lax.dot_general(a, b, (dims, ((), ())), preferred_element_type=f32)


def attention_forward_body(heads, query_ref, all_ref, seg_col_ref, seg_row_ref, out_ref, lse_ref):
    width = heads * HEAD_DIM
    bias = jnp.where(seg_col_ref[:, :1] == seg_row_ref[:1, :], 0.0, masked_score)
    for h in range(heads):
        at = h * HEAD_DIM
        query = query_ref[:, at : at + HEAD_DIM]
        key = all_ref[:, width + at : width + at + HEAD_DIM]
        value = all_ref[:, 2 * width + at : 2 * width + at + HEAD_DIM]
        scores = mm(key, query, ((1,), (1,))) * (HEAD_DIM ** (-0.5) * log2_e) + bias
        peak = jnp.max(scores, axis=0, keepdims=True)
        probs = jnp.exp2(scores - peak)
        total = jnp.sum(probs, axis=0, keepdims=True)
        mixed = mm(value, probs.astype(bf16), ((0,), (0,))) / total
        out_ref[:, at : at + HEAD_DIM] = mixed.T.astype(bf16)
        lse_ref[h : h + 1, :] = peak + jnp.log2(total)


def attention_backward_body(
    heads,
    query_ref,
    all_ref,
    grad_ref,
    lse_ref,
    seg_col_ref,
    seg_row_ref,
    out_ref,
    key_acc,
    value_acc,
):
    width = heads * HEAD_DIM
    step = pl.program_id(0)
    rows = query_ref.shape[0]
    scale = HEAD_DIM ** (-0.5)

    @pl.when(step == 0)
    def _():
        key_acc[...] = jnp.zeros_like(key_acc)
        value_acc[...] = jnp.zeros_like(value_acc)

    bias = jnp.where(seg_col_ref[:, :1] == seg_row_ref[:1, :], 0.0, masked_score)
    for h in range(heads):
        at = h * HEAD_DIM
        query = query_ref[:, at : at + HEAD_DIM]
        grad = grad_ref[:, at : at + HEAD_DIM]
        key = all_ref[:, width + at : width + at + HEAD_DIM]
        value = all_ref[:, 2 * width + at : 2 * width + at + HEAD_DIM]
        scores = mm(key, query, ((1,), (1,))) * (scale * log2_e) + bias
        probs = jnp.exp2(scores - lse_ref[h : h + 1, :])
        d_probs = mm(value, grad, ((1,), (1,)))
        row_dot = jnp.sum(probs * d_probs, axis=0, keepdims=True)
        d_scores = (probs * (d_probs - row_dot)).astype(bf16)
        value_acc[h] += mm(probs.astype(bf16), grad)
        key_acc[h] += mm(d_scores, query)
        d_query = mm(key, d_scores, ((0,), (0,))) * scale
        out_ref[pl.ds(pl.multiple_of(step * rows, rows), rows), at : at + HEAD_DIM] = (
            d_query.T.astype(bf16)
        )

    @pl.when(step == pl.num_programs(0) - 1)
    def _():
        for h in range(heads):
            at = h * HEAD_DIM
            out_ref[:, width + at : width + at + HEAD_DIM] = (key_acc[h] * scale).astype(bf16)
            out_ref[:, 2 * width + at : 2 * width + at + HEAD_DIM] = value_acc[h].astype(bf16)


def attention_forward(qkv, seg_col, seg_row, rows):
    length, triple = qkv.shape
    width = triple // 3
    heads = width // HEAD_DIM

    def body(*refs):
        attention_forward_body(heads, *refs)

    return pl.pallas_call(
        body,
        grid=(length // rows,),
        in_specs=[
            pl.BlockSpec((rows, triple), lambda i: (i, 0)),
            pl.BlockSpec((length, triple), lambda i: (0, 0)),
            pl.BlockSpec((length, 128), lambda i: (0, 0)),
            pl.BlockSpec((8, rows), lambda i: (0, i)),
        ],
        out_specs=[
            pl.BlockSpec((rows, width), lambda i: (i, 0)),
            pl.BlockSpec((8, rows), lambda i: (0, i)),
        ],
        out_shape=[
            jax.ShapeDtypeStruct((length, width), bf16),
            jax.ShapeDtypeStruct((8, length), f32),
        ],
        name="attention_forward",
        cost_estimate=pl.CostEstimate(
            flops=16 * heads * length * length * HEAD_DIM,
            transcendentals=heads * length * length,
            bytes_accessed=12 * length * triple,
        ),
    )(qkv, qkv, seg_col, seg_row)


def attention_backward(qkv, grad, lse, seg_col, seg_row, rows):
    length, triple = qkv.shape
    width = triple // 3
    heads = width // HEAD_DIM

    def body(*refs):
        attention_backward_body(heads, *refs)

    return pl.pallas_call(
        body,
        grid=(length // rows,),
        in_specs=[
            pl.BlockSpec((rows, triple), lambda i: (i, 0)),
            pl.BlockSpec((length, triple), lambda i: (0, 0)),
            pl.BlockSpec((rows, width), lambda i: (i, 0)),
            pl.BlockSpec((8, rows), lambda i: (0, i)),
            pl.BlockSpec((length, 128), lambda i: (0, 0)),
            pl.BlockSpec((8, rows), lambda i: (0, i)),
        ],
        out_specs=pl.BlockSpec((length, triple), lambda i: (0, 0)),
        out_shape=jax.ShapeDtypeStruct((length, triple), bf16),
        scratch_shapes=[
            pltpu.VMEM((heads, length, HEAD_DIM), f32),
            pltpu.VMEM((heads, length, HEAD_DIM), f32),
        ],
        name="attention_backward",
        cost_estimate=pl.CostEstimate(
            flops=40 * heads * length * length * HEAD_DIM,
            transcendentals=heads * length * length,
            bytes_accessed=18 * length * triple,
        ),
    )(qkv, qkv, grad, lse, seg_col, seg_row)


def from_peer(value, peer):
    return lax.ppermute(value, "ctx", [(r, r ^ peer) for r in range(4)])


def from_core(value):
    return lax.ppermute(value, "fsdp", [(f, f ^ 1) for f in range(lax.axis_size("fsdp"))])


def pick(stack, index):
    return lax.dynamic_index_in_dim(stack, index, 0, keepdims=False)


def by_rank(value, me):
    stack = jnp.stack([value] + [from_peer(value, j) for j in (1, 2, 3)])
    return [pick(stack, me ^ r) for r in range(4)]


def add_sent(own, received):
    return (own.astype(f32) + received.astype(f32)).astype(bf16)


def line_scatter(parts):
    chips = parts.shape[0]
    z = lax.axis_index("fsdp") // 2
    up = jnp.zeros_like(parts[0])
    down = up
    for s in range(1, chips):
        sent = add_sent(pick(parts, jnp.clip(z + chips - s, 0, chips - 1)), up)
        up = lax.ppermute(
            sent, "fsdp", [(f, f + 2) for f in range(2 * chips - 2) if f // 2 < s]
        )
        sent = add_sent(pick(parts, jnp.clip(z - chips + s, 0, chips - 1)), down)
        down = lax.ppermute(
            sent, "fsdp", [(f, f - 2) for f in range(2, 2 * chips) if f // 2 > chips - 1 - s]
        )
    return pick(parts, z).astype(f32) + up.astype(f32) + down.astype(f32)


def reduce_everywhere(partial, me, axis):
    xx, y = me % 2, me // 2
    core = lax.axis_index("fsdp") % 2
    pairs = partial.reshape((partial.shape[0] // 2, 2) + partial.shape[1:])
    kept = lax.dynamic_index_in_dim(pairs, core, 1, keepdims=False)
    other = lax.dynamic_index_in_dim(pairs, 1 - core, 1, keepdims=False)
    held = add_sent(kept, from_core(other.astype(bf16)))

    def halves(value):
        return jnp.stack(jnp.split(value, 2, axis=axis))

    first, second = jnp.split(held, 2, axis=axis)
    first, second = halves(first), halves(second)
    first = add_sent(pick(first, xx), from_peer(pick(first, 1 - xx), 1))
    second = add_sent(pick(second, y), from_peer(pick(second, 1 - y), 2))
    first, second = halves(first), halves(second)
    first = add_sent(pick(first, y), from_peer(pick(first, 1 - y), 2))
    second = add_sent(pick(second, xx), from_peer(pick(second, 1 - xx), 1))
    mine = line_scatter(jnp.concatenate([first, second], axis=axis)).astype(bf16)
    ranks = by_rank(mine, me)
    first, second = zip(*[jnp.split(r, 2, axis=axis - 1) for r in ranks])
    order = [first[2 * b + a] for a in (0, 1) for b in (0, 1)] + list(second)
    return jnp.concatenate(order, axis=axis - 1).astype(f32)


def on_plane(
    hidden_in,
    doc_starts,
    w_qkv,
    w_attn_out,
    w_ff_in,
    w_ff_out,
    proj_bias,
    ff_in_bias,
    ln_gain,
    ln_shift,
    out_grad,
):
    me = lax.axis_index("ctx")
    micro, _, rows, model_width = hidden_in.shape
    shards = lax.axis_size("fsdp")
    part = model_width // 4
    inner_width = w_ff_in.shape[1]
    streams = [hidden_in[m, 0] for m in range(micro)]

    own_columns = jnp.concatenate(
        [
            lax.dynamic_slice_in_dim(w_qkv, b * model_width + me * part, part, 1)
            for b in range(3)
        ],
        axis=1,
    )
    small = jnp.concatenate([v.reshape(-1) for v in (proj_bias, ff_in_bias, ln_gain, ln_shift)])
    first_rows = jnp.concatenate([own_columns, small.reshape(-1, 3 * part)], axis=0)
    first_all = lax.all_gather(first_rows, "fsdp", axis=0)
    w_own = first_all[:, : w_qkv.shape[0]].reshape(model_width, 3 * part)
    small_all = first_all[:, w_qkv.shape[0] :].reshape(shards, -1).astype(f32)
    at = 0
    wholes = []
    for count, length in (
        (4, proj_bias.shape[1]),
        (1, ff_in_bias.shape[0]),
        (2, ln_gain.shape[1]),
        (2, ln_shift.shape[1]),
    ):
        piece = small_all[:, at : at + count * length].reshape(shards, count, length)
        wholes.append(piece.transpose(1, 0, 2).reshape(count, shards * length))
        at += count * length
    bias_all, inner_bias, gains, shifts = wholes
    qkv_bias = jnp.concatenate(
        [
            lax.dynamic_slice_in_dim(bias_all[0], me * part, part),
            jnp.zeros((part,), f32),
            lax.dynamic_slice_in_dim(bias_all[1], me * part, part),
        ]
    )

    arrived = [[x] + [from_peer(x, j) for j in (1, 2, 3)] for x in streams]
    w_out_all = lax.all_gather(w_attn_out, "fsdp", axis=0, tiled=True)
    w_in_all = lax.all_gather(w_ff_in, "fsdp", axis=0, tiled=True)
    w_last_all = lax.all_gather(w_ff_out, "fsdp", axis=0, tiled=True)
    groups = w_out_all.reshape(4, part, model_width)
    w_out_rel = jnp.concatenate([pick(groups, me ^ j) for j in range(4)], axis=0)

    positions = jnp.concatenate(
        [(me ^ j) * rows + jnp.arange(rows, dtype=jnp.int32) for j in range(4)]
    )
    sequence = []
    pieces = []
    for m in range(micro):
        seg = jnp.sum(
            (positions[:, None] >= doc_starts[m, 0][None, :]).astype(jnp.int32), axis=1
        ).astype(f32)
        seg_col = jnp.broadcast_to(seg[:, None], (4 * rows, 128))
        seg_row = jnp.broadcast_to(seg[None, :], (8, 4 * rows))
        x_all = jnp.concatenate(arrived[m], axis=0)
        qkv = (mm(x_all, w_own) + qkv_bias).astype(bf16)
        mixed, lse = attention_forward(qkv, seg_col, seg_row, rows)
        sequence.append((x_all, qkv, lse, seg_col, seg_row))
        pieces.append(
            jnp.concatenate(
                [mixed[:rows]]
                + [from_peer(mixed[j * rows : (j + 1) * rows], j) for j in (1, 2, 3)],
                axis=1,
            )
        )
    heads_out = jnp.concatenate(pieces, axis=0)
    stream = jnp.concatenate(streams, axis=0)

    first_sum = stream.astype(f32) + mm(heads_out, w_out_rel) + bias_all[2]
    normed, normal_one, inverse_one = layer_norm_parts(first_sum, gains[0], shifts[0])
    normed_low = normed.astype(bf16)
    inner_act = mm(normed_low, w_in_all) + inner_bias[0]
    activated = jax.nn.gelu(inner_act, approximate=False).astype(bf16)
    second_sum = normed + mm(activated, w_last_all) + bias_all[3]
    result, normal_two, inverse_two = layer_norm_parts(second_sum, gains[1], shifts[1])

    grad_rows = jnp.concatenate([out_grad[m, 0] for m in range(micro)], axis=0).astype(f32)
    d_second = norm_backward(grad_rows, normal_two, inverse_two, gains[1])
    g_gain_two = jnp.sum(grad_rows * normal_two, axis=0)
    g_shift_two = jnp.sum(grad_rows, axis=0)
    d_ff_out = d_second.astype(bf16)
    g_bias_out = jnp.sum(d_ff_out.astype(f32), axis=0)
    g_w_ff_out = mm(activated, d_ff_out, ((0,), (0,))).astype(bf16)
    g_last = reduce_everywhere(g_w_ff_out.reshape(shards, -1, model_width), me, 1)
    d_inner = (mm(d_ff_out, w_last_all, ((1,), (1,))) * gelu_slope(inner_act)).astype(bf16)
    g_ff_in_bias = jnp.sum(d_inner.astype(f32), axis=0)
    g_w_ff_in = mm(normed_low, d_inner, ((0,), (0,))).astype(bf16)
    g_in = reduce_everywhere(g_w_ff_in.reshape(shards, -1, inner_width), me, 2)
    d_normed = d_second + mm(d_inner, w_in_all, ((1,), (1,)))
    d_first = norm_backward(d_normed, normal_one, inverse_one, gains[0])
    g_gain_one = jnp.sum(d_normed * normal_one, axis=0)
    g_shift_one = jnp.sum(d_normed, axis=0)
    d_branch = d_first.astype(bf16)
    g_bias_attn = jnp.sum(d_branch.astype(f32), axis=0)
    d_heads = mm(d_branch, w_out_rel, ((1,), (1,))).astype(bf16)
    g_out_rel = mm(heads_out, d_branch, ((0,), (0,))).astype(bf16).reshape(4, part, model_width)
    g_w_out = jnp.concatenate([pick(g_out_rel, me ^ r) for r in range(4)], axis=0)
    small_grads = [
        v.reshape(-1, shards, v.shape[-1] // shards).transpose(1, 0, 2).reshape(shards, -1)
        for v in (
            jnp.stack([g_bias_attn, g_bias_out]),
            g_ff_in_bias[None],
            jnp.stack([g_gain_one, g_gain_two]),
            jnp.stack([g_shift_one, g_shift_two]),
        )
    ]
    small_flat = jnp.concatenate(small_grads, axis=1)
    small_count = small_flat.shape[1]
    small_rows = -(-small_count // model_width)
    small_flat = jnp.pad(small_flat, ((0, 0), (0, small_rows * model_width - small_count)))
    tail = jnp.concatenate(
        [
            g_w_out.reshape(shards, -1, model_width),
            small_flat.astype(bf16).reshape(shards, small_rows, model_width),
        ],
        axis=1,
    )
    tail_sum = lax.psum(lax.psum_scatter(tail, "fsdp", scatter_dimension=0), "ctx").astype(f32)

    grads = []
    own_grad = None
    own_bias = None
    for m in range(micro):
        x_all, qkv, lse, seg_col, seg_row = sequence[m]
        block = d_heads[m * rows : (m + 1) * rows]
        d_mixed = jnp.concatenate(
            [block[:, :part]]
            + [from_peer(block[:, j * part : (j + 1) * part], j) for j in (1, 2, 3)],
            axis=0,
        )
        d_qkv = attention_backward(qkv, d_mixed, lse, seg_col, seg_row, rows)
        d_x = mm(d_qkv, w_own, ((1,), (1,))).astype(bf16)
        total = d_first[m * rows : (m + 1) * rows] + d_x[:rows].astype(f32)
        for j in (1, 2, 3):
            total = total + from_peer(d_x[j * rows : (j + 1) * rows], j).astype(f32)
        grads.append(total.astype(bf16)[None, None])
        term = mm(x_all, d_qkv, ((0,), (0,)))
        bias_term = jnp.sum(d_qkv.astype(f32), axis=0)
        own_grad = term if own_grad is None else own_grad + term
        own_bias = bias_term if own_bias is None else own_bias + bias_term
    own_all = jnp.concatenate(
        [
            own_grad.astype(bf16).reshape(shards, -1, 3 * part),
            jnp.broadcast_to(own_bias.astype(bf16), (shards, 1, 3 * part)),
        ],
        axis=1,
    )
    own_sum = lax.psum_scatter(own_all, "fsdp", scatter_dimension=0)
    own_ranks = by_rank(own_sum, me)
    whole = jnp.stack(own_ranks).astype(f32)
    g_qkv = (
        whole[:, :-1].reshape(4, -1, 3, part).transpose(1, 2, 0, 3).reshape(-1, 3 * model_width)
    )
    both = whole[:, -1].reshape(4, 3, part).transpose(1, 0, 2).reshape(3, model_width)
    own_shard = lax.axis_index("fsdp") * proj_bias.shape[1]
    both = lax.dynamic_slice_in_dim(both, own_shard, proj_bias.shape[1], 1)

    g_out = tail_sum[: w_attn_out.shape[0]]
    flat = tail_sum[w_attn_out.shape[0] :].reshape(-1)
    narrow = proj_bias.shape[1]
    bias_pair = flat[: 2 * narrow].reshape(2, narrow)
    at = 2 * narrow
    inner_bias_grad = flat[at : at + ff_in_bias.shape[0]]
    at += ff_in_bias.shape[0]
    gain_grad = flat[at : at + 2 * narrow].reshape(2, narrow)
    at += 2 * narrow
    shift_grad = flat[at : at + 2 * narrow].reshape(2, narrow)
    bias_grad = jnp.concatenate([both[0:1], both[2:3], bias_pair], axis=0)
    return (
        result.astype(bf16).reshape(out_grad.shape),
        jnp.concatenate(grads, axis=0),
        g_qkv,
        g_out,
        g_in,
        g_last,
        bias_grad,
        inner_bias_grad,
        gain_grad,
        shift_grad,
    )


def solution(mesh):
    plane = mesh.shape["ctx"] == 4 and mesh.shape["fsdp"] == 8
    return jax.shard_map(
        on_plane if plane else on_device,
        mesh=mesh,
        in_specs=(
            P(None, "fsdp", "ctx", None),
            P(None, "fsdp", None),
            P("fsdp", None),
            P("fsdp", None),
            P("fsdp", None),
            P("fsdp", None),
            P(None, "fsdp"),
            P("fsdp"),
            P(None, "fsdp"),
            P(None, "fsdp"),
            P(None, "fsdp", "ctx", None),
        ),
        out_specs=(
            P(None, "fsdp", "ctx", None),
            P(None, "fsdp", "ctx", None),
            P("fsdp", None),
            P("fsdp", None),
            P("fsdp", None),
            P("fsdp", None),
            P(None, "fsdp"),
            P("fsdp"),
            P(None, "fsdp"),
            P(None, "fsdp"),
        ),
        check_vma=False,
    )
```

```python
import jax
import jax.numpy as jnp
from jax import lax
from jax.experimental import pallas as pl
from jax.experimental.pallas import tpu as pltpu
from jax.sharding import PartitionSpec as P

HEADS = 12
HEAD_DIM = 64


norm_epsilon = 1e-12
masked_score = -1e30
inv_root_two = 0.7071067811865476
inv_root_tau = 0.3989422804014327
log2_e = 1.4426950408889634

def for_sending(value):

    def short(part):
        return part.astype(jnp.bfloat16) if part.dtype == jnp.float32 else part

    return jax.tree.map(short, value)


def layer_norm_parts(values, gain_row, shift_row):
    centre = values - jnp.mean(values, axis=-1, keepdims=True)
    inverse = lax.rsqrt(jnp.mean(centre * centre, axis=-1, keepdims=True) + norm_epsilon)
    normal = centre * inverse
    return (normal * gain_row + shift_row, normal, inverse)


def norm_backward(grad_rows, normal, inverse, gain_row):
    scaled = grad_rows * gain_row
    return inverse * (
        scaled
        - jnp.mean(scaled, axis=-1, keepdims=True)
        - normal * jnp.mean(scaled * normal, axis=-1, keepdims=True)
    )


def gelu_slope(inner_act):
    return (
        0.5 * (1.0 + jax.scipy.special.erf(inner_act * inv_root_two))
        + inner_act * jnp.exp(-0.5 * inner_act * inner_act) * inv_root_tau
    )


def segment_ids(positions, starts):
    return jnp.sum((positions[:, None] >= starts[None, :]).astype(jnp.int32), axis=1)


def gather_weights(shards):
    return (
        lax.all_gather(shards[0], "fsdp", axis=0, tiled=True),
        lax.all_gather(shards[1], "fsdp", axis=0, tiled=True),
        lax.all_gather(shards[2], "fsdp", axis=0, tiled=True),
        lax.all_gather(shards[3], "fsdp", axis=0, tiled=True),
        lax.all_gather(shards[4], "fsdp", axis=1, tiled=True),
        lax.all_gather(shards[5], "fsdp", axis=0, tiled=True),
        lax.all_gather(shards[6], "fsdp", axis=1, tiled=True),
        lax.all_gather(shards[7], "fsdp", axis=1, tiled=True),
    )


def reduce_weights(terms):
    return (
        lax.psum_scatter(
            terms[0].astype(jnp.bfloat16), "fsdp", scatter_dimension=0, tiled=True
        ).astype(jnp.float32),
        lax.psum_scatter(
            terms[1].astype(jnp.bfloat16), "fsdp", scatter_dimension=0, tiled=True
        ).astype(jnp.float32),
        lax.psum_scatter(
            terms[2].astype(jnp.bfloat16), "fsdp", scatter_dimension=0, tiled=True
        ).astype(jnp.float32),
        lax.psum_scatter(
            terms[3].astype(jnp.bfloat16), "fsdp", scatter_dimension=0, tiled=True
        ).astype(jnp.float32),
        lax.psum_scatter(
            terms[4].astype(jnp.bfloat16), "fsdp", scatter_dimension=1, tiled=True
        ).astype(jnp.float32),
        lax.psum_scatter(
            terms[5].astype(jnp.bfloat16), "fsdp", scatter_dimension=0, tiled=True
        ).astype(jnp.float32),
        lax.psum_scatter(
            terms[6].astype(jnp.bfloat16), "fsdp", scatter_dimension=1, tiled=True
        ).astype(jnp.float32),
        lax.psum_scatter(
            terms[7].astype(jnp.bfloat16), "fsdp", scatter_dimension=1, tiled=True
        ).astype(jnp.float32),
    )


def forward_pass(stream, starts, whole, rank_ctx):
    w_qkv, w_attn_out, w_ff_in, w_ff_out, proj_bias, ff_in_bias, ln_gain, ln_shift = whole
    row_count = stream.shape[0]
    model_width = stream.shape[1]
    bias_float = proj_bias.astype(jnp.float32)
    qkv_bias = jnp.concatenate([bias_float[0], jnp.zeros_like(bias_float[0]), bias_float[1]])
    packed = (jnp.dot(stream, w_qkv, preferred_element_type=jnp.float32) + qkv_bias).astype(
        jnp.bfloat16
    )
    query_part = packed[:, :model_width]
    key_part = packed[:, model_width : 2 * model_width]
    value_part = packed[:, 2 * model_width :]
    key_all, value_all = (
        lax.all_gather(key_part, "ctx", axis=0, tiled=True),
        lax.all_gather(value_part, "ctx", axis=0, tiled=True),
    )
    seq_len = key_all.shape[0]
    query_seg = segment_ids(rank_ctx * row_count + jnp.arange(row_count, dtype=jnp.int32), starts)
    key_seg = segment_ids(jnp.arange(seq_len, dtype=jnp.int32), starts)
    same_doc = query_seg[:, None] == key_seg[None, :]
    query_heads = query_part.reshape(row_count, HEADS, HEAD_DIM)
    key_heads = key_all.reshape(seq_len, HEADS, HEAD_DIM)
    value_heads = value_all.reshape(seq_len, HEADS, HEAD_DIM)
    scores = jnp.einsum(
        "qhd,khd->hqk", query_heads, key_heads, preferred_element_type=jnp.float32
    ) * HEAD_DIM ** (-0.5)
    scores = jnp.where(same_doc[None], scores, masked_score)
    row_peak = jnp.max(scores, axis=-1, keepdims=True)
    exp_scores = jnp.exp(scores - row_peak)
    row_total = jnp.sum(exp_scores, axis=-1, keepdims=True)
    attn_probs = exp_scores / row_total
    log_total = row_peak + jnp.log(row_total)
    mixed = jnp.einsum(
        "hqk,khd->qhd",
        attn_probs.astype(jnp.bfloat16),
        value_heads,
        preferred_element_type=jnp.float32,
    ).reshape(row_count, model_width)
    heads_out = mixed.astype(jnp.bfloat16)
    first_sum = (
        stream.astype(jnp.float32)
        + jnp.dot(heads_out, w_attn_out, preferred_element_type=jnp.float32)
        + bias_float[2]
    )
    normed, normal_one, inverse_one = layer_norm_parts(
        first_sum, ln_gain[0].astype(jnp.float32), ln_shift[0].astype(jnp.float32)
    )
    normed_low = normed.astype(jnp.bfloat16)
    inner_act = jnp.dot(
        normed_low, w_ff_in, preferred_element_type=jnp.float32
    ) + ff_in_bias.astype(jnp.float32)
    activated = jax.nn.gelu(inner_act, approximate=False).astype(jnp.bfloat16)
    second_sum = (
        normed + jnp.dot(activated, w_ff_out, preferred_element_type=jnp.float32) + bias_float[3]
    )
    result, normal_two, inverse_two = layer_norm_parts(
        second_sum, ln_gain[1].astype(jnp.float32), ln_shift[1].astype(jnp.float32)
    )
    kept = (
        query_heads,
        key_all,
        value_all,
        same_doc,
        log_total,
        mixed,
        heads_out,
        normal_one,
        inverse_one,
        normed_low,
        inner_act,
        activated,
        normal_two,
        inverse_two,
    )
    return (result, kept)


def backward_pass(grad_rows, stream, kept, whole):
    w_qkv, w_attn_out, w_ff_in, w_ff_out, proj_bias, ff_in_bias, ln_gain, ln_shift = whole
    (
        query_heads,
        key_all,
        value_all,
        same_doc,
        log_total,
        mixed,
        heads_out,
        normal_one,
        inverse_one,
        normed_low,
        inner_act,
        activated,
        normal_two,
        inverse_two,
    ) = kept
    row_count = stream.shape[0]
    model_width = stream.shape[1]
    seq_len = key_all.shape[0]
    scale = HEAD_DIM ** (-0.5)
    d_second = norm_backward(grad_rows, normal_two, inverse_two, ln_gain[1].astype(jnp.float32))
    g_gain_two = jnp.sum(grad_rows * normal_two, axis=0)
    g_shift_two = jnp.sum(grad_rows, axis=0)
    d_ff_out = d_second.astype(jnp.bfloat16)
    g_bias_out = jnp.sum(d_ff_out.astype(jnp.float32), axis=0)
    g_w_ff_out = jnp.einsum("tf,td->fd", activated, d_ff_out, preferred_element_type=jnp.float32)
    d_activated = jnp.einsum("td,fd->tf", d_ff_out, w_ff_out, preferred_element_type=jnp.float32)
    d_inner = (d_activated * gelu_slope(inner_act)).astype(jnp.bfloat16)
    g_ff_in_bias = jnp.sum(d_inner.astype(jnp.float32), axis=0)
    g_w_ff_in = jnp.einsum("td,tf->df", normed_low, d_inner, preferred_element_type=jnp.float32)
    d_normed = d_second + jnp.einsum(
        "tf,df->td", d_inner, w_ff_in, preferred_element_type=jnp.float32
    )
    d_first = norm_backward(d_normed, normal_one, inverse_one, ln_gain[0].astype(jnp.float32))
    g_gain_one = jnp.sum(d_normed * normal_one, axis=0)
    g_shift_one = jnp.sum(d_normed, axis=0)
    d_branch = d_first.astype(jnp.bfloat16)
    g_bias_attn = jnp.sum(d_branch.astype(jnp.float32), axis=0)
    g_w_attn_out = jnp.einsum("tc,td->cd", heads_out, d_branch, preferred_element_type=jnp.float32)
    d_heads = jnp.einsum(
        "td,cd->tc", d_branch, w_attn_out, preferred_element_type=jnp.float32
    ).astype(jnp.bfloat16)
    d_heads_split = d_heads.reshape(row_count, HEADS, HEAD_DIM)
    key_heads = key_all.reshape(seq_len, HEADS, HEAD_DIM)
    value_heads = value_all.reshape(seq_len, HEADS, HEAD_DIM)
    scores = (
        jnp.einsum("qhd,khd->hqk", query_heads, key_heads, preferred_element_type=jnp.float32)
        * scale
    )
    scores = jnp.where(same_doc[None], scores, masked_score)
    attn_probs = jnp.exp(scores - log_total)
    d_probs = jnp.einsum(
        "qhd,khd->hqk", d_heads_split, value_heads, preferred_element_type=jnp.float32
    )
    row_dot = jnp.sum(attn_probs * d_probs, axis=-1)
    d_scores = (attn_probs * (d_probs - row_dot[:, :, None])).astype(jnp.bfloat16)
    d_query = (
        (
            jnp.einsum("hqk,khd->qhd", d_scores, key_heads, preferred_element_type=jnp.float32)
            * scale
        )
        .reshape(row_count, model_width)
        .astype(jnp.bfloat16)
    )
    probs_low = attn_probs.astype(jnp.bfloat16)
    d_key_rows = (
        jnp.einsum("hqk,qhd->khd", d_scores, query_heads, preferred_element_type=jnp.float32)
        * scale
    )
    d_value_rows = jnp.einsum(
        "hqk,qhd->khd", probs_low, d_heads_split, preferred_element_type=jnp.float32
    )
    d_key_value = lax.psum_scatter(
        jnp.concatenate(
            [
                d_key_rows.reshape(lax.axis_size("ctx") * row_count, model_width),
                d_value_rows.reshape(lax.axis_size("ctx") * row_count, model_width),
            ],
            axis=1,
        ).astype(jnp.bfloat16),
        "ctx",
        scatter_dimension=0,
        tiled=True,
    )
    d_packed = jnp.concatenate([d_query, d_key_value], axis=1)
    g_bias_query = jnp.sum(d_query.astype(jnp.float32), axis=0)
    g_bias_value = jnp.sum(d_key_value[:, model_width:].astype(jnp.float32), axis=0)
    g_w_qkv = jnp.einsum("td,te->de", stream, d_packed, preferred_element_type=jnp.float32)
    d_stream = d_first + jnp.einsum(
        "te,de->td", d_packed, w_qkv, preferred_element_type=jnp.float32
    )
    terms = (
        g_w_qkv,
        g_w_attn_out,
        g_w_ff_in,
        g_w_ff_out,
        jnp.stack([g_bias_query, g_bias_value, g_bias_attn, g_bias_out]),
        g_ff_in_bias,
        jnp.stack([g_gain_one, g_gain_two]),
        jnp.stack([g_shift_one, g_shift_two]),
    )
    return (d_stream.astype(jnp.bfloat16), terms)


def on_device(
    hidden_in,
    doc_starts,
    w_qkv,
    w_attn_out,
    w_ff_in,
    w_ff_out,
    proj_bias,
    ff_in_bias,
    ln_gain,
    ln_shift,
    out_grad,
):
    rank_ctx = lax.axis_index("ctx")
    shards = (w_qkv, w_attn_out, w_ff_in, w_ff_out, proj_bias, ff_in_bias, ln_gain, ln_shift)
    output_list = []
    grad_list = []
    running = None
    for micro_step in range(hidden_in.shape[0]):
        stream = hidden_in[micro_step, 0]
        starts = doc_starts[micro_step, 0]
        forward_weights = gather_weights(shards)
        result, kept = forward_pass(stream, starts, forward_weights, rank_ctx)
        backward_weights = gather_weights(shards)
        d_stream, terms = backward_pass(
            out_grad[micro_step, 0].astype(jnp.float32), stream, kept, backward_weights
        )
        if micro_step == 0:
            running = terms
        else:
            running = jax.tree.map(jnp.add, running, terms)
        output_list.append(result.astype(jnp.bfloat16)[None, None])
        grad_list.append(d_stream[None, None])
    running = reduce_weights(running)
    summed = jax.tree.map(
        lambda part: part.astype(jnp.float32), lax.psum(for_sending(running), "ctx")
    )
    return (
        jnp.concatenate(output_list, axis=0),
        jnp.concatenate(grad_list, axis=0),
        summed[0],
        summed[1],
        summed[2],
        summed[3],
        summed[4],
        summed[5],
        summed[6],
        summed[7],
    )

f32 = jnp.float32
bf16 = jnp.bfloat16


def mm(a, b, dims=((1,), (0,))):
    return lax.dot_general(a, b, (dims, ((), ())), preferred_element_type=f32)


def document_bias(info_ref, length, rows, step, docs):
    at = step * rows + lax.broadcasted_iota(jnp.int32, (1, rows), 1)
    low = jnp.zeros((1, rows), jnp.int32)
    high = jnp.full((1, rows), length, jnp.int32)
    for d in range(docs):
        start = info_ref[1 + d]
        low = jnp.where(at >= start, jnp.maximum(low, start), low)
        high = jnp.where(at < start, jnp.minimum(high, start), high)
    other = lax.broadcasted_iota(jnp.int32, (length, rows), 0)
    return jnp.where((other >= low) & (other < high), 0.0, masked_score)


def block_of(info_ref, peer, rows):
    return pl.ds(pl.multiple_of((info_ref[0] ^ peer) * rows, rows), rows)


def attention_forward(info, parts, picks, weight, bias, docs):
    rows = parts[0].shape[-2]
    model_width = parts[0].shape[-1]
    triple = weight.shape[1]
    width = triple // 3
    heads = width // HEAD_DIM
    length = 4 * rows

    def body(info_ref, x0, x1, x2, x3, weight_ref, bias_ref, qkv_ref, out_ref, lse_ref):
        step = pl.program_id(0)

        @pl.when(step == 0)
        def _():
            for peer, x in enumerate((x0, x1, x2, x3)):
                qkv_ref[block_of(info_ref, peer, rows), :] = (
                    mm(x[...], weight_ref[...]) + bias_ref[:1, :]
                ).astype(bf16)

        mask = document_bias(info_ref, length, rows, step, docs)
        here = pl.ds(pl.multiple_of(step * rows, rows), rows)
        for h in range(heads):
            at = h * HEAD_DIM
            query = qkv_ref[here, at : at + HEAD_DIM]
            key = qkv_ref[:, width + at : width + at + HEAD_DIM]
            value = qkv_ref[:, 2 * width + at : 2 * width + at + HEAD_DIM]
            scores = mm(key, query, ((1,), (1,))) * (HEAD_DIM ** (-0.5) * log2_e) + mask
            peak = jnp.max(scores, axis=0, keepdims=True)
            probs = jnp.exp2(scores - peak)
            total = jnp.sum(probs, axis=0, keepdims=True)
            mixed = mm(value, probs.astype(bf16), ((0,), (0,))) / total
            out_ref[:, at : at + HEAD_DIM] = mixed.T.astype(bf16)
            lse_ref[h : h + 1, :] = peak + jnp.log2(total)

    def part_spec(pick_at):
        return pl.BlockSpec((None, rows, model_width), lambda i, n: (pick_at, 0, 0))

    return pl.pallas_call(
        body,
        grid_spec=pltpu.PrefetchScalarGridSpec(
            num_scalar_prefetch=1,
            grid=(4,),
            in_specs=[part_spec(p) for p in picks]
            + [
                pl.BlockSpec((model_width, triple), lambda i, n: (0, 0)),
                pl.BlockSpec((8, triple), lambda i, n: (0, 0)),
            ],
            out_specs=[
                pl.BlockSpec((length, triple), lambda i, n: (0, 0)),
                pl.BlockSpec((None, rows, width), lambda i, n: (i, 0, 0)),
                pl.BlockSpec((8, rows), lambda i, n: (0, i)),
            ],
        ),
        out_shape=[
            jax.ShapeDtypeStruct((length, triple), bf16),
            jax.ShapeDtypeStruct((4, rows, width), bf16),
            jax.ShapeDtypeStruct((8, length), f32),
        ],
        name="attention_forward",
        cost_estimate=pl.CostEstimate(
            flops=16 * heads * length * length * HEAD_DIM + 2 * length * model_width * triple,
            transcendentals=heads * length * length,
            bytes_accessed=4 * length * model_width,
        ),
    )(info, *parts, weight, bias)


def attention_backward(info, qkv, grad, grad_at, lse, parts, picks, weight, before, docs):
    rows = parts[0].shape[-2]
    model_width = parts[0].shape[-1]
    length, triple = qkv.shape
    width = triple // 3
    heads = width // HEAD_DIM
    scale = HEAD_DIM ** (-0.5)

    def body(info_ref, qkv_ref, grad_ref, lse_ref, x0, x1, x2, x3, weight_ref, *rest):
        if before is None:
            old, old_bias = None, None
            d_x_ref, d_w_ref, d_b_ref, key_acc, value_acc, d_qkv = rest
        else:
            old, old_bias, d_x_ref, d_w_ref, d_b_ref, key_acc, value_acc, d_qkv = rest
        step = pl.program_id(0)

        @pl.when(step == 0)
        def _():
            key_acc[...] = jnp.zeros_like(key_acc)
            value_acc[...] = jnp.zeros_like(value_acc)

        mask = document_bias(info_ref, length, rows, step, docs)
        here = pl.ds(pl.multiple_of(step * rows, rows), rows)
        for h in range(heads):
            at = h * HEAD_DIM
            query = qkv_ref[here, at : at + HEAD_DIM]
            grad = grad_ref[:, at : at + HEAD_DIM]
            key = qkv_ref[:, width + at : width + at + HEAD_DIM]
            value = qkv_ref[:, 2 * width + at : 2 * width + at + HEAD_DIM]
            scores = mm(key, query, ((1,), (1,))) * (scale * log2_e) + mask
            probs = jnp.exp2(scores - lse_ref[h : h + 1, :])
            d_probs = mm(value, grad, ((1,), (1,)))
            row_dot = jnp.sum(probs * d_probs, axis=0, keepdims=True)
            d_scores = (probs * (d_probs - row_dot)).astype(bf16)
            value_acc[h] += mm(probs.astype(bf16), grad)
            key_acc[h] += mm(d_scores, query)
            d_query = mm(key, d_scores, ((0,), (0,))) * scale
            d_qkv[here, at : at + HEAD_DIM] = d_query.T.astype(bf16)

        @pl.when(step == 3)
        def _():
            for h in range(heads):
                at = h * HEAD_DIM
                d_qkv[:, width + at : width + at + HEAD_DIM] = (key_acc[h] * scale).astype(bf16)
                d_qkv[:, 2 * width + at : 2 * width + at + HEAD_DIM] = value_acc[h].astype(bf16)
            total = None if old is None else old[...]
            for peer, x in enumerate((x0, x1, x2, x3)):
                term = mm(x[...], d_qkv[block_of(info_ref, peer, rows), :], ((0,), (0,)))
                total = term if total is None else total + term
            d_w_ref[...] = total
            column = jnp.sum(d_qkv[...].astype(f32), axis=0, keepdims=True)
            d_b_ref[...] = jnp.broadcast_to(column, d_b_ref.shape) + (
                0.0 if old is None else old_bias[...]
            )
            for r in range(4):
                d_x_ref[r] = mm(
                    d_qkv[r * rows : (r + 1) * rows, :], weight_ref[...], ((1,), (1,))
                ).astype(bf16)

    def part_spec(pick_at):
        return pl.BlockSpec((None, rows, model_width), lambda i, n: (pick_at, 0, 0))

    def whole(shape):
        return pl.BlockSpec(shape, lambda i, n: (0,) * len(shape))

    sum_shapes = [(model_width, triple), (8, triple)]
    return pl.pallas_call(
        body,
        grid_spec=pltpu.PrefetchScalarGridSpec(
            num_scalar_prefetch=1,
            grid=(4,),
            in_specs=[
                whole((length, triple)),
                pl.BlockSpec((None, rows, width), lambda i, n: (i, grad_at, 0)),
                pl.BlockSpec((8, rows), lambda i, n: (0, i)),
            ]
            + [part_spec(p) for p in picks]
            + [whole((model_width, triple))]
            + ([] if before is None else [whole(v) for v in sum_shapes]),
            out_specs=[whole((4, rows, model_width))] + [whole(v) for v in sum_shapes],
            scratch_shapes=[
                pltpu.VMEM((heads, length, HEAD_DIM), f32),
                pltpu.VMEM((heads, length, HEAD_DIM), f32),
                pltpu.VMEM((length, triple), bf16),
            ],
        ),
        out_shape=[jax.ShapeDtypeStruct((4, rows, model_width), bf16)]
        + [jax.ShapeDtypeStruct(v, f32) for v in sum_shapes],
        name="attention_backward",
        cost_estimate=pl.CostEstimate(
            flops=40 * heads * length * length * HEAD_DIM + 4 * length * model_width * triple,
            transcendentals=heads * length * length,
            bytes_accessed=8 * length * model_width,
        ),
    )(info, qkv, grad, lse, *parts, weight, *(() if before is None else before))


def from_peer(value, peer):
    return lax.ppermute(value, "ctx", [(r, r ^ peer) for r in range(4)])


def from_core(value):
    return lax.ppermute(value, "fsdp", [(f, f ^ 1) for f in range(lax.axis_size("fsdp"))])


def pick(stack, index):
    return lax.dynamic_index_in_dim(stack, index, 0, keepdims=False)


def add_sent(own, received):
    return (own.astype(f32) + received.astype(f32)).astype(bf16)


def tie(*values):
    return lax.optimization_barrier(values)


def along_chips(value, hops):
    size = lax.axis_size("fsdp")
    return lax.ppermute(value, "fsdp", [(f, (f + 2 * hops) % size) for f in range(size)])


def core_send(partial):
    core = lax.axis_index("fsdp") % 2
    pairs = partial.reshape((partial.shape[0] // 2, 2) + partial.shape[1:])
    kept = lax.dynamic_index_in_dim(pairs, core, 1, keepdims=False)
    other = lax.dynamic_index_in_dim(pairs, 1 - core, 1, keepdims=False)
    return kept, from_core(other)


def halves(value, axis):
    return jnp.stack(jnp.split(value, 2, axis=axis))


def plane_send(held, me, axis):
    xx, y = me % 2, me // 2
    first, second = jnp.split(held, 2, axis=axis)
    first, second = halves(first, axis), halves(second, axis)
    kept = pick(first, xx), pick(second, y)
    return kept, (from_peer(pick(first, 1 - xx), 1), from_peer(pick(second, 1 - y), 2))


def plane_send_again(kept, received, me, axis):
    xx, y = me % 2, me // 2
    first = halves(add_sent(kept[0], received[0]), axis)
    second = halves(add_sent(kept[1], received[1]), axis)
    kept = pick(first, y), pick(second, xx)
    return kept, (from_peer(pick(first, 1 - y), 2), from_peer(pick(second, 1 - xx), 1))


def join_plane(kept, received, axis):
    return jnp.concatenate([add_sent(k, r) for k, r in zip(kept, received)], axis=axis)


def line_send(parts):
    chips = parts.shape[0]
    z = lax.axis_index("fsdp") // 2
    received = tuple(
        along_chips(pick(parts, (z + k) % chips), k) for k in range(1, chips)
    )
    return pick(parts, z), received


def line_sum(kept, received):
    total = kept.astype(f32)
    for r in received:
        total = total + r.astype(f32)
    return total.astype(bf16)


def exchange(blocks):
    return lax.all_to_all(blocks, "ctx", 0, 0)


def peers_send(value):
    return value, tuple(from_peer(value, j) for j in (1, 2, 3))


def in_rank_order(value, received, me):
    stack = jnp.stack([value] + list(received))
    return [pick(stack, me ^ r) for r in range(4)]


def join_ranks(ranks, axis):
    first, second = zip(*[jnp.split(r, 2, axis=axis) for r in ranks])
    order = [first[2 * b + a] for a in (0, 1) for b in (0, 1)] + list(second)
    return jnp.concatenate(order, axis=axis).astype(f32)


def gelu_parts(inner_act):
    cdf = 0.5 * (1.0 + lax.erf(inner_act * inv_root_two))
    slope = cdf + inner_act * jnp.exp(-0.5 * inner_act * inner_act) * inv_root_tau
    return inner_act * cdf, slope


def on_plane(
    hidden_in,
    doc_starts,
    w_qkv,
    w_attn_out,
    w_ff_in,
    w_ff_out,
    proj_bias,
    ff_in_bias,
    ln_gain,
    ln_shift,
    out_grad,
):
    me = lax.axis_index("ctx")
    micro, _, rows, model_width = hidden_in.shape
    shards = lax.axis_size("fsdp")
    part = model_width // 4
    inner_width = w_ff_in.shape[1]
    streams = [hidden_in[m, 0] for m in range(micro)]

    own_columns = jnp.concatenate(
        [
            lax.dynamic_slice_in_dim(w_qkv, b * model_width + me * part, part, 1)
            for b in range(3)
        ],
        axis=1,
    )
    small = jnp.concatenate([v.reshape(-1) for v in (proj_bias, ff_in_bias, ln_gain, ln_shift)])
    first_rows = jnp.concatenate([own_columns, small.reshape(-1, 3 * part)], axis=0)
    head_got = tuple(from_peer(streams[0], j) for j in (1, 2, 3))
    rest, head_first = hidden_in[1:, 0], hidden_in[0]
    rest_got = tuple(from_peer(rest, j) for j in (1, 2, 3))
    first_all = lax.all_gather(first_rows, "fsdp", axis=0)
    w_own = first_all[:, : w_qkv.shape[0]].reshape(model_width, 3 * part)
    small_all = first_all[:, w_qkv.shape[0] :].reshape(shards, -1).astype(f32)
    at = 0
    wholes = []
    for count, length in (
        (4, proj_bias.shape[1]),
        (1, ff_in_bias.shape[0]),
        (2, ln_gain.shape[1]),
        (2, ln_shift.shape[1]),
    ):
        piece = small_all[:, at : at + count * length].reshape(shards, count, length)
        wholes.append(piece.transpose(1, 0, 2).reshape(count, shards * length))
        at += count * length
    bias_all, inner_bias, gains, shifts = wholes
    qkv_bias = jnp.concatenate(
        [
            lax.dynamic_slice_in_dim(bias_all[0], me * part, part),
            jnp.zeros((part,), f32),
            lax.dynamic_slice_in_dim(bias_all[1], me * part, part),
        ]
    )

    w_pair = lax.all_gather(
        jnp.concatenate([w_ff_in, w_attn_out], axis=1), "fsdp", axis=0, tiled=True
    )
    w_in_all = w_pair[:, :inner_width]
    w_last_all = lax.all_gather(w_ff_out, "fsdp", axis=0, tiled=True)
    w_out_all = w_pair[:, inner_width:]

    docs = doc_starts.shape[2]
    bias_rows = jnp.broadcast_to(qkv_bias[None], (8, 3 * part))
    infos = []
    inputs = []
    sequence = []
    pieces = []
    for m in range(micro):
        infos.append(jnp.concatenate([me[None].astype(jnp.int32), doc_starts[m, 0]]))
        if m == 0:
            parts = (head_first,) + tuple(v[None] for v in head_got)
            picks = (0, 0, 0, 0)
        else:
            parts = (hidden_in.reshape(micro, rows, model_width),) + rest_got
            picks = (m, m - 1, m - 1, m - 1)
        inputs.append((parts, picks))
        qkv, out, lse = attention_forward(infos[m], parts, picks, w_own, bias_rows, docs)
        sequence.append((qkv, lse))
        ready = exchange(out)
        pieces.append(jnp.concatenate([ready[r] for r in range(4)], axis=1))
    heads_out = jnp.concatenate(pieces, axis=0)
    stream = jnp.concatenate(streams, axis=0)

    first_sum = stream.astype(f32) + mm(heads_out, w_out_all) + bias_all[2]
    normed, normal_one, inverse_one = layer_norm_parts(first_sum, gains[0], shifts[0])
    normed_low = normed.astype(bf16)
    inner_act = mm(normed_low, w_in_all) + inner_bias[0]
    activated, slope = gelu_parts(inner_act)
    activated = activated.astype(bf16)
    activated, slope = tie(activated, slope.astype(bf16))
    second_sum = normed + mm(activated, w_last_all) + bias_all[3]
    result, normal_two, inverse_two = layer_norm_parts(second_sum, gains[1], shifts[1])

    grad_rows = jnp.concatenate([out_grad[m, 0] for m in range(micro)], axis=0).astype(f32)
    d_second = norm_backward(grad_rows, normal_two, inverse_two, gains[1])
    g_gain_two = jnp.sum(grad_rows * normal_two, axis=0)
    g_shift_two = jnp.sum(grad_rows, axis=0)
    d_ff_out = d_second.astype(bf16)
    g_bias_out = jnp.sum(d_ff_out.astype(f32), axis=0)
    g_w_ff_out = mm(activated, d_ff_out, ((0,), (0,))).astype(bf16)
    last = lax.psum_scatter(g_w_ff_out, "fsdp", scatter_dimension=0, tiled=True)
    d_inner = (mm(d_ff_out, w_last_all, ((1,), (1,))) * slope.astype(f32)).astype(bf16)
    g_ff_in_bias = jnp.sum(d_inner.astype(f32), axis=0)
    g_w_ff_in = mm(normed_low, d_inner, ((0,), (0,))).astype(bf16)

    d_normed = d_second + mm(d_inner, w_in_all, ((1,), (1,)))
    d_first = norm_backward(d_normed, normal_one, inverse_one, gains[0])
    g_gain_one = jnp.sum(d_normed * normal_one, axis=0)
    g_shift_one = jnp.sum(d_normed, axis=0)
    d_branch = d_first.astype(bf16)
    g_bias_attn = jnp.sum(d_branch.astype(f32), axis=0)
    d_heads = mm(d_branch, w_out_all, ((1,), (1,))).astype(bf16)
    split_heads = d_heads.reshape(micro * rows, 4, part).transpose(1, 0, 2)
    split_heads, d_branch = tie(split_heads, d_branch)
    d_mixed = [exchange(split_heads[:, :rows]), exchange(split_heads[:, rows:])]

    g_w_out = mm(heads_out, d_branch, ((0,), (0,))).astype(bf16)
    small_grads = jnp.concatenate(
        [
            v.reshape(-1, shards, v.shape[-1] // shards).transpose(1, 0, 2).reshape(shards, -1)
            for v in (
                jnp.stack([g_bias_attn, g_bias_out]),
                g_ff_in_bias[None],
                jnp.stack([g_gain_one, g_gain_two]),
                jnp.stack([g_shift_one, g_shift_two]),
            )
        ],
        axis=1,
    ).astype(bf16)
    depth = model_width // shards
    spare = -(inner_width + model_width) % 1024
    small_grads = jnp.pad(small_grads, ((0, 0), (0, depth * spare - small_grads.shape[1])))
    joined = jnp.concatenate(
        [
            g_w_ff_in.reshape(shards, depth, inner_width),
            g_w_out.reshape(shards, depth, model_width),
            small_grads.reshape(shards, depth, spare),
        ],
        axis=2,
    )
    in_kept, in_got = core_send(joined)
    d_mixed[0], in_kept, in_got = tie(d_mixed[0], in_kept, in_got)
    in_kept, in_got = plane_send(add_sent(in_kept, in_got), me, 2)

    sums = []
    own = None
    for m in range(micro):
        qkv, lse = sequence[m]
        parts, picks = inputs[m]
        d_x, *own = attention_backward(
            infos[m],
            qkv,
            d_mixed[min(m, 1)],
            max(m - 1, 0),
            lse,
            parts,
            picks,
            w_own,
            own,
            docs,
        )
        if m == 0:
            own[0], in_got, d_mixed[1] = tie(own[0], in_got, d_mixed[1])
            in_kept, in_got = plane_send_again(in_kept, in_got, me, 2)
        elif m == 1:
            own[0], in_got, last, sums[0] = tie(own[0], in_got, last, sums[0])
            in_kept, in_got = line_send(join_plane(in_kept, in_got, 2))
            last_got = from_peer(last, 1)
        elif m == 2:
            own[0], in_got, last_got, sums[1] = tie(own[0], in_got, last_got, sums[1])
            in_kept, in_got = peers_send(line_sum(in_kept, in_got))
            last = add_sent(last, last_got)
            last_got = from_peer(last, 2)
        sums.append(exchange(d_x))
    own_grad, own_bias = own[0], own[1][0]
    own_all = jnp.concatenate(
        [
            own_grad.astype(bf16).reshape(shards, -1, 3 * part),
            jnp.broadcast_to(own_bias.astype(bf16), (shards, 1, 3 * part)),
        ],
        axis=1,
    )
    own_kept, own_got = core_send(own_all)
    own_kept, own_got = line_send(add_sent(own_kept, own_got))
    own_kept, own_got = peers_send(line_sum(own_kept, own_got))
    in_grad = d_first + jnp.concatenate(
        [jnp.sum(v.astype(f32), axis=0) for v in sums], axis=0
    )
    whole = jnp.stack(in_rank_order(own_kept, own_got, me)).astype(f32)
    g_qkv = (
        whole[:, :-1].reshape(4, -1, 3, part).transpose(1, 2, 0, 3).reshape(-1, 3 * model_width)
    )
    both = whole[:, -1].reshape(4, 3, part).transpose(1, 0, 2).reshape(3, model_width)
    own_shard = lax.axis_index("fsdp") * proj_bias.shape[1]
    both = lax.dynamic_slice_in_dim(both, own_shard, proj_bias.shape[1], 1)
    g_last = last.astype(f32) + last_got.astype(f32)
    g_joined = join_ranks(in_rank_order(in_kept, in_got, me), 1)
    g_in = g_joined[:, :inner_width]
    g_out = g_joined[:, inner_width : inner_width + model_width]
    flat = g_joined[:, inner_width + model_width :].reshape(-1)
    narrow = proj_bias.shape[1]
    bias_pair = flat[: 2 * narrow].reshape(2, narrow)
    at = 2 * narrow
    inner_bias_grad = flat[at : at + ff_in_bias.shape[0]]
    at += ff_in_bias.shape[0]
    gain_grad = flat[at : at + 2 * narrow].reshape(2, narrow)
    at += 2 * narrow
    shift_grad = flat[at : at + 2 * narrow].reshape(2, narrow)
    bias_grad = jnp.concatenate([both[0:1], both[2:3], bias_pair], axis=0)
    return (
        result.astype(bf16).reshape(out_grad.shape),
        in_grad.astype(bf16).reshape(hidden_in.shape),
        g_qkv,
        g_out,
        g_in,
        g_last,
        bias_grad,
        inner_bias_grad,
        gain_grad,
        shift_grad,
    )


def solution(mesh):
    plane = mesh.shape["ctx"] == 4 and mesh.shape["fsdp"] == 8
    return jax.shard_map(
        on_plane if plane else on_device,
        mesh=mesh,
        in_specs=(
            P(None, "fsdp", "ctx", None),
            P(None, "fsdp", None),
            P("fsdp", None),
            P("fsdp", None),
            P("fsdp", None),
            P("fsdp", None),
            P(None, "fsdp"),
            P("fsdp"),
            P(None, "fsdp"),
            P(None, "fsdp"),
            P(None, "fsdp", "ctx", None),
        ),
        out_specs=(
            P(None, "fsdp", "ctx", None),
            P(None, "fsdp", "ctx", None),
            P("fsdp", None),
            P("fsdp", None),
            P("fsdp", None),
            P("fsdp", None),
            P(None, "fsdp"),
            P("fsdp"),
            P(None, "fsdp"),
            P(None, "fsdp"),
        ),
        check_vma=False,
    )
```

```python
import jax
import jax.numpy as jnp
from jax import lax
from jax.experimental import pallas as pl
from jax.experimental.pallas import tpu as pltpu
from jax.sharding import PartitionSpec as P

HEADS = 12
HEAD_DIM = 64


norm_epsilon = 1e-12
masked_score = -1e30
inv_root_two = 0.7071067811865476
inv_root_tau = 0.3989422804014327
log2_e = 1.4426950408889634

def for_sending(value):

    def short(part):
        return part.astype(jnp.bfloat16) if part.dtype == jnp.float32 else part

    return jax.tree.map(short, value)


def layer_norm_parts(values, gain_row, shift_row):
    centre = values - jnp.mean(values, axis=-1, keepdims=True)
    inverse = lax.rsqrt(jnp.mean(centre * centre, axis=-1, keepdims=True) + norm_epsilon)
    normal = centre * inverse
    return (normal * gain_row + shift_row, normal, inverse)


def norm_backward(grad_rows, normal, inverse, gain_row):
    scaled = grad_rows * gain_row
    return inverse * (
        scaled
        - jnp.mean(scaled, axis=-1, keepdims=True)
        - normal * jnp.mean(scaled * normal, axis=-1, keepdims=True)
    )


def gelu_slope(inner_act):
    return (
        0.5 * (1.0 + jax.scipy.special.erf(inner_act * inv_root_two))
        + inner_act * jnp.exp(-0.5 * inner_act * inner_act) * inv_root_tau
    )


def segment_ids(positions, starts):
    return jnp.sum((positions[:, None] >= starts[None, :]).astype(jnp.int32), axis=1)


def gather_weights(shards):
    return (
        lax.all_gather(shards[0], "fsdp", axis=0, tiled=True),
        lax.all_gather(shards[1], "fsdp", axis=0, tiled=True),
        lax.all_gather(shards[2], "fsdp", axis=0, tiled=True),
        lax.all_gather(shards[3], "fsdp", axis=0, tiled=True),
        lax.all_gather(shards[4], "fsdp", axis=1, tiled=True),
        lax.all_gather(shards[5], "fsdp", axis=0, tiled=True),
        lax.all_gather(shards[6], "fsdp", axis=1, tiled=True),
        lax.all_gather(shards[7], "fsdp", axis=1, tiled=True),
    )


def reduce_weights(terms):
    return (
        lax.psum_scatter(
            terms[0].astype(jnp.bfloat16), "fsdp", scatter_dimension=0, tiled=True
        ).astype(jnp.float32),
        lax.psum_scatter(
            terms[1].astype(jnp.bfloat16), "fsdp", scatter_dimension=0, tiled=True
        ).astype(jnp.float32),
        lax.psum_scatter(
            terms[2].astype(jnp.bfloat16), "fsdp", scatter_dimension=0, tiled=True
        ).astype(jnp.float32),
        lax.psum_scatter(
            terms[3].astype(jnp.bfloat16), "fsdp", scatter_dimension=0, tiled=True
        ).astype(jnp.float32),
        lax.psum_scatter(
            terms[4].astype(jnp.bfloat16), "fsdp", scatter_dimension=1, tiled=True
        ).astype(jnp.float32),
        lax.psum_scatter(
            terms[5].astype(jnp.bfloat16), "fsdp", scatter_dimension=0, tiled=True
        ).astype(jnp.float32),
        lax.psum_scatter(
            terms[6].astype(jnp.bfloat16), "fsdp", scatter_dimension=1, tiled=True
        ).astype(jnp.float32),
        lax.psum_scatter(
            terms[7].astype(jnp.bfloat16), "fsdp", scatter_dimension=1, tiled=True
        ).astype(jnp.float32),
    )


def forward_pass(stream, starts, whole, rank_ctx):
    w_qkv, w_attn_out, w_ff_in, w_ff_out, proj_bias, ff_in_bias, ln_gain, ln_shift = whole
    row_count = stream.shape[0]
    model_width = stream.shape[1]
    bias_float = proj_bias.astype(jnp.float32)
    qkv_bias = jnp.concatenate([bias_float[0], jnp.zeros_like(bias_float[0]), bias_float[1]])
    packed = (jnp.dot(stream, w_qkv, preferred_element_type=jnp.float32) + qkv_bias).astype(
        jnp.bfloat16
    )
    query_part = packed[:, :model_width]
    key_part = packed[:, model_width : 2 * model_width]
    value_part = packed[:, 2 * model_width :]
    key_all, value_all = (
        lax.all_gather(key_part, "ctx", axis=0, tiled=True),
        lax.all_gather(value_part, "ctx", axis=0, tiled=True),
    )
    seq_len = key_all.shape[0]
    query_seg = segment_ids(rank_ctx * row_count + jnp.arange(row_count, dtype=jnp.int32), starts)
    key_seg = segment_ids(jnp.arange(seq_len, dtype=jnp.int32), starts)
    same_doc = query_seg[:, None] == key_seg[None, :]
    query_heads = query_part.reshape(row_count, HEADS, HEAD_DIM)
    key_heads = key_all.reshape(seq_len, HEADS, HEAD_DIM)
    value_heads = value_all.reshape(seq_len, HEADS, HEAD_DIM)
    scores = jnp.einsum(
        "qhd,khd->hqk", query_heads, key_heads, preferred_element_type=jnp.float32
    ) * HEAD_DIM ** (-0.5)
    scores = jnp.where(same_doc[None], scores, masked_score)
    row_peak = jnp.max(scores, axis=-1, keepdims=True)
    exp_scores = jnp.exp(scores - row_peak)
    row_total = jnp.sum(exp_scores, axis=-1, keepdims=True)
    attn_probs = exp_scores / row_total
    log_total = row_peak + jnp.log(row_total)
    mixed = jnp.einsum(
        "hqk,khd->qhd",
        attn_probs.astype(jnp.bfloat16),
        value_heads,
        preferred_element_type=jnp.float32,
    ).reshape(row_count, model_width)
    heads_out = mixed.astype(jnp.bfloat16)
    first_sum = (
        stream.astype(jnp.float32)
        + jnp.dot(heads_out, w_attn_out, preferred_element_type=jnp.float32)
        + bias_float[2]
    )
    normed, normal_one, inverse_one = layer_norm_parts(
        first_sum, ln_gain[0].astype(jnp.float32), ln_shift[0].astype(jnp.float32)
    )
    normed_low = normed.astype(jnp.bfloat16)
    inner_act = jnp.dot(
        normed_low, w_ff_in, preferred_element_type=jnp.float32
    ) + ff_in_bias.astype(jnp.float32)
    activated = jax.nn.gelu(inner_act, approximate=False).astype(jnp.bfloat16)
    second_sum = (
        normed + jnp.dot(activated, w_ff_out, preferred_element_type=jnp.float32) + bias_float[3]
    )
    result, normal_two, inverse_two = layer_norm_parts(
        second_sum, ln_gain[1].astype(jnp.float32), ln_shift[1].astype(jnp.float32)
    )
    kept = (
        query_heads,
        key_all,
        value_all,
        same_doc,
        log_total,
        mixed,
        heads_out,
        normal_one,
        inverse_one,
        normed_low,
        inner_act,
        activated,
        normal_two,
        inverse_two,
    )
    return (result, kept)


def backward_pass(grad_rows, stream, kept, whole):
    w_qkv, w_attn_out, w_ff_in, w_ff_out, proj_bias, ff_in_bias, ln_gain, ln_shift = whole
    (
        query_heads,
        key_all,
        value_all,
        same_doc,
        log_total,
        mixed,
        heads_out,
        normal_one,
        inverse_one,
        normed_low,
        inner_act,
        activated,
        normal_two,
        inverse_two,
    ) = kept
    row_count = stream.shape[0]
    model_width = stream.shape[1]
    seq_len = key_all.shape[0]
    scale = HEAD_DIM ** (-0.5)
    d_second = norm_backward(grad_rows, normal_two, inverse_two, ln_gain[1].astype(jnp.float32))
    g_gain_two = jnp.sum(grad_rows * normal_two, axis=0)
    g_shift_two = jnp.sum(grad_rows, axis=0)
    d_ff_out = d_second.astype(jnp.bfloat16)
    g_bias_out = jnp.sum(d_ff_out.astype(jnp.float32), axis=0)
    g_w_ff_out = jnp.einsum("tf,td->fd", activated, d_ff_out, preferred_element_type=jnp.float32)
    d_activated = jnp.einsum("td,fd->tf", d_ff_out, w_ff_out, preferred_element_type=jnp.float32)
    d_inner = (d_activated * gelu_slope(inner_act)).astype(jnp.bfloat16)
    g_ff_in_bias = jnp.sum(d_inner.astype(jnp.float32), axis=0)
    g_w_ff_in = jnp.einsum("td,tf->df", normed_low, d_inner, preferred_element_type=jnp.float32)
    d_normed = d_second + jnp.einsum(
        "tf,df->td", d_inner, w_ff_in, preferred_element_type=jnp.float32
    )
    d_first = norm_backward(d_normed, normal_one, inverse_one, ln_gain[0].astype(jnp.float32))
    g_gain_one = jnp.sum(d_normed * normal_one, axis=0)
    g_shift_one = jnp.sum(d_normed, axis=0)
    d_branch = d_first.astype(jnp.bfloat16)
    g_bias_attn = jnp.sum(d_branch.astype(jnp.float32), axis=0)
    g_w_attn_out = jnp.einsum("tc,td->cd", heads_out, d_branch, preferred_element_type=jnp.float32)
    d_heads = jnp.einsum(
        "td,cd->tc", d_branch, w_attn_out, preferred_element_type=jnp.float32
    ).astype(jnp.bfloat16)
    d_heads_split = d_heads.reshape(row_count, HEADS, HEAD_DIM)
    key_heads = key_all.reshape(seq_len, HEADS, HEAD_DIM)
    value_heads = value_all.reshape(seq_len, HEADS, HEAD_DIM)
    scores = (
        jnp.einsum("qhd,khd->hqk", query_heads, key_heads, preferred_element_type=jnp.float32)
        * scale
    )
    scores = jnp.where(same_doc[None], scores, masked_score)
    attn_probs = jnp.exp(scores - log_total)
    d_probs = jnp.einsum(
        "qhd,khd->hqk", d_heads_split, value_heads, preferred_element_type=jnp.float32
    )
    row_dot = jnp.sum(attn_probs * d_probs, axis=-1)
    d_scores = (attn_probs * (d_probs - row_dot[:, :, None])).astype(jnp.bfloat16)
    d_query = (
        (
            jnp.einsum("hqk,khd->qhd", d_scores, key_heads, preferred_element_type=jnp.float32)
            * scale
        )
        .reshape(row_count, model_width)
        .astype(jnp.bfloat16)
    )
    probs_low = attn_probs.astype(jnp.bfloat16)
    d_key_rows = (
        jnp.einsum("hqk,qhd->khd", d_scores, query_heads, preferred_element_type=jnp.float32)
        * scale
    )
    d_value_rows = jnp.einsum(
        "hqk,qhd->khd", probs_low, d_heads_split, preferred_element_type=jnp.float32
    )
    d_key_value = lax.psum_scatter(
        jnp.concatenate(
            [
                d_key_rows.reshape(lax.axis_size("ctx") * row_count, model_width),
                d_value_rows.reshape(lax.axis_size("ctx") * row_count, model_width),
            ],
            axis=1,
        ).astype(jnp.bfloat16),
        "ctx",
        scatter_dimension=0,
        tiled=True,
    )
    d_packed = jnp.concatenate([d_query, d_key_value], axis=1)
    g_bias_query = jnp.sum(d_query.astype(jnp.float32), axis=0)
    g_bias_value = jnp.sum(d_key_value[:, model_width:].astype(jnp.float32), axis=0)
    g_w_qkv = jnp.einsum("td,te->de", stream, d_packed, preferred_element_type=jnp.float32)
    d_stream = d_first + jnp.einsum(
        "te,de->td", d_packed, w_qkv, preferred_element_type=jnp.float32
    )
    terms = (
        g_w_qkv,
        g_w_attn_out,
        g_w_ff_in,
        g_w_ff_out,
        jnp.stack([g_bias_query, g_bias_value, g_bias_attn, g_bias_out]),
        g_ff_in_bias,
        jnp.stack([g_gain_one, g_gain_two]),
        jnp.stack([g_shift_one, g_shift_two]),
    )
    return (d_stream.astype(jnp.bfloat16), terms)


def on_device(
    hidden_in,
    doc_starts,
    w_qkv,
    w_attn_out,
    w_ff_in,
    w_ff_out,
    proj_bias,
    ff_in_bias,
    ln_gain,
    ln_shift,
    out_grad,
):
    rank_ctx = lax.axis_index("ctx")
    shards = (w_qkv, w_attn_out, w_ff_in, w_ff_out, proj_bias, ff_in_bias, ln_gain, ln_shift)
    output_list = []
    grad_list = []
    running = None
    for micro_step in range(hidden_in.shape[0]):
        stream = hidden_in[micro_step, 0]
        starts = doc_starts[micro_step, 0]
        forward_weights = gather_weights(shards)
        result, kept = forward_pass(stream, starts, forward_weights, rank_ctx)
        backward_weights = gather_weights(shards)
        d_stream, terms = backward_pass(
            out_grad[micro_step, 0].astype(jnp.float32), stream, kept, backward_weights
        )
        if micro_step == 0:
            running = terms
        else:
            running = jax.tree.map(jnp.add, running, terms)
        output_list.append(result.astype(jnp.bfloat16)[None, None])
        grad_list.append(d_stream[None, None])
    running = reduce_weights(running)
    summed = jax.tree.map(
        lambda part: part.astype(jnp.float32), lax.psum(for_sending(running), "ctx")
    )
    return (
        jnp.concatenate(output_list, axis=0),
        jnp.concatenate(grad_list, axis=0),
        summed[0],
        summed[1],
        summed[2],
        summed[3],
        summed[4],
        summed[5],
        summed[6],
        summed[7],
    )

f32 = jnp.float32
bf16 = jnp.bfloat16


def mm(a, b, dims=((1,), (0,))):
    return lax.dot_general(a, b, (dims, ((), ())), preferred_element_type=f32)


def document_bias(info_ref, length, rows, step, docs):
    at = step * rows + lax.broadcasted_iota(jnp.int32, (1, rows), 1)
    low = jnp.zeros((1, rows), jnp.int32)
    high = jnp.full((1, rows), length, jnp.int32)
    for d in range(docs):
        start = info_ref[1 + d]
        low = jnp.where(at >= start, jnp.maximum(low, start), low)
        high = jnp.where(at < start, jnp.minimum(high, start), high)
    other = lax.broadcasted_iota(jnp.int32, (length, rows), 0)
    return jnp.where((other >= low) & (other < high), 0.0, masked_score)


def block_of(info_ref, peer, rows):
    return pl.ds(pl.multiple_of((info_ref[0] ^ peer) * rows, rows), rows)


def attention_forward(info, parts, picks, weight, bias, docs):
    rows = parts[0].shape[-2]
    model_width = parts[0].shape[-1]
    triple = weight.shape[1]
    width = triple // 3
    heads = width // HEAD_DIM
    length = 4 * rows

    def body(info_ref, x0, x1, x2, x3, weight_ref, bias_ref, qkv_ref, out_ref, lse_ref):
        step = pl.program_id(0)

        @pl.when(step == 0)
        def _():
            for peer, x in enumerate((x0, x1, x2, x3)):
                qkv_ref[block_of(info_ref, peer, rows), :] = (
                    mm(x[...], weight_ref[...]) + bias_ref[:1, :]
                ).astype(bf16)

        mask = document_bias(info_ref, length, rows, step, docs)
        here = pl.ds(pl.multiple_of(step * rows, rows), rows)
        for h in range(heads):
            at = h * HEAD_DIM
            query = qkv_ref[here, at : at + HEAD_DIM]
            key = qkv_ref[:, width + at : width + at + HEAD_DIM]
            value = qkv_ref[:, 2 * width + at : 2 * width + at + HEAD_DIM]
            scores = mm(key, query, ((1,), (1,))) * (HEAD_DIM ** (-0.5) * log2_e) + mask
            peak = jnp.max(scores, axis=0, keepdims=True)
            probs = jnp.exp2(scores - peak)
            total = jnp.sum(probs, axis=0, keepdims=True)
            mixed = mm(value, probs.astype(bf16), ((0,), (0,))) / total
            out_ref[at : at + HEAD_DIM, :] = mixed.astype(bf16)
            lse_ref[h : h + 1, :] = peak + jnp.log2(total)

    def part_spec(pick_at):
        return pl.BlockSpec((None, rows, model_width), lambda i, n: (pick_at, 0, 0))

    return pl.pallas_call(
        body,
        grid_spec=pltpu.PrefetchScalarGridSpec(
            num_scalar_prefetch=1,
            grid=(4,),
            in_specs=[part_spec(p) for p in picks]
            + [
                pl.BlockSpec((model_width, triple), lambda i, n: (0, 0)),
                pl.BlockSpec((8, triple), lambda i, n: (0, 0)),
            ],
            out_specs=[
                pl.BlockSpec((length, triple), lambda i, n: (0, 0)),
                pl.BlockSpec((None, width, rows), lambda i, n: (i, 0, 0)),
                pl.BlockSpec((8, rows), lambda i, n: (0, i)),
            ],
        ),
        out_shape=[
            jax.ShapeDtypeStruct((length, triple), bf16),
            jax.ShapeDtypeStruct((4, width, rows), bf16),
            jax.ShapeDtypeStruct((8, length), f32),
        ],
        name="attention_forward",
        cost_estimate=pl.CostEstimate(
            flops=16 * heads * length * length * HEAD_DIM + 2 * length * model_width * triple,
            transcendentals=heads * length * length,
            bytes_accessed=4 * length * model_width,
        ),
    )(info, *parts, weight, bias)


def attention_backward(info, qkv, grad, grad_at, lse, parts, picks, weight, before, docs, shards):
    rows = parts[0].shape[-2]
    model_width = parts[0].shape[-1]
    length, triple = qkv.shape
    width = triple // 3
    heads = width // HEAD_DIM
    scale = HEAD_DIM ** (-0.5)
    final = shards > 0
    depth = model_width // max(shards, 1)

    def body(info_ref, qkv_ref, grad_ref, lse_ref, x0, x1, x2, x3, weight_ref, *rest):
        if before is None:
            old, old_bias = None, None
            d_x_ref, d_w_ref, d_b_ref, key_acc, value_acc, d_qkv, *more = rest
        else:
            old, old_bias, d_x_ref, d_w_ref, d_b_ref, key_acc, value_acc, d_qkv, *more = rest
        all_sum = more[0] if final else None
        step = pl.program_id(0)

        @pl.when(step == 0)
        def _():
            key_acc[...] = jnp.zeros_like(key_acc)
            value_acc[...] = jnp.zeros_like(value_acc)

        mask = document_bias(info_ref, length, rows, step, docs)
        here = pl.ds(pl.multiple_of(step * rows, rows), rows)
        for h in range(heads):
            at = h * HEAD_DIM
            query = qkv_ref[here, at : at + HEAD_DIM]
            grad = grad_ref[at : at + HEAD_DIM, :]
            key = qkv_ref[:, width + at : width + at + HEAD_DIM]
            value = qkv_ref[:, 2 * width + at : 2 * width + at + HEAD_DIM]
            scores = mm(key, query, ((1,), (1,))) * (scale * log2_e) + mask
            probs = jnp.exp2(scores - lse_ref[h : h + 1, :])
            d_probs = mm(value, grad)
            row_dot = jnp.sum(probs * d_probs, axis=0, keepdims=True)
            d_scores = (probs * (d_probs - row_dot)).astype(bf16)
            value_acc[h] += mm(probs.astype(bf16), grad, ((1,), (1,)))
            key_acc[h] += mm(d_scores, query)
            d_query = mm(key, d_scores, ((0,), (0,))) * scale
            d_qkv[here, at : at + HEAD_DIM] = d_query.T.astype(bf16)

        @pl.when(step == 3)
        def _():
            for h in range(heads):
                at = h * HEAD_DIM
                d_qkv[:, width + at : width + at + HEAD_DIM] = (key_acc[h] * scale).astype(bf16)
                d_qkv[:, 2 * width + at : 2 * width + at + HEAD_DIM] = value_acc[h].astype(bf16)
            total = None if old is None else old[...]
            for peer, x in enumerate((x0, x1, x2, x3)):
                term = mm(x[...], d_qkv[block_of(info_ref, peer, rows), :], ((0,), (0,)))
                total = term if total is None else total + term
            column = jnp.sum(d_qkv[...].astype(f32), axis=0, keepdims=True)
            column = jnp.broadcast_to(column, (8, triple)) + (
                0.0 if old is None else old_bias[...]
            )
            if final:
                core = info_ref[1 + docs]
                all_sum[...] = total
                for c, to_ref in ((0, d_w_ref), (1, d_b_ref)):
                    for z in range(shards // 2):
                        at = pl.multiple_of((2 * z + (core ^ c)) * depth, depth)
                        to_ref[z, :depth, :] = all_sum[pl.ds(at, depth), :].astype(bf16)
                        to_ref[z, depth:, :] = jnp.concatenate([column, column]).astype(bf16)
            else:
                d_w_ref[...] = total
                d_b_ref[...] = column
            for r in range(4):
                d_x_ref[r] = mm(
                    d_qkv[r * rows : (r + 1) * rows, :], weight_ref[...], ((1,), (1,))
                ).astype(bf16)

    def part_spec(pick_at):
        return pl.BlockSpec((None, rows, model_width), lambda i, n: (pick_at, 0, 0))

    def whole(shape):
        return pl.BlockSpec(shape, lambda i, n: (0,) * len(shape))

    sum_shapes = [(model_width, triple), (8, triple)]
    last_shapes = [(shards // 2, depth + 16, triple)] * 2 if final else sum_shapes
    return pl.pallas_call(
        body,
        grid_spec=pltpu.PrefetchScalarGridSpec(
            num_scalar_prefetch=1,
            grid=(4,),
            in_specs=[
                whole((length, triple)),
                pl.BlockSpec((None, width, rows), lambda i, n: (i, 0, grad_at)),
                pl.BlockSpec((8, rows), lambda i, n: (0, i)),
            ]
            + [part_spec(p) for p in picks]
            + [whole((model_width, triple))]
            + ([] if before is None else [whole(v) for v in sum_shapes]),
            out_specs=[whole((4, rows, model_width))] + [whole(v) for v in last_shapes],
            scratch_shapes=[
                pltpu.VMEM((heads, length, HEAD_DIM), f32),
                pltpu.VMEM((heads, length, HEAD_DIM), f32),
                pltpu.VMEM((length, triple), bf16),
            ]
            + ([pltpu.VMEM((model_width, triple), f32)] if final else []),
        ),
        out_shape=[jax.ShapeDtypeStruct((4, rows, model_width), bf16)]
        + [jax.ShapeDtypeStruct(v, bf16 if final else f32) for v in last_shapes],
        name="attention_backward",
        cost_estimate=pl.CostEstimate(
            flops=40 * heads * length * length * HEAD_DIM + 4 * length * model_width * triple,
            transcendentals=heads * length * length,
            bytes_accessed=8 * length * model_width,
        ),
    )(info, qkv, grad, lse, *parts, weight, *(() if before is None else before))


def heads_backward(d_branch, heads_out, w_pair, pair_at, small, rows):
    count, model_width = d_branch.shape
    shards, extra = small.shape[0], small.shape[1]
    part = model_width // 4
    depth = model_width // shards

    def body(d_ref, h_ref, w_ref, small_ref, first_ref, rest_ref, tail_ref):
        for r in range(4):
            block = mm(w_ref[r * part : (r + 1) * part, :], d_ref[...], ((1,), (1,)))
            first_ref[r] = block[:, :rows].astype(bf16)
            rest_ref[r] = block[:, rows:].astype(bf16)
        whole = mm(h_ref[...], d_ref[...]).astype(bf16)
        for f in range(shards):
            tail_ref[f, :depth, :] = whole[f * depth : (f + 1) * depth]
            tail_ref[f, depth:, :] = small_ref[f]

    def whole_spec(shape):
        return pl.BlockSpec(shape, lambda i: (0,) * len(shape))

    outs = [(4, part, rows), (4, part, count - rows), (shards, depth + extra, model_width)]
    return pl.pallas_call(
        body,
        grid=(1,),
        in_specs=[
            whole_spec((count, model_width)),
            whole_spec((model_width, count)),
            pl.BlockSpec((model_width, model_width), lambda i: (0, pair_at)),
            whole_spec(small.shape),
        ],
        out_specs=[whole_spec(v) for v in outs],
        out_shape=[jax.ShapeDtypeStruct(v, bf16) for v in outs],
        name="heads_backward",
        cost_estimate=pl.CostEstimate(
            flops=4 * count * model_width * model_width,
            transcendentals=0,
            bytes_accessed=10 * count * model_width,
        ),
    )(d_branch, heads_out, w_pair, small)


def core_add(where, kept, got):
    chips, depth, width = kept.shape

    def body(where_ref, kept_ref, got_ref, own_ref, *to_refs):
        for k, to_ref in enumerate((own_ref,) + to_refs):
            at = lax.rem(where_ref[0] + k, chips)
            total = kept_ref[at].astype(f32) + got_ref[at].astype(f32)
            to_ref[...] = total.astype(to_ref.dtype)

    spec = pl.BlockSpec((chips, depth, width), lambda i, n: (0, 0, 0))
    out = pl.BlockSpec((depth, width), lambda i, n: (0, 0))
    return pl.pallas_call(
        body,
        grid_spec=pltpu.PrefetchScalarGridSpec(
            num_scalar_prefetch=1, grid=(1,), in_specs=[spec, spec], out_specs=[out] * chips
        ),
        out_shape=[jax.ShapeDtypeStruct((depth, width), f32)]
        + [jax.ShapeDtypeStruct((depth, width), bf16)] * (chips - 1),
        name="core_add",
    )(where, kept, got)


def stack_sums(in_kept, in_got, own_kept, own_got):
    depth, width = in_kept.shape
    extent, triple = own_kept.shape
    chips = len(in_got) + 1

    def body(*refs):
        *ins, out_ref = refs

        def total(parts):
            value = parts[0][...].astype(f32)
            for p in parts[1:]:
                value = value + p[...].astype(f32)
            return value.astype(bf16)

        out_ref[:depth, :] = total(ins[:chips])
        out_ref[depth:, :triple] = total(ins[chips:])
        out_ref[depth:, triple:] = jnp.zeros((extent, width - triple), bf16)

    return pl.pallas_call(
        body,
        out_shape=jax.ShapeDtypeStruct((depth + extent, width), bf16),
        name="stack_sums",
    )(in_kept, *in_got, own_kept, *own_got)


def join_columns(me, pieces, in_shape, own_shape):
    depth, width = in_shape
    triple = own_shape[1]
    part, half = triple // 3, width // 2

    def body(me_ref, p0, p1, p2, p3, qkv_ref, bias_ref, in_ref):
        values = [p[...].astype(f32) for p in (p0, p1, p2, p3)]
        for r in range(4):
            piece = values[0]
            for j in (1, 2, 3):
                piece = jnp.where(me_ref[0] == r ^ j, values[j], piece)
            for b in range(3):
                block = piece[depth:, b * part : (b + 1) * part]
                at = b * 4 * part + r * part
                qkv_ref[:, at : at + part] = block[:depth]
                bias_ref[:, at : at + part] = block[depth : depth + 8]
            at = (2 * (r % 2) + r // 2) * half
            in_ref[:, at : at + half] = piece[:depth, :half]
            at = (4 + r) * half
            in_ref[:, at : at + half] = piece[:depth, half:]

    spec = pl.BlockSpec(pieces[0].shape, lambda i, n: (0, 0))
    outs = [(depth, 4 * triple), (8, 4 * triple), (depth, 4 * width)]
    return pl.pallas_call(
        body,
        grid_spec=pltpu.PrefetchScalarGridSpec(
            num_scalar_prefetch=1,
            grid=(1,),
            in_specs=[spec] * 4,
            out_specs=[pl.BlockSpec(v, lambda i, n: (0, 0)) for v in outs],
        ),
        out_shape=[jax.ShapeDtypeStruct(v, f32) for v in outs],
        name="join_columns",
    )(me, *pieces)


def from_peer(value, peer):
    return lax.ppermute(value, "ctx", [(r, r ^ peer) for r in range(4)])


def from_core(value):
    return lax.ppermute(value, "fsdp", [(f, f ^ 1) for f in range(lax.axis_size("fsdp"))])


def pick(stack, index):
    return lax.dynamic_index_in_dim(stack, index, 0, keepdims=False)


def add_sent(own, received):
    return (own.astype(f32) + received.astype(f32)).astype(bf16)


def tie(*values):
    return lax.optimization_barrier(values)


def along_chips(value, hops):
    size = lax.axis_size("fsdp")
    return lax.ppermute(value, "fsdp", [(f, (f + 2 * hops) % size) for f in range(size)])


def core_send(partial):
    core = lax.axis_index("fsdp") % 2
    pairs = partial.reshape((partial.shape[0] // 2, 2) + partial.shape[1:])
    kept = lax.dynamic_index_in_dim(pairs, core, 1, keepdims=False)
    other = lax.dynamic_index_in_dim(pairs, 1 - core, 1, keepdims=False)
    return kept, from_core(other)


def halves(value, axis):
    return jnp.stack(jnp.split(value, 2, axis=axis))


def plane_send(held, me, axis):
    xx, y = me % 2, me // 2
    first, second = jnp.split(held, 2, axis=axis)
    first, second = halves(first, axis), halves(second, axis)
    kept = pick(first, xx), pick(second, y)
    return kept, (from_peer(pick(first, 1 - xx), 1), from_peer(pick(second, 1 - y), 2))


def plane_send_again(kept, received, me, axis):
    xx, y = me % 2, me // 2
    first = halves(add_sent(kept[0], received[0]), axis)
    second = halves(add_sent(kept[1], received[1]), axis)
    kept = pick(first, y), pick(second, xx)
    return kept, (from_peer(pick(first, 1 - y), 2), from_peer(pick(second, 1 - xx), 1))


def join_plane(kept, received, axis):
    return jnp.concatenate([add_sent(k, r) for k, r in zip(kept, received)], axis=axis)


def line_send(parts):
    chips = parts.shape[0]
    z = lax.axis_index("fsdp") // 2
    received = tuple(
        along_chips(pick(parts, (z + k) % chips), k) for k in range(1, chips)
    )
    return pick(parts, z), received


def line_sum(kept, received):
    total = kept.astype(f32)
    for r in received:
        total = total + r.astype(f32)
    return total.astype(bf16)


def exchange(blocks):
    return lax.all_to_all(blocks, "ctx", 0, 0)


def peers_send(value):
    return value, tuple(from_peer(value, j) for j in (1, 2, 3))


def in_rank_order(value, received, me):
    stack = jnp.stack([value] + list(received))
    return [pick(stack, me ^ r) for r in range(4)]


def join_ranks(ranks, axis):
    first, second = zip(*[jnp.split(r, 2, axis=axis) for r in ranks])
    order = [first[2 * b + a] for a in (0, 1) for b in (0, 1)] + list(second)
    return jnp.concatenate(order, axis=axis).astype(f32)


def gelu_parts(inner_act):
    cdf = 0.5 * (1.0 + lax.erf(inner_act * inv_root_two))
    slope = cdf + inner_act * jnp.exp(-0.5 * inner_act * inner_act) * inv_root_tau
    return inner_act * cdf, slope


def on_plane(
    hidden_in,
    doc_starts,
    w_qkv,
    w_attn_out,
    w_ff_in,
    w_ff_out,
    proj_bias,
    ff_in_bias,
    ln_gain,
    ln_shift,
    out_grad,
):
    me = lax.axis_index("ctx")
    micro, _, rows, model_width = hidden_in.shape
    shards = lax.axis_size("fsdp")
    part = model_width // 4
    inner_width = w_ff_in.shape[1]
    streams = [hidden_in[m, 0] for m in range(micro)]

    own_columns = jnp.concatenate(
        [
            lax.dynamic_slice_in_dim(w_qkv, b * model_width + me * part, part, 1)
            for b in range(3)
        ],
        axis=1,
    )
    small = jnp.concatenate([v.reshape(-1) for v in (proj_bias, ff_in_bias, ln_gain, ln_shift)])
    first_rows = jnp.concatenate([own_columns, small.reshape(-1, 3 * part)], axis=0)
    head_got = tuple(from_peer(streams[0], j) for j in (1, 2, 3))
    rest, head_first = hidden_in[1:, 0], hidden_in[0]
    across, along = from_peer(rest, 1), from_peer(rest, 2)
    first_all = lax.all_gather(first_rows, "fsdp", axis=0)
    w_own = first_all[:, : w_qkv.shape[0]].reshape(model_width, 3 * part)
    small_all = first_all[:, w_qkv.shape[0] :].reshape(shards, -1).astype(f32)
    at = 0
    wholes = []
    for count, length in (
        (4, proj_bias.shape[1]),
        (1, ff_in_bias.shape[0]),
        (2, ln_gain.shape[1]),
        (2, ln_shift.shape[1]),
    ):
        piece = small_all[:, at : at + count * length].reshape(shards, count, length)
        wholes.append(piece.transpose(1, 0, 2).reshape(count, shards * length))
        at += count * length
    bias_all, inner_bias, gains, shifts = wholes
    qkv_bias = jnp.concatenate(
        [
            lax.dynamic_slice_in_dim(bias_all[0], me * part, part),
            jnp.zeros((part,), f32),
            lax.dynamic_slice_in_dim(bias_all[1], me * part, part),
        ]
    )

    w_pair = lax.all_gather(
        jnp.concatenate([w_ff_in, w_attn_out], axis=1), "fsdp", axis=0, tiled=True
    )
    w_in_all = w_pair[:, :inner_width]
    w_last_all = lax.all_gather(w_ff_out, "fsdp", axis=0, tiled=True)
    w_out_all = w_pair[:, inner_width:]

    w_own, across, along = tie(w_own, across, along)
    corner = [
        from_peer(across[m : m + 1], 2) if m % 2 == 0 else from_peer(along[m : m + 1], 1)
        for m in range(micro - 1)
    ]

    docs = doc_starts.shape[2]
    rank = lax.axis_index("fsdp")
    bias_rows = jnp.broadcast_to(qkv_bias[None], (8, 3 * part))
    infos = []
    inputs = []
    sequence = []
    pieces = []
    for m in range(micro):
        infos.append(jnp.concatenate([me[None], doc_starts[m, 0], rank[None] % 2]))
        if m == 0:
            parts = (head_first,) + tuple(v[None] for v in head_got)
            picks = (0, 0, 0, 0)
        else:
            parts = (hidden_in.reshape(micro, rows, model_width), across, along, corner[m - 1])
            picks = (m, m - 1, m - 1, 0)
        inputs.append((parts, picks))
        qkv, out, lse = attention_forward(infos[m], parts, picks, w_own, bias_rows, docs)
        sequence.append((qkv, lse))
        pieces.append(exchange(out).reshape(model_width, rows))
    heads_out = jnp.concatenate(pieces, axis=1)
    stream = jnp.concatenate(streams, axis=0)

    first_sum = stream.astype(f32) + mm(heads_out, w_out_all, ((0,), (0,))) + bias_all[2]
    normed, normal_one, inverse_one = layer_norm_parts(first_sum, gains[0], shifts[0])
    normed_low = normed.astype(bf16)
    inner_act = mm(normed_low, w_in_all) + inner_bias[0]
    activated, slope = gelu_parts(inner_act)
    activated = activated.astype(bf16)
    activated, slope = tie(activated, slope.astype(bf16))
    second_sum = normed + mm(activated, w_last_all) + bias_all[3]
    result, normal_two, inverse_two = layer_norm_parts(second_sum, gains[1], shifts[1])

    grad_rows = jnp.concatenate([out_grad[m, 0] for m in range(micro)], axis=0).astype(f32)
    d_second = norm_backward(grad_rows, normal_two, inverse_two, gains[1])
    g_gain_two = jnp.sum(grad_rows * normal_two, axis=0)
    g_shift_two = jnp.sum(grad_rows, axis=0)
    d_ff_out = d_second.astype(bf16)
    g_bias_out = jnp.sum(d_ff_out.astype(f32), axis=0)
    g_w_ff_out = mm(activated, d_ff_out, ((0,), (0,))).astype(bf16)
    d_ff_out, g_w_ff_out = tie(d_ff_out, g_w_ff_out)
    last = lax.psum_scatter(g_w_ff_out, "fsdp", scatter_dimension=0, tiled=True)
    d_inner = (mm(d_ff_out, w_last_all, ((1,), (1,))) * slope.astype(f32)).astype(bf16)
    g_ff_in_bias = jnp.sum(d_inner.astype(f32), axis=0)
    g_w_ff_in = mm(normed_low, d_inner, ((0,), (0,))).astype(bf16)
    in_kept, in_got = core_send(g_w_ff_in.reshape(shards, -1, inner_width))
    d_inner, g_w_ff_in = tie(d_inner, g_w_ff_in)

    d_normed = d_second + mm(d_inner, w_in_all, ((1,), (1,)))
    d_first = norm_backward(d_normed, normal_one, inverse_one, gains[0])
    g_gain_one = jnp.sum(d_normed * normal_one, axis=0)
    g_shift_one = jnp.sum(d_normed, axis=0)
    d_branch = d_first.astype(bf16)
    g_bias_attn = jnp.sum(d_branch.astype(f32), axis=0)
    small_grads = jnp.concatenate(
        [
            v.reshape(-1, shards, v.shape[-1] // shards).transpose(1, 0, 2).reshape(shards, -1)
            for v in (
                jnp.stack([g_bias_attn, g_bias_out]),
                g_ff_in_bias[None],
                jnp.stack([g_gain_one, g_gain_two]),
                jnp.stack([g_shift_one, g_shift_two]),
            )
        ],
        axis=1,
    ).astype(bf16)
    small_count = small_grads.shape[1]
    depth = model_width // shards
    small_rows = 16 * -(-small_count // (16 * model_width))
    small_grads = jnp.pad(small_grads, ((0, 0), (0, small_rows * model_width - small_count)))
    small_grads, in_kept, in_got = tie(small_grads, in_kept, in_got)
    first_heads, rest_heads, tail = heads_backward(
        d_branch,
        heads_out,
        w_pair,
        inner_width // model_width,
        small_grads.reshape(shards, small_rows, model_width),
        rows,
    )
    d_mixed = [exchange(first_heads)]
    rest_heads, d_mixed[0] = tie(rest_heads, d_mixed[0])
    d_mixed.append(exchange(rest_heads))
    tail = lax.psum_scatter(tail, "fsdp", scatter_dimension=0)
    in_kept, in_got = plane_send(add_sent(in_kept, in_got), me, 2)

    sums = []
    own = None
    for m in range(micro):
        qkv, lse = sequence[m]
        parts, picks = inputs[m]
        d_x, *own = attention_backward(
            infos[m],
            qkv,
            d_mixed[min(m, 1)],
            max(m - 1, 0),
            lse,
            parts,
            picks,
            w_own,
            own,
            docs,
            shards if m + 1 == micro else 0,
        )
        if m == 0:
            own[0], in_got, last, d_mixed[1] = tie(own[0], in_got, last, d_mixed[1])
            in_kept, in_got = plane_send_again(in_kept, in_got, me, 2)
            last_got = from_peer(last, 1)
        elif m == 1:
            own[0], in_got, sums[0] = tie(own[0], in_got, sums[0])
            in_kept, in_got = line_send(join_plane(in_kept, in_got, 2))
        elif m == 2:
            own_got = from_core(own[1])
            own[0], last_got, sums[1] = tie(own[0], last_got, sums[1])
            last = add_sent(last, last_got)
            last_got = from_peer(last, 2)
            tail_got = from_peer(tail, 1)
        sums.append(exchange(d_x))
    own_sum, *own_sent = core_add(rank[None] // 2, own[0], own_got)
    own_got = tuple(along_chips(v, k + 1) for k, v in enumerate(own_sent))
    own_sum, tail_got = tie(own_sum, tail_got)
    tail = add_sent(tail, tail_got)
    tail_got = from_peer(tail, 2)
    pieces = stack_sums(in_kept, in_got, own_sum, own_got)
    pieces = (pieces,) + tuple(from_peer(pieces, j) for j in (1, 2, 3))
    g_qkv, both, g_in = join_columns(me[None], pieces, in_kept.shape, own_sum.shape)
    g_qkv, last_got, tail_got = tie(g_qkv, last_got, tail_got)
    both = both[0].reshape(3, model_width)
    in_grad = d_first + jnp.concatenate(
        [jnp.sum(v.astype(f32), axis=0) for v in sums], axis=0
    )
    own_shard = lax.axis_index("fsdp") * proj_bias.shape[1]
    both = lax.dynamic_slice_in_dim(both, own_shard, proj_bias.shape[1], 1)
    g_last = last.astype(f32) + last_got.astype(f32)
    tail = tail.astype(f32) + tail_got.astype(f32)
    g_out = tail[: w_attn_out.shape[0]]
    flat = tail[w_attn_out.shape[0] :].reshape(-1)
    narrow = proj_bias.shape[1]
    bias_pair = flat[: 2 * narrow].reshape(2, narrow)
    at = 2 * narrow
    inner_bias_grad = flat[at : at + ff_in_bias.shape[0]]
    at += ff_in_bias.shape[0]
    gain_grad = flat[at : at + 2 * narrow].reshape(2, narrow)
    at += 2 * narrow
    shift_grad = flat[at : at + 2 * narrow].reshape(2, narrow)
    bias_grad = jnp.concatenate([both[0:1], both[2:3], bias_pair], axis=0)
    return (
        result.astype(bf16).reshape(out_grad.shape),
        in_grad.astype(bf16).reshape(hidden_in.shape),
        g_qkv,
        g_out,
        g_in,
        g_last,
        bias_grad,
        inner_bias_grad,
        gain_grad,
        shift_grad,
    )


def solution(mesh):
    plane = mesh.shape["ctx"] == 4 and mesh.shape["fsdp"] == 8
    return jax.shard_map(
        on_plane if plane else on_device,
        mesh=mesh,
        in_specs=(
            P(None, "fsdp", "ctx", None),
            P(None, "fsdp", None),
            P("fsdp", None),
            P("fsdp", None),
            P("fsdp", None),
            P("fsdp", None),
            P(None, "fsdp"),
            P("fsdp"),
            P(None, "fsdp"),
            P(None, "fsdp"),
            P(None, "fsdp", "ctx", None),
        ),
        out_specs=(
            P(None, "fsdp", "ctx", None),
            P(None, "fsdp", "ctx", None),
            P("fsdp", None),
            P("fsdp", None),
            P("fsdp", None),
            P("fsdp", None),
            P(None, "fsdp"),
            P("fsdp"),
            P(None, "fsdp"),
            P(None, "fsdp"),
        ),
        check_vma=False,
    )
```

```python
import jax
import jax.numpy as jnp
from jax import lax
from jax.experimental import pallas as pl
from jax.experimental.pallas import tpu as pltpu
from jax.sharding import PartitionSpec as P

HEADS = 12
HEAD_DIM = 64


norm_epsilon = 1e-12
masked_score = -1e30
inv_root_two = 0.7071067811865476
inv_root_tau = 0.3989422804014327
log2_e = 1.4426950408889634

def for_sending(value):

    def short(part):
        return part.astype(jnp.bfloat16) if part.dtype == jnp.float32 else part

    return jax.tree.map(short, value)


def layer_norm_parts(values, gain_row, shift_row):
    centre = values - jnp.mean(values, axis=-1, keepdims=True)
    inverse = lax.rsqrt(jnp.mean(centre * centre, axis=-1, keepdims=True) + norm_epsilon)
    normal = centre * inverse
    return (normal * gain_row + shift_row, normal, inverse)


def norm_backward(grad_rows, normal, inverse, gain_row):
    scaled = grad_rows * gain_row
    return inverse * (
        scaled
        - jnp.mean(scaled, axis=-1, keepdims=True)
        - normal * jnp.mean(scaled * normal, axis=-1, keepdims=True)
    )


def gelu_slope(inner_act):
    return (
        0.5 * (1.0 + jax.scipy.special.erf(inner_act * inv_root_two))
        + inner_act * jnp.exp(-0.5 * inner_act * inner_act) * inv_root_tau
    )


def segment_ids(positions, starts):
    return jnp.sum((positions[:, None] >= starts[None, :]).astype(jnp.int32), axis=1)


def gather_weights(shards):
    return (
        lax.all_gather(shards[0], "fsdp", axis=0, tiled=True),
        lax.all_gather(shards[1], "fsdp", axis=0, tiled=True),
        lax.all_gather(shards[2], "fsdp", axis=0, tiled=True),
        lax.all_gather(shards[3], "fsdp", axis=0, tiled=True),
        lax.all_gather(shards[4], "fsdp", axis=1, tiled=True),
        lax.all_gather(shards[5], "fsdp", axis=0, tiled=True),
        lax.all_gather(shards[6], "fsdp", axis=1, tiled=True),
        lax.all_gather(shards[7], "fsdp", axis=1, tiled=True),
    )


def reduce_weights(terms):
    return (
        lax.psum_scatter(
            terms[0].astype(jnp.bfloat16), "fsdp", scatter_dimension=0, tiled=True
        ).astype(jnp.float32),
        lax.psum_scatter(
            terms[1].astype(jnp.bfloat16), "fsdp", scatter_dimension=0, tiled=True
        ).astype(jnp.float32),
        lax.psum_scatter(
            terms[2].astype(jnp.bfloat16), "fsdp", scatter_dimension=0, tiled=True
        ).astype(jnp.float32),
        lax.psum_scatter(
            terms[3].astype(jnp.bfloat16), "fsdp", scatter_dimension=0, tiled=True
        ).astype(jnp.float32),
        lax.psum_scatter(
            terms[4].astype(jnp.bfloat16), "fsdp", scatter_dimension=1, tiled=True
        ).astype(jnp.float32),
        lax.psum_scatter(
            terms[5].astype(jnp.bfloat16), "fsdp", scatter_dimension=0, tiled=True
        ).astype(jnp.float32),
        lax.psum_scatter(
            terms[6].astype(jnp.bfloat16), "fsdp", scatter_dimension=1, tiled=True
        ).astype(jnp.float32),
        lax.psum_scatter(
            terms[7].astype(jnp.bfloat16), "fsdp", scatter_dimension=1, tiled=True
        ).astype(jnp.float32),
    )


def forward_pass(stream, starts, whole, rank_ctx):
    w_qkv, w_attn_out, w_ff_in, w_ff_out, proj_bias, ff_in_bias, ln_gain, ln_shift = whole
    row_count = stream.shape[0]
    model_width = stream.shape[1]
    bias_float = proj_bias.astype(jnp.float32)
    qkv_bias = jnp.concatenate([bias_float[0], jnp.zeros_like(bias_float[0]), bias_float[1]])
    packed = (jnp.dot(stream, w_qkv, preferred_element_type=jnp.float32) + qkv_bias).astype(
        jnp.bfloat16
    )
    query_part = packed[:, :model_width]
    key_part = packed[:, model_width : 2 * model_width]
    value_part = packed[:, 2 * model_width :]
    key_all, value_all = (
        lax.all_gather(key_part, "ctx", axis=0, tiled=True),
        lax.all_gather(value_part, "ctx", axis=0, tiled=True),
    )
    seq_len = key_all.shape[0]
    query_seg = segment_ids(rank_ctx * row_count + jnp.arange(row_count, dtype=jnp.int32), starts)
    key_seg = segment_ids(jnp.arange(seq_len, dtype=jnp.int32), starts)
    same_doc = query_seg[:, None] == key_seg[None, :]
    query_heads = query_part.reshape(row_count, HEADS, HEAD_DIM)
    key_heads = key_all.reshape(seq_len, HEADS, HEAD_DIM)
    value_heads = value_all.reshape(seq_len, HEADS, HEAD_DIM)
    scores = jnp.einsum(
        "qhd,khd->hqk", query_heads, key_heads, preferred_element_type=jnp.float32
    ) * HEAD_DIM ** (-0.5)
    scores = jnp.where(same_doc[None], scores, masked_score)
    row_peak = jnp.max(scores, axis=-1, keepdims=True)
    exp_scores = jnp.exp(scores - row_peak)
    row_total = jnp.sum(exp_scores, axis=-1, keepdims=True)
    attn_probs = exp_scores / row_total
    log_total = row_peak + jnp.log(row_total)
    mixed = jnp.einsum(
        "hqk,khd->qhd",
        attn_probs.astype(jnp.bfloat16),
        value_heads,
        preferred_element_type=jnp.float32,
    ).reshape(row_count, model_width)
    heads_out = mixed.astype(jnp.bfloat16)
    first_sum = (
        stream.astype(jnp.float32)
        + jnp.dot(heads_out, w_attn_out, preferred_element_type=jnp.float32)
        + bias_float[2]
    )
    normed, normal_one, inverse_one = layer_norm_parts(
        first_sum, ln_gain[0].astype(jnp.float32), ln_shift[0].astype(jnp.float32)
    )
    normed_low = normed.astype(jnp.bfloat16)
    inner_act = jnp.dot(
        normed_low, w_ff_in, preferred_element_type=jnp.float32
    ) + ff_in_bias.astype(jnp.float32)
    activated = jax.nn.gelu(inner_act, approximate=False).astype(jnp.bfloat16)
    second_sum = (
        normed + jnp.dot(activated, w_ff_out, preferred_element_type=jnp.float32) + bias_float[3]
    )
    result, normal_two, inverse_two = layer_norm_parts(
        second_sum, ln_gain[1].astype(jnp.float32), ln_shift[1].astype(jnp.float32)
    )
    kept = (
        query_heads,
        key_all,
        value_all,
        same_doc,
        log_total,
        mixed,
        heads_out,
        normal_one,
        inverse_one,
        normed_low,
        inner_act,
        activated,
        normal_two,
        inverse_two,
    )
    return (result, kept)


def backward_pass(grad_rows, stream, kept, whole):
    w_qkv, w_attn_out, w_ff_in, w_ff_out, proj_bias, ff_in_bias, ln_gain, ln_shift = whole
    (
        query_heads,
        key_all,
        value_all,
        same_doc,
        log_total,
        mixed,
        heads_out,
        normal_one,
        inverse_one,
        normed_low,
        inner_act,
        activated,
        normal_two,
        inverse_two,
    ) = kept
    row_count = stream.shape[0]
    model_width = stream.shape[1]
    seq_len = key_all.shape[0]
    scale = HEAD_DIM ** (-0.5)
    d_second = norm_backward(grad_rows, normal_two, inverse_two, ln_gain[1].astype(jnp.float32))
    g_gain_two = jnp.sum(grad_rows * normal_two, axis=0)
    g_shift_two = jnp.sum(grad_rows, axis=0)
    d_ff_out = d_second.astype(jnp.bfloat16)
    g_bias_out = jnp.sum(d_ff_out.astype(jnp.float32), axis=0)
    g_w_ff_out = jnp.einsum("tf,td->fd", activated, d_ff_out, preferred_element_type=jnp.float32)
    d_activated = jnp.einsum("td,fd->tf", d_ff_out, w_ff_out, preferred_element_type=jnp.float32)
    d_inner = (d_activated * gelu_slope(inner_act)).astype(jnp.bfloat16)
    g_ff_in_bias = jnp.sum(d_inner.astype(jnp.float32), axis=0)
    g_w_ff_in = jnp.einsum("td,tf->df", normed_low, d_inner, preferred_element_type=jnp.float32)
    d_normed = d_second + jnp.einsum(
        "tf,df->td", d_inner, w_ff_in, preferred_element_type=jnp.float32
    )
    d_first = norm_backward(d_normed, normal_one, inverse_one, ln_gain[0].astype(jnp.float32))
    g_gain_one = jnp.sum(d_normed * normal_one, axis=0)
    g_shift_one = jnp.sum(d_normed, axis=0)
    d_branch = d_first.astype(jnp.bfloat16)
    g_bias_attn = jnp.sum(d_branch.astype(jnp.float32), axis=0)
    g_w_attn_out = jnp.einsum("tc,td->cd", heads_out, d_branch, preferred_element_type=jnp.float32)
    d_heads = jnp.einsum(
        "td,cd->tc", d_branch, w_attn_out, preferred_element_type=jnp.float32
    ).astype(jnp.bfloat16)
    d_heads_split = d_heads.reshape(row_count, HEADS, HEAD_DIM)
    key_heads = key_all.reshape(seq_len, HEADS, HEAD_DIM)
    value_heads = value_all.reshape(seq_len, HEADS, HEAD_DIM)
    scores = (
        jnp.einsum("qhd,khd->hqk", query_heads, key_heads, preferred_element_type=jnp.float32)
        * scale
    )
    scores = jnp.where(same_doc[None], scores, masked_score)
    attn_probs = jnp.exp(scores - log_total)
    d_probs = jnp.einsum(
        "qhd,khd->hqk", d_heads_split, value_heads, preferred_element_type=jnp.float32
    )
    row_dot = jnp.sum(attn_probs * d_probs, axis=-1)
    d_scores = (attn_probs * (d_probs - row_dot[:, :, None])).astype(jnp.bfloat16)
    d_query = (
        (
            jnp.einsum("hqk,khd->qhd", d_scores, key_heads, preferred_element_type=jnp.float32)
            * scale
        )
        .reshape(row_count, model_width)
        .astype(jnp.bfloat16)
    )
    probs_low = attn_probs.astype(jnp.bfloat16)
    d_key_rows = (
        jnp.einsum("hqk,qhd->khd", d_scores, query_heads, preferred_element_type=jnp.float32)
        * scale
    )
    d_value_rows = jnp.einsum(
        "hqk,qhd->khd", probs_low, d_heads_split, preferred_element_type=jnp.float32
    )
    d_key_value = lax.psum_scatter(
        jnp.concatenate(
            [
                d_key_rows.reshape(lax.axis_size("ctx") * row_count, model_width),
                d_value_rows.reshape(lax.axis_size("ctx") * row_count, model_width),
            ],
            axis=1,
        ).astype(jnp.bfloat16),
        "ctx",
        scatter_dimension=0,
        tiled=True,
    )
    d_packed = jnp.concatenate([d_query, d_key_value], axis=1)
    g_bias_query = jnp.sum(d_query.astype(jnp.float32), axis=0)
    g_bias_value = jnp.sum(d_key_value[:, model_width:].astype(jnp.float32), axis=0)
    g_w_qkv = jnp.einsum("td,te->de", stream, d_packed, preferred_element_type=jnp.float32)
    d_stream = d_first + jnp.einsum(
        "te,de->td", d_packed, w_qkv, preferred_element_type=jnp.float32
    )
    terms = (
        g_w_qkv,
        g_w_attn_out,
        g_w_ff_in,
        g_w_ff_out,
        jnp.stack([g_bias_query, g_bias_value, g_bias_attn, g_bias_out]),
        g_ff_in_bias,
        jnp.stack([g_gain_one, g_gain_two]),
        jnp.stack([g_shift_one, g_shift_two]),
    )
    return (d_stream.astype(jnp.bfloat16), terms)


def on_device(
    hidden_in,
    doc_starts,
    w_qkv,
    w_attn_out,
    w_ff_in,
    w_ff_out,
    proj_bias,
    ff_in_bias,
    ln_gain,
    ln_shift,
    out_grad,
):
    rank_ctx = lax.axis_index("ctx")
    shards = (w_qkv, w_attn_out, w_ff_in, w_ff_out, proj_bias, ff_in_bias, ln_gain, ln_shift)
    output_list = []
    grad_list = []
    running = None
    for micro_step in range(hidden_in.shape[0]):
        stream = hidden_in[micro_step, 0]
        starts = doc_starts[micro_step, 0]
        forward_weights = gather_weights(shards)
        result, kept = forward_pass(stream, starts, forward_weights, rank_ctx)
        backward_weights = gather_weights(shards)
        d_stream, terms = backward_pass(
            out_grad[micro_step, 0].astype(jnp.float32), stream, kept, backward_weights
        )
        if micro_step == 0:
            running = terms
        else:
            running = jax.tree.map(jnp.add, running, terms)
        output_list.append(result.astype(jnp.bfloat16)[None, None])
        grad_list.append(d_stream[None, None])
    running = reduce_weights(running)
    summed = jax.tree.map(
        lambda part: part.astype(jnp.float32), lax.psum(for_sending(running), "ctx")
    )
    return (
        jnp.concatenate(output_list, axis=0),
        jnp.concatenate(grad_list, axis=0),
        summed[0],
        summed[1],
        summed[2],
        summed[3],
        summed[4],
        summed[5],
        summed[6],
        summed[7],
    )

f32 = jnp.float32
bf16 = jnp.bfloat16


def mm(a, b, dims=((1,), (0,))):
    return lax.dot_general(a, b, (dims, ((), ())), preferred_element_type=f32)


def document_bias(info_ref, length, rows, step, docs):
    at = step * rows + lax.broadcasted_iota(jnp.int32, (1, rows), 1)
    low = jnp.zeros((1, rows), jnp.int32)
    high = jnp.full((1, rows), length, jnp.int32)
    for d in range(docs):
        start = info_ref[1 + d]
        low = jnp.where(at >= start, jnp.maximum(low, start), low)
        high = jnp.where(at < start, jnp.minimum(high, start), high)
    other = lax.broadcasted_iota(jnp.int32, (length, rows), 0)
    return jnp.where((other >= low) & (other < high), 0.0, masked_score)


def block_of(info_ref, peer, rows):
    return pl.ds(pl.multiple_of((info_ref[0] ^ peer) * rows, rows), rows)


def attention_forward(info, parts, picks, weight, bias, docs):
    rows = parts[0].shape[-2]
    model_width = parts[0].shape[-1]
    triple = weight.shape[1]
    width = triple // 3
    heads = width // HEAD_DIM
    length = 4 * rows

    def body(info_ref, x0, x1, x2, x3, weight_ref, bias_ref, qkv_ref, out_ref, lse_ref):
        step = pl.program_id(0)

        @pl.when(step == 0)
        def _():
            for peer, x in enumerate((x0, x1, x2, x3)):
                qkv_ref[block_of(info_ref, peer, rows), :] = (
                    mm(x[...], weight_ref[...]) + bias_ref[:1, :]
                ).astype(bf16)

        mask = document_bias(info_ref, length, rows, step, docs)
        here = pl.ds(pl.multiple_of(step * rows, rows), rows)
        for h in range(heads):
            at = h * HEAD_DIM
            query = qkv_ref[here, at : at + HEAD_DIM]
            key = qkv_ref[:, width + at : width + at + HEAD_DIM]
            value = qkv_ref[:, 2 * width + at : 2 * width + at + HEAD_DIM]
            scores = mm(key, query, ((1,), (1,))) * (HEAD_DIM ** (-0.5) * log2_e) + mask
            peak = jnp.max(scores, axis=0, keepdims=True)
            probs = jnp.exp2(scores - peak)
            total = jnp.sum(probs, axis=0, keepdims=True)
            mixed = mm(value, probs.astype(bf16), ((0,), (0,))) / total
            out_ref[at : at + HEAD_DIM, :] = mixed.astype(bf16)
            lse_ref[h : h + 1, :] = peak + jnp.log2(total)

    def part_spec(pick_at):
        return pl.BlockSpec((None, rows, model_width), lambda i, n: (pick_at, 0, 0))

    return pl.pallas_call(
        body,
        grid_spec=pltpu.PrefetchScalarGridSpec(
            num_scalar_prefetch=1,
            grid=(4,),
            in_specs=[part_spec(p) for p in picks]
            + [
                pl.BlockSpec((model_width, triple), lambda i, n: (0, 0)),
                pl.BlockSpec((8, triple), lambda i, n: (0, 0)),
            ],
            out_specs=[
                pl.BlockSpec((length, triple), lambda i, n: (0, 0)),
                pl.BlockSpec((None, width, rows), lambda i, n: (i, 0, 0)),
                pl.BlockSpec((8, rows), lambda i, n: (0, i)),
            ],
        ),
        out_shape=[
            jax.ShapeDtypeStruct((length, triple), bf16),
            jax.ShapeDtypeStruct((4, width, rows), bf16),
            jax.ShapeDtypeStruct((8, length), f32),
        ],
        name="attention_forward",
        cost_estimate=pl.CostEstimate(
            flops=16 * heads * length * length * HEAD_DIM + 2 * length * model_width * triple,
            transcendentals=heads * length * length,
            bytes_accessed=4 * length * model_width,
        ),
    )(info, *parts, weight, bias)


def attention_backward(info, qkv, grad, grad_at, lse, parts, picks, weight, before, docs, shards):
    rows = parts[0].shape[-2]
    model_width = parts[0].shape[-1]
    length, triple = qkv.shape
    width = triple // 3
    heads = width // HEAD_DIM
    scale = HEAD_DIM ** (-0.5)
    final = shards > 0
    depth = model_width // max(shards, 1)

    def body(info_ref, qkv_ref, grad_ref, lse_ref, x0, x1, x2, x3, weight_ref, *rest):
        if before is None:
            old, old_bias = None, None
            d_x_ref, d_w_ref, d_b_ref, key_acc, value_acc, d_qkv, *more = rest
        else:
            old, old_bias, d_x_ref, d_w_ref, d_b_ref, key_acc, value_acc, d_qkv, *more = rest
        all_sum = more[0] if final else None
        step = pl.program_id(0)

        @pl.when(step == 0)
        def _():
            key_acc[...] = jnp.zeros_like(key_acc)
            value_acc[...] = jnp.zeros_like(value_acc)

        mask = document_bias(info_ref, length, rows, step, docs)
        here = pl.ds(pl.multiple_of(step * rows, rows), rows)
        for h in range(heads):
            at = h * HEAD_DIM
            query = qkv_ref[here, at : at + HEAD_DIM]
            grad = grad_ref[at : at + HEAD_DIM, :]
            key = qkv_ref[:, width + at : width + at + HEAD_DIM]
            value = qkv_ref[:, 2 * width + at : 2 * width + at + HEAD_DIM]
            scores = mm(key, query, ((1,), (1,))) * (scale * log2_e) + mask
            probs = jnp.exp2(scores - lse_ref[h : h + 1, :])
            d_probs = mm(value, grad)
            row_dot = jnp.sum(probs * d_probs, axis=0, keepdims=True)
            d_scores = (probs * (d_probs - row_dot)).astype(bf16)
            value_acc[h] += mm(probs.astype(bf16), grad, ((1,), (1,)))
            key_acc[h] += mm(d_scores, query)
            d_query = mm(key, d_scores, ((0,), (0,))) * scale
            d_qkv[here, at : at + HEAD_DIM] = d_query.T.astype(bf16)

        @pl.when(step == 3)
        def _():
            for h in range(heads):
                at = h * HEAD_DIM
                d_qkv[:, width + at : width + at + HEAD_DIM] = (key_acc[h] * scale).astype(bf16)
                d_qkv[:, 2 * width + at : 2 * width + at + HEAD_DIM] = value_acc[h].astype(bf16)
            total = None if old is None else old[...]
            for peer, x in enumerate((x0, x1, x2, x3)):
                term = mm(x[...], d_qkv[block_of(info_ref, peer, rows), :], ((0,), (0,)))
                total = term if total is None else total + term
            column = jnp.sum(d_qkv[...].astype(f32), axis=0, keepdims=True)
            column = jnp.broadcast_to(column, (8, triple)) + (
                0.0 if old is None else old_bias[...]
            )
            if final:
                core = info_ref[1 + docs]
                all_sum[...] = total
                for c, to_ref in ((0, d_w_ref), (1, d_b_ref)):
                    for z in range(shards // 2):
                        at = pl.multiple_of((2 * z + (core ^ c)) * depth, depth)
                        to_ref[z, :depth, :] = all_sum[pl.ds(at, depth), :].astype(bf16)
                        to_ref[z, depth:, :] = jnp.concatenate([column, column]).astype(bf16)
            else:
                d_w_ref[...] = total
                d_b_ref[...] = column
            for r in range(4):
                d_x_ref[r] = mm(
                    d_qkv[r * rows : (r + 1) * rows, :], weight_ref[...], ((1,), (1,))
                ).astype(bf16)

    def part_spec(pick_at):
        return pl.BlockSpec((None, rows, model_width), lambda i, n: (pick_at, 0, 0))

    def whole(shape):
        return pl.BlockSpec(shape, lambda i, n: (0,) * len(shape))

    sum_shapes = [(model_width, triple), (8, triple)]
    last_shapes = [(shards // 2, depth + 16, triple)] * 2 if final else sum_shapes
    return pl.pallas_call(
        body,
        grid_spec=pltpu.PrefetchScalarGridSpec(
            num_scalar_prefetch=1,
            grid=(4,),
            in_specs=[
                whole((length, triple)),
                pl.BlockSpec((None, width, rows), lambda i, n: (i, 0, grad_at)),
                pl.BlockSpec((8, rows), lambda i, n: (0, i)),
            ]
            + [part_spec(p) for p in picks]
            + [whole((model_width, triple))]
            + ([] if before is None else [whole(v) for v in sum_shapes]),
            out_specs=[whole((4, rows, model_width))] + [whole(v) for v in last_shapes],
            scratch_shapes=[
                pltpu.VMEM((heads, length, HEAD_DIM), f32),
                pltpu.VMEM((heads, length, HEAD_DIM), f32),
                pltpu.VMEM((length, triple), bf16),
            ]
            + ([pltpu.VMEM((model_width, triple), f32)] if final else []),
        ),
        out_shape=[jax.ShapeDtypeStruct((4, rows, model_width), bf16)]
        + [jax.ShapeDtypeStruct(v, bf16 if final else f32) for v in last_shapes],
        name="attention_backward",
        cost_estimate=pl.CostEstimate(
            flops=40 * heads * length * length * HEAD_DIM + 4 * length * model_width * triple,
            transcendentals=heads * length * length,
            bytes_accessed=8 * length * model_width,
        ),
    )(info, qkv, grad, lse, *parts, weight, *(() if before is None else before))


def heads_backward(d_branch, heads_out, w_pair, pair_at, small, rows):
    count, model_width = d_branch.shape
    shards, extra = small.shape[0], small.shape[1]
    part = model_width // 4
    depth = model_width // shards

    def body(d_ref, h_ref, w_ref, small_ref, first_ref, rest_ref, tail_ref):
        for r in range(4):
            block = mm(w_ref[r * part : (r + 1) * part, :], d_ref[...], ((1,), (1,)))
            first_ref[r] = block[:, :rows].astype(bf16)
            rest_ref[r] = block[:, rows:].astype(bf16)
        whole = mm(h_ref[...], d_ref[...]).astype(bf16)
        for f in range(shards):
            tail_ref[f, :depth, :] = whole[f * depth : (f + 1) * depth]
            tail_ref[f, depth:, :] = small_ref[f]

    def whole_spec(shape):
        return pl.BlockSpec(shape, lambda i: (0,) * len(shape))

    outs = [(4, part, rows), (4, part, count - rows), (shards, depth + extra, model_width)]
    return pl.pallas_call(
        body,
        grid=(1,),
        in_specs=[
            whole_spec((count, model_width)),
            whole_spec((model_width, count)),
            pl.BlockSpec((model_width, model_width), lambda i: (0, pair_at)),
            whole_spec(small.shape),
        ],
        out_specs=[whole_spec(v) for v in outs],
        out_shape=[jax.ShapeDtypeStruct(v, bf16) for v in outs],
        name="heads_backward",
        cost_estimate=pl.CostEstimate(
            flops=4 * count * model_width * model_width,
            transcendentals=0,
            bytes_accessed=10 * count * model_width,
        ),
    )(d_branch, heads_out, w_pair, small)


def core_add(where, kept, got):
    chips, depth, width = kept.shape

    def body(where_ref, kept_ref, got_ref, own_ref, *to_refs):
        for k, to_ref in enumerate((own_ref,) + to_refs):
            at = lax.rem(where_ref[0] + k, chips)
            total = kept_ref[at].astype(f32) + got_ref[at].astype(f32)
            to_ref[...] = total.astype(to_ref.dtype)

    spec = pl.BlockSpec((chips, depth, width), lambda i, n: (0, 0, 0))
    out = pl.BlockSpec((depth, width), lambda i, n: (0, 0))
    return pl.pallas_call(
        body,
        grid_spec=pltpu.PrefetchScalarGridSpec(
            num_scalar_prefetch=1, grid=(1,), in_specs=[spec, spec], out_specs=[out] * chips
        ),
        out_shape=[jax.ShapeDtypeStruct((depth, width), f32)]
        + [jax.ShapeDtypeStruct((depth, width), bf16)] * (chips - 1),
        name="core_add",
    )(where, kept, got)


def join_columns(me, pieces, depth):
    extent, triple = pieces[0].shape
    part = triple // 3

    def body(me_ref, p0, p1, p2, p3, out_ref, bias_ref):
        values = [p[...].astype(f32) for p in (p0, p1, p2, p3)]
        for r in range(4):
            piece = values[0]
            for j in (1, 2, 3):
                piece = jnp.where(me_ref[0] == r ^ j, values[j], piece)
            for b in range(3):
                block = piece[:, b * part : (b + 1) * part]
                at = b * 4 * part + r * part
                out_ref[:, at : at + part] = block[:depth]
                bias_ref[:, at : at + part] = block[depth : depth + 8]

    spec = pl.BlockSpec((extent, triple), lambda i, n: (0, 0))
    return pl.pallas_call(
        body,
        grid_spec=pltpu.PrefetchScalarGridSpec(
            num_scalar_prefetch=1,
            grid=(1,),
            in_specs=[spec] * 4,
            out_specs=[
                pl.BlockSpec((depth, 4 * triple), lambda i, n: (0, 0)),
                pl.BlockSpec((8, 4 * triple), lambda i, n: (0, 0)),
            ],
        ),
        out_shape=[
            jax.ShapeDtypeStruct((depth, 4 * triple), f32),
            jax.ShapeDtypeStruct((8, 4 * triple), f32),
        ],
        name="join_columns",
    )(me, *pieces)


def from_peer(value, peer):
    return lax.ppermute(value, "ctx", [(r, r ^ peer) for r in range(4)])


def from_core(value):
    return lax.ppermute(value, "fsdp", [(f, f ^ 1) for f in range(lax.axis_size("fsdp"))])


def pick(stack, index):
    return lax.dynamic_index_in_dim(stack, index, 0, keepdims=False)


def add_sent(own, received):
    return (own.astype(f32) + received.astype(f32)).astype(bf16)


def tie(*values):
    return lax.optimization_barrier(values)


def along_chips(value, hops):
    size = lax.axis_size("fsdp")
    return lax.ppermute(value, "fsdp", [(f, (f + 2 * hops) % size) for f in range(size)])


def core_send(partial):
    core = lax.axis_index("fsdp") % 2
    pairs = partial.reshape((partial.shape[0] // 2, 2) + partial.shape[1:])
    kept = lax.dynamic_index_in_dim(pairs, core, 1, keepdims=False)
    other = lax.dynamic_index_in_dim(pairs, 1 - core, 1, keepdims=False)
    return kept, from_core(other)


def halves(value, axis):
    return jnp.stack(jnp.split(value, 2, axis=axis))


def plane_send(held, me, axis):
    xx, y = me % 2, me // 2
    first, second = jnp.split(held, 2, axis=axis)
    first, second = halves(first, axis), halves(second, axis)
    kept = pick(first, xx), pick(second, y)
    return kept, (from_peer(pick(first, 1 - xx), 1), from_peer(pick(second, 1 - y), 2))


def plane_send_again(kept, received, me, axis):
    xx, y = me % 2, me // 2
    first = halves(add_sent(kept[0], received[0]), axis)
    second = halves(add_sent(kept[1], received[1]), axis)
    kept = pick(first, y), pick(second, xx)
    return kept, (from_peer(pick(first, 1 - y), 2), from_peer(pick(second, 1 - xx), 1))


def join_plane(kept, received, axis):
    return jnp.concatenate([add_sent(k, r) for k, r in zip(kept, received)], axis=axis)


def line_send(parts):
    chips = parts.shape[0]
    z = lax.axis_index("fsdp") // 2
    received = tuple(
        along_chips(pick(parts, (z + k) % chips), k) for k in range(1, chips)
    )
    return pick(parts, z), received


def line_sum(kept, received):
    total = kept.astype(f32)
    for r in received:
        total = total + r.astype(f32)
    return total.astype(bf16)


def exchange(blocks):
    return lax.all_to_all(blocks, "ctx", 0, 0)


def peers_send(value):
    return value, tuple(from_peer(value, j) for j in (1, 2, 3))


def in_rank_order(value, received, me):
    stack = jnp.stack([value] + list(received))
    return [pick(stack, me ^ r) for r in range(4)]


def join_ranks(ranks, axis):
    first, second = zip(*[jnp.split(r, 2, axis=axis) for r in ranks])
    order = [first[2 * b + a] for a in (0, 1) for b in (0, 1)] + list(second)
    return jnp.concatenate(order, axis=axis).astype(f32)


def gelu_parts(inner_act):
    cdf = 0.5 * (1.0 + lax.erf(inner_act * inv_root_two))
    slope = cdf + inner_act * jnp.exp(-0.5 * inner_act * inner_act) * inv_root_tau
    return inner_act * cdf, slope


def on_plane(
    hidden_in,
    doc_starts,
    w_qkv,
    w_attn_out,
    w_ff_in,
    w_ff_out,
    proj_bias,
    ff_in_bias,
    ln_gain,
    ln_shift,
    out_grad,
):
    me = lax.axis_index("ctx")
    micro, _, rows, model_width = hidden_in.shape
    shards = lax.axis_size("fsdp")
    part = model_width // 4
    inner_width = w_ff_in.shape[1]
    streams = [hidden_in[m, 0] for m in range(micro)]

    own_columns = jnp.concatenate(
        [
            lax.dynamic_slice_in_dim(w_qkv, b * model_width + me * part, part, 1)
            for b in range(3)
        ],
        axis=1,
    )
    small = jnp.concatenate([v.reshape(-1) for v in (proj_bias, ff_in_bias, ln_gain, ln_shift)])
    first_rows = jnp.concatenate([own_columns, small.reshape(-1, 3 * part)], axis=0)
    head_got = tuple(from_peer(streams[0], j) for j in (1, 2, 3))
    rest, head_first = hidden_in[1:, 0], hidden_in[0]
    across, along = from_peer(rest, 1), from_peer(rest, 2)
    first_all = lax.all_gather(first_rows, "fsdp", axis=0)
    w_own = first_all[:, : w_qkv.shape[0]].reshape(model_width, 3 * part)
    small_all = first_all[:, w_qkv.shape[0] :].reshape(shards, -1).astype(f32)
    at = 0
    wholes = []
    for count, length in (
        (4, proj_bias.shape[1]),
        (1, ff_in_bias.shape[0]),
        (2, ln_gain.shape[1]),
        (2, ln_shift.shape[1]),
    ):
        piece = small_all[:, at : at + count * length].reshape(shards, count, length)
        wholes.append(piece.transpose(1, 0, 2).reshape(count, shards * length))
        at += count * length
    bias_all, inner_bias, gains, shifts = wholes
    qkv_bias = jnp.concatenate(
        [
            lax.dynamic_slice_in_dim(bias_all[0], me * part, part),
            jnp.zeros((part,), f32),
            lax.dynamic_slice_in_dim(bias_all[1], me * part, part),
        ]
    )

    w_pair = lax.all_gather(
        jnp.concatenate([w_ff_in, w_attn_out], axis=1), "fsdp", axis=0, tiled=True
    )
    w_in_all = w_pair[:, :inner_width]
    w_last_all = lax.all_gather(w_ff_out, "fsdp", axis=0, tiled=True)
    w_out_all = w_pair[:, inner_width:]

    w_own, across, along = tie(w_own, across, along)
    corner = [
        from_peer(across[m : m + 1], 2) if m % 2 == 0 else from_peer(along[m : m + 1], 1)
        for m in range(micro - 1)
    ]

    docs = doc_starts.shape[2]
    rank = lax.axis_index("fsdp")
    bias_rows = jnp.broadcast_to(qkv_bias[None], (8, 3 * part))
    infos = []
    inputs = []
    sequence = []
    pieces = []
    for m in range(micro):
        infos.append(jnp.concatenate([me[None], doc_starts[m, 0], rank[None] % 2]))
        if m == 0:
            parts = (head_first,) + tuple(v[None] for v in head_got)
            picks = (0, 0, 0, 0)
        else:
            parts = (hidden_in.reshape(micro, rows, model_width), across, along, corner[m - 1])
            picks = (m, m - 1, m - 1, 0)
        inputs.append((parts, picks))
        qkv, out, lse = attention_forward(infos[m], parts, picks, w_own, bias_rows, docs)
        sequence.append((qkv, lse))
        pieces.append(exchange(out).reshape(model_width, rows))
    heads_out = jnp.concatenate(pieces, axis=1)
    stream = jnp.concatenate(streams, axis=0)

    first_sum = stream.astype(f32) + mm(heads_out, w_out_all, ((0,), (0,))) + bias_all[2]
    normed, normal_one, inverse_one = layer_norm_parts(first_sum, gains[0], shifts[0])
    normed_low = normed.astype(bf16)
    inner_act = mm(normed_low, w_in_all) + inner_bias[0]
    activated, slope = gelu_parts(inner_act)
    activated = activated.astype(bf16)
    activated, slope = tie(activated, slope.astype(bf16))
    second_sum = normed + mm(activated, w_last_all) + bias_all[3]
    result, normal_two, inverse_two = layer_norm_parts(second_sum, gains[1], shifts[1])

    grad_rows = jnp.concatenate([out_grad[m, 0] for m in range(micro)], axis=0).astype(f32)
    d_second = norm_backward(grad_rows, normal_two, inverse_two, gains[1])
    g_gain_two = jnp.sum(grad_rows * normal_two, axis=0)
    g_shift_two = jnp.sum(grad_rows, axis=0)
    d_ff_out = d_second.astype(bf16)
    g_bias_out = jnp.sum(d_ff_out.astype(f32), axis=0)
    g_w_ff_out = mm(activated, d_ff_out, ((0,), (0,))).astype(bf16)
    d_ff_out, g_w_ff_out = tie(d_ff_out, g_w_ff_out)
    last = lax.psum_scatter(g_w_ff_out, "fsdp", scatter_dimension=0, tiled=True)
    d_inner = (mm(d_ff_out, w_last_all, ((1,), (1,))) * slope.astype(f32)).astype(bf16)
    g_ff_in_bias = jnp.sum(d_inner.astype(f32), axis=0)
    g_w_ff_in = mm(normed_low, d_inner, ((0,), (0,))).astype(bf16)
    d_inner, g_w_ff_in = tie(d_inner, g_w_ff_in)
    inside = lax.psum_scatter(g_w_ff_in, "fsdp", scatter_dimension=0, tiled=True)

    d_normed = d_second + mm(d_inner, w_in_all, ((1,), (1,)))
    d_first = norm_backward(d_normed, normal_one, inverse_one, gains[0])
    g_gain_one = jnp.sum(d_normed * normal_one, axis=0)
    g_shift_one = jnp.sum(d_normed, axis=0)
    d_branch = d_first.astype(bf16)
    g_bias_attn = jnp.sum(d_branch.astype(f32), axis=0)
    small_grads = jnp.concatenate(
        [
            v.reshape(-1, shards, v.shape[-1] // shards).transpose(1, 0, 2).reshape(shards, -1)
            for v in (
                jnp.stack([g_bias_attn, g_bias_out]),
                g_ff_in_bias[None],
                jnp.stack([g_gain_one, g_gain_two]),
                jnp.stack([g_shift_one, g_shift_two]),
            )
        ],
        axis=1,
    ).astype(bf16)
    small_count = small_grads.shape[1]
    depth = model_width // shards
    small_rows = 16 * -(-small_count // (16 * model_width))
    small_grads = jnp.pad(small_grads, ((0, 0), (0, small_rows * model_width - small_count)))
    first_heads, rest_heads, tail = heads_backward(
        d_branch,
        heads_out,
        w_pair,
        inner_width // model_width,
        small_grads.reshape(shards, small_rows, model_width),
        rows,
    )
    d_mixed = [exchange(first_heads)]
    rest_heads, d_mixed[0] = tie(rest_heads, d_mixed[0])
    d_mixed.append(exchange(rest_heads))
    tail = lax.psum_scatter(tail, "fsdp", scatter_dimension=0)
    sums = []
    own = None
    for m in range(micro):
        qkv, lse = sequence[m]
        parts, picks = inputs[m]
        d_x, *own = attention_backward(
            infos[m],
            qkv,
            d_mixed[min(m, 1)],
            max(m - 1, 0),
            lse,
            parts,
            picks,
            w_own,
            own,
            docs,
            shards if m + 1 == micro else 0,
        )
        if m == 0:
            own[0], last, d_mixed[1] = tie(own[0], last, d_mixed[1])
            last_got = from_peer(last, 1)
        elif m == 1:
            own[0], last_got, inside, sums[0] = tie(own[0], last_got, inside, sums[0])
            last = add_sent(last, last_got)
            last_got = from_peer(last, 2)
            inside_got = from_peer(inside, 1)
        elif m == 2:
            own_got = from_core(own[1])
            own[0], last_got, inside_got, sums[1] = tie(
                own[0], last_got, inside_got, sums[1]
            )
            inside = add_sent(inside, inside_got)
            inside_got = from_peer(inside, 2)
        sums.append(exchange(d_x))
    own_sum, *own_sent = core_add(rank[None] // 2, own[0], own_got)
    own_got = tuple(along_chips(v, k + 1) for k, v in enumerate(own_sent))
    own_sum, tail = tie(own_sum, tail)
    tail_got = from_peer(tail, 1)
    own_kept = line_sum(own_sum, own_got)
    pieces = (own_kept,) + tuple(from_peer(own_kept, j) for j in (1, 2, 3))
    own_kept, tail_got = tie(own_kept, tail_got)
    tail = add_sent(tail, tail_got)
    tail_got = from_peer(tail, 2)
    g_qkv, both = join_columns(me[None], pieces, depth)
    g_qkv, inside_got, tail_got = tie(g_qkv, inside_got, tail_got)
    both = both[0].reshape(3, model_width)
    in_grad = d_first + jnp.concatenate(
        [jnp.sum(v.astype(f32), axis=0) for v in sums], axis=0
    )
    own_shard = lax.axis_index("fsdp") * proj_bias.shape[1]
    both = lax.dynamic_slice_in_dim(both, own_shard, proj_bias.shape[1], 1)
    g_in = inside.astype(f32) + inside_got.astype(f32)
    g_last = last.astype(f32) + last_got.astype(f32)
    tail = tail.astype(f32) + tail_got.astype(f32)
    g_out = tail[: w_attn_out.shape[0]]
    flat = tail[w_attn_out.shape[0] :].reshape(-1)
    narrow = proj_bias.shape[1]
    bias_pair = flat[: 2 * narrow].reshape(2, narrow)
    at = 2 * narrow
    inner_bias_grad = flat[at : at + ff_in_bias.shape[0]]
    at += ff_in_bias.shape[0]
    gain_grad = flat[at : at + 2 * narrow].reshape(2, narrow)
    at += 2 * narrow
    shift_grad = flat[at : at + 2 * narrow].reshape(2, narrow)
    bias_grad = jnp.concatenate([both[0:1], both[2:3], bias_pair], axis=0)
    return (
        result.astype(bf16).reshape(out_grad.shape),
        in_grad.astype(bf16).reshape(hidden_in.shape),
        g_qkv,
        g_out,
        g_in,
        g_last,
        bias_grad,
        inner_bias_grad,
        gain_grad,
        shift_grad,
    )


def solution(mesh):
    plane = mesh.shape["ctx"] == 4 and mesh.shape["fsdp"] == 8
    return jax.shard_map(
        on_plane if plane else on_device,
        mesh=mesh,
        in_specs=(
            P(None, "fsdp", "ctx", None),
            P(None, "fsdp", None),
            P("fsdp", None),
            P("fsdp", None),
            P("fsdp", None),
            P("fsdp", None),
            P(None, "fsdp"),
            P("fsdp"),
            P(None, "fsdp"),
            P(None, "fsdp"),
            P(None, "fsdp", "ctx", None),
        ),
        out_specs=(
            P(None, "fsdp", "ctx", None),
            P(None, "fsdp", "ctx", None),
            P("fsdp", None),
            P("fsdp", None),
            P("fsdp", None),
            P("fsdp", None),
            P(None, "fsdp"),
            P("fsdp"),
            P(None, "fsdp"),
            P(None, "fsdp"),
        ),
        check_vma=False,
    )
```

```python
import jax
import jax.numpy as jnp
from jax import lax
from jax.experimental import pallas as pl
from jax.experimental.pallas import tpu as pltpu
from jax.sharding import PartitionSpec as P

HEADS = 12
HEAD_DIM = 64


norm_epsilon = 1e-12
masked_score = -1e30
inv_root_two = 0.7071067811865476
inv_root_tau = 0.3989422804014327
log2_e = 1.4426950408889634

def for_sending(value):

    def short(part):
        return part.astype(jnp.bfloat16) if part.dtype == jnp.float32 else part

    return jax.tree.map(short, value)


def layer_norm_parts(values, gain_row, shift_row):
    centre = values - jnp.mean(values, axis=-1, keepdims=True)
    inverse = lax.rsqrt(jnp.mean(centre * centre, axis=-1, keepdims=True) + norm_epsilon)
    normal = centre * inverse
    return (normal * gain_row + shift_row, normal, inverse)


def norm_backward(grad_rows, normal, inverse, gain_row):
    scaled = grad_rows * gain_row
    return inverse * (
        scaled
        - jnp.mean(scaled, axis=-1, keepdims=True)
        - normal * jnp.mean(scaled * normal, axis=-1, keepdims=True)
    )


def gelu_slope(inner_act):
    return (
        0.5 * (1.0 + jax.scipy.special.erf(inner_act * inv_root_two))
        + inner_act * jnp.exp(-0.5 * inner_act * inner_act) * inv_root_tau
    )


def segment_ids(positions, starts):
    return jnp.sum((positions[:, None] >= starts[None, :]).astype(jnp.int32), axis=1)


def gather_weights(shards):
    return (
        lax.all_gather(shards[0], "fsdp", axis=0, tiled=True),
        lax.all_gather(shards[1], "fsdp", axis=0, tiled=True),
        lax.all_gather(shards[2], "fsdp", axis=0, tiled=True),
        lax.all_gather(shards[3], "fsdp", axis=0, tiled=True),
        lax.all_gather(shards[4], "fsdp", axis=1, tiled=True),
        lax.all_gather(shards[5], "fsdp", axis=0, tiled=True),
        lax.all_gather(shards[6], "fsdp", axis=1, tiled=True),
        lax.all_gather(shards[7], "fsdp", axis=1, tiled=True),
    )


def reduce_weights(terms):
    return (
        lax.psum_scatter(
            terms[0].astype(jnp.bfloat16), "fsdp", scatter_dimension=0, tiled=True
        ).astype(jnp.float32),
        lax.psum_scatter(
            terms[1].astype(jnp.bfloat16), "fsdp", scatter_dimension=0, tiled=True
        ).astype(jnp.float32),
        lax.psum_scatter(
            terms[2].astype(jnp.bfloat16), "fsdp", scatter_dimension=0, tiled=True
        ).astype(jnp.float32),
        lax.psum_scatter(
            terms[3].astype(jnp.bfloat16), "fsdp", scatter_dimension=0, tiled=True
        ).astype(jnp.float32),
        lax.psum_scatter(
            terms[4].astype(jnp.bfloat16), "fsdp", scatter_dimension=1, tiled=True
        ).astype(jnp.float32),
        lax.psum_scatter(
            terms[5].astype(jnp.bfloat16), "fsdp", scatter_dimension=0, tiled=True
        ).astype(jnp.float32),
        lax.psum_scatter(
            terms[6].astype(jnp.bfloat16), "fsdp", scatter_dimension=1, tiled=True
        ).astype(jnp.float32),
        lax.psum_scatter(
            terms[7].astype(jnp.bfloat16), "fsdp", scatter_dimension=1, tiled=True
        ).astype(jnp.float32),
    )


def forward_pass(stream, starts, whole, rank_ctx):
    w_qkv, w_attn_out, w_ff_in, w_ff_out, proj_bias, ff_in_bias, ln_gain, ln_shift = whole
    row_count = stream.shape[0]
    model_width = stream.shape[1]
    bias_float = proj_bias.astype(jnp.float32)
    qkv_bias = jnp.concatenate([bias_float[0], jnp.zeros_like(bias_float[0]), bias_float[1]])
    packed = (jnp.dot(stream, w_qkv, preferred_element_type=jnp.float32) + qkv_bias).astype(
        jnp.bfloat16
    )
    query_part = packed[:, :model_width]
    key_part = packed[:, model_width : 2 * model_width]
    value_part = packed[:, 2 * model_width :]
    key_all, value_all = (
        lax.all_gather(key_part, "ctx", axis=0, tiled=True),
        lax.all_gather(value_part, "ctx", axis=0, tiled=True),
    )
    seq_len = key_all.shape[0]
    query_seg = segment_ids(rank_ctx * row_count + jnp.arange(row_count, dtype=jnp.int32), starts)
    key_seg = segment_ids(jnp.arange(seq_len, dtype=jnp.int32), starts)
    same_doc = query_seg[:, None] == key_seg[None, :]
    query_heads = query_part.reshape(row_count, HEADS, HEAD_DIM)
    key_heads = key_all.reshape(seq_len, HEADS, HEAD_DIM)
    value_heads = value_all.reshape(seq_len, HEADS, HEAD_DIM)
    scores = jnp.einsum(
        "qhd,khd->hqk", query_heads, key_heads, preferred_element_type=jnp.float32
    ) * HEAD_DIM ** (-0.5)
    scores = jnp.where(same_doc[None], scores, masked_score)
    row_peak = jnp.max(scores, axis=-1, keepdims=True)
    exp_scores = jnp.exp(scores - row_peak)
    row_total = jnp.sum(exp_scores, axis=-1, keepdims=True)
    attn_probs = exp_scores / row_total
    log_total = row_peak + jnp.log(row_total)
    mixed = jnp.einsum(
        "hqk,khd->qhd",
        attn_probs.astype(jnp.bfloat16),
        value_heads,
        preferred_element_type=jnp.float32,
    ).reshape(row_count, model_width)
    heads_out = mixed.astype(jnp.bfloat16)
    first_sum = (
        stream.astype(jnp.float32)
        + jnp.dot(heads_out, w_attn_out, preferred_element_type=jnp.float32)
        + bias_float[2]
    )
    normed, normal_one, inverse_one = layer_norm_parts(
        first_sum, ln_gain[0].astype(jnp.float32), ln_shift[0].astype(jnp.float32)
    )
    normed_low = normed.astype(jnp.bfloat16)
    inner_act = jnp.dot(
        normed_low, w_ff_in, preferred_element_type=jnp.float32
    ) + ff_in_bias.astype(jnp.float32)
    activated = jax.nn.gelu(inner_act, approximate=False).astype(jnp.bfloat16)
    second_sum = (
        normed + jnp.dot(activated, w_ff_out, preferred_element_type=jnp.float32) + bias_float[3]
    )
    result, normal_two, inverse_two = layer_norm_parts(
        second_sum, ln_gain[1].astype(jnp.float32), ln_shift[1].astype(jnp.float32)
    )
    kept = (
        query_heads,
        key_all,
        value_all,
        same_doc,
        log_total,
        mixed,
        heads_out,
        normal_one,
        inverse_one,
        normed_low,
        inner_act,
        activated,
        normal_two,
        inverse_two,
    )
    return (result, kept)


def backward_pass(grad_rows, stream, kept, whole):
    w_qkv, w_attn_out, w_ff_in, w_ff_out, proj_bias, ff_in_bias, ln_gain, ln_shift = whole
    (
        query_heads,
        key_all,
        value_all,
        same_doc,
        log_total,
        mixed,
        heads_out,
        normal_one,
        inverse_one,
        normed_low,
        inner_act,
        activated,
        normal_two,
        inverse_two,
    ) = kept
    row_count = stream.shape[0]
    model_width = stream.shape[1]
    seq_len = key_all.shape[0]
    scale = HEAD_DIM ** (-0.5)
    d_second = norm_backward(grad_rows, normal_two, inverse_two, ln_gain[1].astype(jnp.float32))
    g_gain_two = jnp.sum(grad_rows * normal_two, axis=0)
    g_shift_two = jnp.sum(grad_rows, axis=0)
    d_ff_out = d_second.astype(jnp.bfloat16)
    g_bias_out = jnp.sum(d_ff_out.astype(jnp.float32), axis=0)
    g_w_ff_out = jnp.einsum("tf,td->fd", activated, d_ff_out, preferred_element_type=jnp.float32)
    d_activated = jnp.einsum("td,fd->tf", d_ff_out, w_ff_out, preferred_element_type=jnp.float32)
    d_inner = (d_activated * gelu_slope(inner_act)).astype(jnp.bfloat16)
    g_ff_in_bias = jnp.sum(d_inner.astype(jnp.float32), axis=0)
    g_w_ff_in = jnp.einsum("td,tf->df", normed_low, d_inner, preferred_element_type=jnp.float32)
    d_normed = d_second + jnp.einsum(
        "tf,df->td", d_inner, w_ff_in, preferred_element_type=jnp.float32
    )
    d_first = norm_backward(d_normed, normal_one, inverse_one, ln_gain[0].astype(jnp.float32))
    g_gain_one = jnp.sum(d_normed * normal_one, axis=0)
    g_shift_one = jnp.sum(d_normed, axis=0)
    d_branch = d_first.astype(jnp.bfloat16)
    g_bias_attn = jnp.sum(d_branch.astype(jnp.float32), axis=0)
    g_w_attn_out = jnp.einsum("tc,td->cd", heads_out, d_branch, preferred_element_type=jnp.float32)
    d_heads = jnp.einsum(
        "td,cd->tc", d_branch, w_attn_out, preferred_element_type=jnp.float32
    ).astype(jnp.bfloat16)
    d_heads_split = d_heads.reshape(row_count, HEADS, HEAD_DIM)
    key_heads = key_all.reshape(seq_len, HEADS, HEAD_DIM)
    value_heads = value_all.reshape(seq_len, HEADS, HEAD_DIM)
    scores = (
        jnp.einsum("qhd,khd->hqk", query_heads, key_heads, preferred_element_type=jnp.float32)
        * scale
    )
    scores = jnp.where(same_doc[None], scores, masked_score)
    attn_probs = jnp.exp(scores - log_total)
    d_probs = jnp.einsum(
        "qhd,khd->hqk", d_heads_split, value_heads, preferred_element_type=jnp.float32
    )
    row_dot = jnp.sum(attn_probs * d_probs, axis=-1)
    d_scores = (attn_probs * (d_probs - row_dot[:, :, None])).astype(jnp.bfloat16)
    d_query = (
        (
            jnp.einsum("hqk,khd->qhd", d_scores, key_heads, preferred_element_type=jnp.float32)
            * scale
        )
        .reshape(row_count, model_width)
        .astype(jnp.bfloat16)
    )
    probs_low = attn_probs.astype(jnp.bfloat16)
    d_key_rows = (
        jnp.einsum("hqk,qhd->khd", d_scores, query_heads, preferred_element_type=jnp.float32)
        * scale
    )
    d_value_rows = jnp.einsum(
        "hqk,qhd->khd", probs_low, d_heads_split, preferred_element_type=jnp.float32
    )
    d_key_value = lax.psum_scatter(
        jnp.concatenate(
            [
                d_key_rows.reshape(lax.axis_size("ctx") * row_count, model_width),
                d_value_rows.reshape(lax.axis_size("ctx") * row_count, model_width),
            ],
            axis=1,
        ).astype(jnp.bfloat16),
        "ctx",
        scatter_dimension=0,
        tiled=True,
    )
    d_packed = jnp.concatenate([d_query, d_key_value], axis=1)
    g_bias_query = jnp.sum(d_query.astype(jnp.float32), axis=0)
    g_bias_value = jnp.sum(d_key_value[:, model_width:].astype(jnp.float32), axis=0)
    g_w_qkv = jnp.einsum("td,te->de", stream, d_packed, preferred_element_type=jnp.float32)
    d_stream = d_first + jnp.einsum(
        "te,de->td", d_packed, w_qkv, preferred_element_type=jnp.float32
    )
    terms = (
        g_w_qkv,
        g_w_attn_out,
        g_w_ff_in,
        g_w_ff_out,
        jnp.stack([g_bias_query, g_bias_value, g_bias_attn, g_bias_out]),
        g_ff_in_bias,
        jnp.stack([g_gain_one, g_gain_two]),
        jnp.stack([g_shift_one, g_shift_two]),
    )
    return (d_stream.astype(jnp.bfloat16), terms)


def on_device(
    hidden_in,
    doc_starts,
    w_qkv,
    w_attn_out,
    w_ff_in,
    w_ff_out,
    proj_bias,
    ff_in_bias,
    ln_gain,
    ln_shift,
    out_grad,
):
    rank_ctx = lax.axis_index("ctx")
    shards = (w_qkv, w_attn_out, w_ff_in, w_ff_out, proj_bias, ff_in_bias, ln_gain, ln_shift)
    output_list = []
    grad_list = []
    running = None
    for micro_step in range(hidden_in.shape[0]):
        stream = hidden_in[micro_step, 0]
        starts = doc_starts[micro_step, 0]
        forward_weights = gather_weights(shards)
        result, kept = forward_pass(stream, starts, forward_weights, rank_ctx)
        backward_weights = gather_weights(shards)
        d_stream, terms = backward_pass(
            out_grad[micro_step, 0].astype(jnp.float32), stream, kept, backward_weights
        )
        if micro_step == 0:
            running = terms
        else:
            running = jax.tree.map(jnp.add, running, terms)
        output_list.append(result.astype(jnp.bfloat16)[None, None])
        grad_list.append(d_stream[None, None])
    running = reduce_weights(running)
    summed = jax.tree.map(
        lambda part: part.astype(jnp.float32), lax.psum(for_sending(running), "ctx")
    )
    return (
        jnp.concatenate(output_list, axis=0),
        jnp.concatenate(grad_list, axis=0),
        summed[0],
        summed[1],
        summed[2],
        summed[3],
        summed[4],
        summed[5],
        summed[6],
        summed[7],
    )

f32 = jnp.float32
bf16 = jnp.bfloat16


def mm(a, b, dims=((1,), (0,))):
    return lax.dot_general(a, b, (dims, ((), ())), preferred_element_type=f32)


def document_bias(info_ref, length, rows, step, docs):
    at = step * rows + lax.broadcasted_iota(jnp.int32, (1, rows), 1)
    low = jnp.zeros((1, rows), jnp.int32)
    high = jnp.full((1, rows), length, jnp.int32)
    for d in range(docs):
        start = info_ref[1 + d]
        low = jnp.where(at >= start, jnp.maximum(low, start), low)
        high = jnp.where(at < start, jnp.minimum(high, start), high)
    other = lax.broadcasted_iota(jnp.int32, (length, rows), 0)
    return jnp.where((other >= low) & (other < high), 0.0, masked_score)


def block_of(info_ref, peer, rows):
    return pl.ds(pl.multiple_of((info_ref[0] ^ peer) * rows, rows), rows)


def attention_forward(info, parts, picks, weight, bias, docs):
    rows = parts[0].shape[-2]
    model_width = parts[0].shape[-1]
    triple = weight.shape[1]
    width = triple // 3
    heads = width // HEAD_DIM
    length = 4 * rows

    def body(info_ref, x0, x1, x2, x3, weight_ref, bias_ref, qkv_ref, out_ref, lse_ref):
        step = pl.program_id(0)

        @pl.when(step == 0)
        def _():
            for peer, x in enumerate((x0, x1, x2, x3)):
                qkv_ref[block_of(info_ref, peer, rows), :] = (
                    mm(x[...], weight_ref[...]) + bias_ref[:1, :]
                ).astype(bf16)

        mask = document_bias(info_ref, length, rows, step, docs)
        here = pl.ds(pl.multiple_of(step * rows, rows), rows)
        for h in range(heads):
            at = h * HEAD_DIM
            query = qkv_ref[here, at : at + HEAD_DIM]
            key = qkv_ref[:, width + at : width + at + HEAD_DIM]
            value = qkv_ref[:, 2 * width + at : 2 * width + at + HEAD_DIM]
            scores = mm(key, query, ((1,), (1,))) * (HEAD_DIM ** (-0.5) * log2_e) + mask
            peak = jnp.max(scores, axis=0, keepdims=True)
            probs = jnp.exp2(scores - peak)
            total = jnp.sum(probs, axis=0, keepdims=True)
            mixed = mm(value, probs.astype(bf16), ((0,), (0,))) / total
            out_ref[at : at + HEAD_DIM, :] = mixed.astype(bf16)
            lse_ref[h : h + 1, :] = peak + jnp.log2(total)

    def part_spec(pick_at):
        return pl.BlockSpec((None, rows, model_width), lambda i, n: (pick_at, 0, 0))

    return pl.pallas_call(
        body,
        grid_spec=pltpu.PrefetchScalarGridSpec(
            num_scalar_prefetch=1,
            grid=(4,),
            in_specs=[part_spec(p) for p in picks]
            + [
                pl.BlockSpec((model_width, triple), lambda i, n: (0, 0)),
                pl.BlockSpec((8, triple), lambda i, n: (0, 0)),
            ],
            out_specs=[
                pl.BlockSpec((length, triple), lambda i, n: (0, 0)),
                pl.BlockSpec((None, width, rows), lambda i, n: (i, 0, 0)),
                pl.BlockSpec((8, rows), lambda i, n: (0, i)),
            ],
        ),
        out_shape=[
            jax.ShapeDtypeStruct((length, triple), bf16),
            jax.ShapeDtypeStruct((4, width, rows), bf16),
            jax.ShapeDtypeStruct((8, length), f32),
        ],
        name="attention_forward",
        cost_estimate=pl.CostEstimate(
            flops=16 * heads * length * length * HEAD_DIM + 2 * length * model_width * triple,
            transcendentals=heads * length * length,
            bytes_accessed=4 * length * model_width,
        ),
    )(info, *parts, weight, bias)


def attention_backward(info, qkv, grad, grad_at, lse, parts, picks, weight, before, docs, shards):
    rows = parts[0].shape[-2]
    model_width = parts[0].shape[-1]
    length, triple = qkv.shape
    width = triple // 3
    heads = width // HEAD_DIM
    scale = HEAD_DIM ** (-0.5)
    final = shards > 0
    depth = model_width // max(shards, 1)

    def body(info_ref, qkv_ref, grad_ref, lse_ref, x0, x1, x2, x3, weight_ref, *rest):
        if before is None:
            old, old_bias = None, None
            d_x_ref, d_w_ref, d_b_ref, key_acc, value_acc, d_qkv, *more = rest
        else:
            old, old_bias, d_x_ref, d_w_ref, d_b_ref, key_acc, value_acc, d_qkv, *more = rest
        all_sum = more[0] if final else None
        step = pl.program_id(0)

        @pl.when(step == 0)
        def _():
            key_acc[...] = jnp.zeros_like(key_acc)
            value_acc[...] = jnp.zeros_like(value_acc)

        mask = document_bias(info_ref, length, rows, step, docs)
        here = pl.ds(pl.multiple_of(step * rows, rows), rows)
        for h in range(heads):
            at = h * HEAD_DIM
            query = qkv_ref[here, at : at + HEAD_DIM]
            grad = grad_ref[at : at + HEAD_DIM, :]
            key = qkv_ref[:, width + at : width + at + HEAD_DIM]
            value = qkv_ref[:, 2 * width + at : 2 * width + at + HEAD_DIM]
            scores = mm(key, query, ((1,), (1,))) * (scale * log2_e) + mask
            probs = jnp.exp2(scores - lse_ref[h : h + 1, :])
            d_probs = mm(value, grad)
            row_dot = jnp.sum(probs * d_probs, axis=0, keepdims=True)
            d_scores = (probs * (d_probs - row_dot)).astype(bf16)
            value_acc[h] += mm(probs.astype(bf16), grad, ((1,), (1,)))
            key_acc[h] += mm(d_scores, query)
            d_query = mm(key, d_scores, ((0,), (0,))) * scale
            d_qkv[here, at : at + HEAD_DIM] = d_query.T.astype(bf16)

        @pl.when(step == 3)
        def _():
            for h in range(heads):
                at = h * HEAD_DIM
                d_qkv[:, width + at : width + at + HEAD_DIM] = (key_acc[h] * scale).astype(bf16)
                d_qkv[:, 2 * width + at : 2 * width + at + HEAD_DIM] = value_acc[h].astype(bf16)
            total = None if old is None else old[...]
            for peer, x in enumerate((x0, x1, x2, x3)):
                term = mm(x[...], d_qkv[block_of(info_ref, peer, rows), :], ((0,), (0,)))
                total = term if total is None else total + term
            column = jnp.sum(d_qkv[...].astype(f32), axis=0, keepdims=True)
            column = jnp.broadcast_to(column, (8, triple)) + (
                0.0 if old is None else old_bias[...]
            )
            if final:
                core = info_ref[1 + docs]
                all_sum[...] = total
                for c, to_ref in ((0, d_w_ref), (1, d_b_ref)):
                    for z in range(shards // 2):
                        at = pl.multiple_of((2 * z + (core ^ c)) * depth, depth)
                        to_ref[z, :depth, :] = all_sum[pl.ds(at, depth), :].astype(bf16)
                        to_ref[z, depth:, :] = jnp.concatenate([column, column]).astype(bf16)
            else:
                d_w_ref[...] = total
                d_b_ref[...] = column
            for r in range(4):
                d_x_ref[r] = mm(
                    d_qkv[r * rows : (r + 1) * rows, :], weight_ref[...], ((1,), (1,))
                ).astype(bf16)

    def part_spec(pick_at):
        return pl.BlockSpec((None, rows, model_width), lambda i, n: (pick_at, 0, 0))

    def whole(shape):
        return pl.BlockSpec(shape, lambda i, n: (0,) * len(shape))

    sum_shapes = [(model_width, triple), (8, triple)]
    last_shapes = [(shards // 2, depth + 16, triple)] * 2 if final else sum_shapes
    return pl.pallas_call(
        body,
        grid_spec=pltpu.PrefetchScalarGridSpec(
            num_scalar_prefetch=1,
            grid=(4,),
            in_specs=[
                whole((length, triple)),
                pl.BlockSpec((None, width, rows), lambda i, n: (i, 0, grad_at)),
                pl.BlockSpec((8, rows), lambda i, n: (0, i)),
            ]
            + [part_spec(p) for p in picks]
            + [whole((model_width, triple))]
            + ([] if before is None else [whole(v) for v in sum_shapes]),
            out_specs=[whole((4, rows, model_width))] + [whole(v) for v in last_shapes],
            scratch_shapes=[
                pltpu.VMEM((heads, length, HEAD_DIM), f32),
                pltpu.VMEM((heads, length, HEAD_DIM), f32),
                pltpu.VMEM((length, triple), bf16),
            ]
            + ([pltpu.VMEM((model_width, triple), f32)] if final else []),
        ),
        out_shape=[jax.ShapeDtypeStruct((4, rows, model_width), bf16)]
        + [jax.ShapeDtypeStruct(v, bf16 if final else f32) for v in last_shapes],
        name="attention_backward",
        cost_estimate=pl.CostEstimate(
            flops=40 * heads * length * length * HEAD_DIM + 4 * length * model_width * triple,
            transcendentals=heads * length * length,
            bytes_accessed=8 * length * model_width,
        ),
    )(info, qkv, grad, lse, *parts, weight, *(() if before is None else before))


def heads_backward(d_branch, heads_out, w_pair, pair_at, small, rows):
    count, model_width = d_branch.shape
    shards, extra = small.shape[0], small.shape[1]
    part = model_width // 4
    depth = model_width // shards

    def body(d_ref, h_ref, w_ref, small_ref, first_ref, rest_ref, tail_ref):
        for r in range(4):
            block = mm(w_ref[r * part : (r + 1) * part, :], d_ref[...], ((1,), (1,)))
            first_ref[r] = block[:, :rows].astype(bf16)
            rest_ref[r] = block[:, rows:].astype(bf16)
        whole = mm(h_ref[...], d_ref[...]).astype(bf16)
        for f in range(shards):
            tail_ref[f, :depth, :] = whole[f * depth : (f + 1) * depth]
            tail_ref[f, depth:, :] = small_ref[f]

    def whole_spec(shape):
        return pl.BlockSpec(shape, lambda i: (0,) * len(shape))

    outs = [(4, part, rows), (4, part, count - rows), (shards, depth + extra, model_width)]
    return pl.pallas_call(
        body,
        grid=(1,),
        in_specs=[
            whole_spec((count, model_width)),
            whole_spec((model_width, count)),
            pl.BlockSpec((model_width, model_width), lambda i: (0, pair_at)),
            whole_spec(small.shape),
        ],
        out_specs=[whole_spec(v) for v in outs],
        out_shape=[jax.ShapeDtypeStruct(v, bf16) for v in outs],
        name="heads_backward",
        cost_estimate=pl.CostEstimate(
            flops=4 * count * model_width * model_width,
            transcendentals=0,
            bytes_accessed=10 * count * model_width,
        ),
    )(d_branch, heads_out, w_pair, small)


def core_add(where, kept, got):
    chips, depth, width = kept.shape

    def body(where_ref, kept_ref, got_ref, own_ref, *to_refs):
        for k, to_ref in enumerate((own_ref,) + to_refs):
            at = lax.rem(where_ref[0] + k, chips)
            total = kept_ref[at].astype(f32) + got_ref[at].astype(f32)
            to_ref[...] = total.astype(to_ref.dtype)

    spec = pl.BlockSpec((chips, depth, width), lambda i, n: (0, 0, 0))
    out = pl.BlockSpec((depth, width), lambda i, n: (0, 0))
    return pl.pallas_call(
        body,
        grid_spec=pltpu.PrefetchScalarGridSpec(
            num_scalar_prefetch=1, grid=(1,), in_specs=[spec, spec], out_specs=[out] * chips
        ),
        out_shape=[jax.ShapeDtypeStruct((depth, width), f32)]
        + [jax.ShapeDtypeStruct((depth, width), bf16)] * (chips - 1),
        name="core_add",
    )(where, kept, got)


def join_columns(me, pieces, depth):
    extent, triple = pieces[0].shape
    part = triple // 3

    def body(me_ref, p0, p1, p2, p3, out_ref, bias_ref):
        values = [p[...].astype(f32) for p in (p0, p1, p2, p3)]
        for r in range(4):
            piece = values[0]
            for j in (1, 2, 3):
                piece = jnp.where(me_ref[0] == r ^ j, values[j], piece)
            for b in range(3):
                block = piece[:, b * part : (b + 1) * part]
                at = b * 4 * part + r * part
                out_ref[:, at : at + part] = block[:depth]
                bias_ref[:, at : at + part] = block[depth : depth + 8]

    spec = pl.BlockSpec((extent, triple), lambda i, n: (0, 0))
    return pl.pallas_call(
        body,
        grid_spec=pltpu.PrefetchScalarGridSpec(
            num_scalar_prefetch=1,
            grid=(1,),
            in_specs=[spec] * 4,
            out_specs=[
                pl.BlockSpec((depth, 4 * triple), lambda i, n: (0, 0)),
                pl.BlockSpec((8, 4 * triple), lambda i, n: (0, 0)),
            ],
        ),
        out_shape=[
            jax.ShapeDtypeStruct((depth, 4 * triple), f32),
            jax.ShapeDtypeStruct((8, 4 * triple), f32),
        ],
        name="join_columns",
    )(me, *pieces)


def from_peer(value, peer):
    return lax.ppermute(value, "ctx", [(r, r ^ peer) for r in range(4)])


def from_core(value):
    return lax.ppermute(value, "fsdp", [(f, f ^ 1) for f in range(lax.axis_size("fsdp"))])


def pick(stack, index):
    return lax.dynamic_index_in_dim(stack, index, 0, keepdims=False)


def add_sent(own, received):
    return (own.astype(f32) + received.astype(f32)).astype(bf16)


def tie(*values):
    return lax.optimization_barrier(values)


def along_chips(value, hops):
    size = lax.axis_size("fsdp")
    return lax.ppermute(value, "fsdp", [(f, (f + 2 * hops) % size) for f in range(size)])


def core_send(partial):
    core = lax.axis_index("fsdp") % 2
    pairs = partial.reshape((partial.shape[0] // 2, 2) + partial.shape[1:])
    kept = lax.dynamic_index_in_dim(pairs, core, 1, keepdims=False)
    other = lax.dynamic_index_in_dim(pairs, 1 - core, 1, keepdims=False)
    return kept, from_core(other)


def halves(value, axis):
    return jnp.stack(jnp.split(value, 2, axis=axis))


def plane_send(held, me, axis):
    xx, y = me % 2, me // 2
    first, second = jnp.split(held, 2, axis=axis)
    first, second = halves(first, axis), halves(second, axis)
    kept = pick(first, xx), pick(second, y)
    return kept, (from_peer(pick(first, 1 - xx), 1), from_peer(pick(second, 1 - y), 2))


def plane_send_again(kept, received, me, axis):
    xx, y = me % 2, me // 2
    first = halves(add_sent(kept[0], received[0]), axis)
    second = halves(add_sent(kept[1], received[1]), axis)
    kept = pick(first, y), pick(second, xx)
    return kept, (from_peer(pick(first, 1 - y), 2), from_peer(pick(second, 1 - xx), 1))


def join_plane(kept, received, axis):
    return jnp.concatenate([add_sent(k, r) for k, r in zip(kept, received)], axis=axis)


def line_send(parts):
    chips = parts.shape[0]
    z = lax.axis_index("fsdp") // 2
    received = tuple(
        along_chips(pick(parts, (z + k) % chips), k) for k in range(1, chips)
    )
    return pick(parts, z), received


def line_sum(kept, received):
    total = kept.astype(f32)
    for r in received:
        total = total + r.astype(f32)
    return total.astype(bf16)


def exchange(blocks):
    return lax.all_to_all(blocks, "ctx", 0, 0)


def peers_send(value):
    return value, tuple(from_peer(value, j) for j in (1, 2, 3))


def in_rank_order(value, received, me):
    stack = jnp.stack([value] + list(received))
    return [pick(stack, me ^ r) for r in range(4)]


def join_ranks(ranks, axis):
    first, second = zip(*[jnp.split(r, 2, axis=axis) for r in ranks])
    order = [first[2 * b + a] for a in (0, 1) for b in (0, 1)] + list(second)
    return jnp.concatenate(order, axis=axis).astype(f32)


def gelu_parts(inner_act):
    cdf = 0.5 * (1.0 + lax.erf(inner_act * inv_root_two))
    slope = cdf + inner_act * jnp.exp(-0.5 * inner_act * inner_act) * inv_root_tau
    return inner_act * cdf, slope


def on_plane(
    hidden_in,
    doc_starts,
    w_qkv,
    w_attn_out,
    w_ff_in,
    w_ff_out,
    proj_bias,
    ff_in_bias,
    ln_gain,
    ln_shift,
    out_grad,
):
    me = lax.axis_index("ctx")
    micro, _, rows, model_width = hidden_in.shape
    shards = lax.axis_size("fsdp")
    part = model_width // 4
    inner_width = w_ff_in.shape[1]
    streams = [hidden_in[m, 0] for m in range(micro)]

    own_columns = jnp.concatenate(
        [
            lax.dynamic_slice_in_dim(w_qkv, b * model_width + me * part, part, 1)
            for b in range(3)
        ],
        axis=1,
    )
    small = jnp.concatenate([v.reshape(-1) for v in (proj_bias, ff_in_bias, ln_gain, ln_shift)])
    first_rows = jnp.concatenate([own_columns, small.reshape(-1, 3 * part)], axis=0)
    head_got = tuple(from_peer(streams[0], j) for j in (1, 2, 3))
    rest, head_first = hidden_in[1:, 0], hidden_in[0]
    across, along = from_peer(rest, 1), from_peer(rest, 2)
    first_all = lax.all_gather(first_rows, "fsdp", axis=0)
    w_own = first_all[:, : w_qkv.shape[0]].reshape(model_width, 3 * part)
    small_all = first_all[:, w_qkv.shape[0] :].reshape(shards, -1).astype(f32)
    at = 0
    wholes = []
    for count, length in (
        (4, proj_bias.shape[1]),
        (1, ff_in_bias.shape[0]),
        (2, ln_gain.shape[1]),
        (2, ln_shift.shape[1]),
    ):
        piece = small_all[:, at : at + count * length].reshape(shards, count, length)
        wholes.append(piece.transpose(1, 0, 2).reshape(count, shards * length))
        at += count * length
    bias_all, inner_bias, gains, shifts = wholes
    qkv_bias = jnp.concatenate(
        [
            lax.dynamic_slice_in_dim(bias_all[0], me * part, part),
            jnp.zeros((part,), f32),
            lax.dynamic_slice_in_dim(bias_all[1], me * part, part),
        ]
    )

    w_pair = lax.all_gather(
        jnp.concatenate([w_ff_in, w_attn_out], axis=1), "fsdp", axis=0, tiled=True
    )
    w_in_all = w_pair[:, :inner_width]
    w_last_all = lax.all_gather(w_ff_out, "fsdp", axis=0, tiled=True)
    w_out_all = w_pair[:, inner_width:]

    w_own, across, along = tie(w_own, across, along)
    corner = [
        from_peer(across[m : m + 1], 2) if m % 2 == 0 else from_peer(along[m : m + 1], 1)
        for m in range(micro - 1)
    ]

    docs = doc_starts.shape[2]
    rank = lax.axis_index("fsdp")
    bias_rows = jnp.broadcast_to(qkv_bias[None], (8, 3 * part))
    infos = []
    inputs = []
    sequence = []
    pieces = []
    for m in range(micro):
        infos.append(jnp.concatenate([me[None], doc_starts[m, 0], rank[None] % 2]))
        if m == 0:
            parts = (head_first,) + tuple(v[None] for v in head_got)
            picks = (0, 0, 0, 0)
        else:
            parts = (hidden_in.reshape(micro, rows, model_width), across, along, corner[m - 1])
            picks = (m, m - 1, m - 1, 0)
        inputs.append((parts, picks))
        qkv, out, lse = attention_forward(infos[m], parts, picks, w_own, bias_rows, docs)
        sequence.append((qkv, lse))
        pieces.append(exchange(out).reshape(model_width, rows))
    heads_out = jnp.concatenate(pieces, axis=1)
    stream = jnp.concatenate(streams, axis=0)

    first_sum = stream.astype(f32) + mm(heads_out, w_out_all, ((0,), (0,))) + bias_all[2]
    normed, normal_one, inverse_one = layer_norm_parts(first_sum, gains[0], shifts[0])
    normed_low = normed.astype(bf16)
    inner_act = mm(normed_low, w_in_all) + inner_bias[0]
    activated, slope = gelu_parts(inner_act)
    activated = activated.astype(bf16)
    activated, slope = tie(activated, slope.astype(bf16))
    second_sum = normed + mm(activated, w_last_all) + bias_all[3]
    result, normal_two, inverse_two = layer_norm_parts(second_sum, gains[1], shifts[1])

    grad_rows = jnp.concatenate([out_grad[m, 0] for m in range(micro)], axis=0).astype(f32)
    d_second = norm_backward(grad_rows, normal_two, inverse_two, gains[1])
    g_gain_two = jnp.sum(grad_rows * normal_two, axis=0)
    g_shift_two = jnp.sum(grad_rows, axis=0)
    d_ff_out = d_second.astype(bf16)
    g_bias_out = jnp.sum(d_ff_out.astype(f32), axis=0)
    g_w_ff_out = mm(activated, d_ff_out, ((0,), (0,))).astype(bf16)
    d_ff_out, g_w_ff_out = tie(d_ff_out, g_w_ff_out)
    last = lax.psum_scatter(g_w_ff_out, "fsdp", scatter_dimension=0, tiled=True)
    d_inner = (mm(d_ff_out, w_last_all, ((1,), (1,))) * slope.astype(f32)).astype(bf16)
    g_ff_in_bias = jnp.sum(d_inner.astype(f32), axis=0)
    g_w_ff_in = mm(normed_low, d_inner, ((0,), (0,))).astype(bf16)
    d_inner, g_w_ff_in = tie(d_inner, g_w_ff_in)
    inside = lax.psum_scatter(g_w_ff_in, "fsdp", scatter_dimension=0, tiled=True)

    d_normed = d_second + mm(d_inner, w_in_all, ((1,), (1,)))
    d_first = norm_backward(d_normed, normal_one, inverse_one, gains[0])
    g_gain_one = jnp.sum(d_normed * normal_one, axis=0)
    g_shift_one = jnp.sum(d_normed, axis=0)
    d_branch = d_first.astype(bf16)
    g_bias_attn = jnp.sum(d_branch.astype(f32), axis=0)
    small_grads = jnp.concatenate(
        [
            v.reshape(-1, shards, v.shape[-1] // shards).transpose(1, 0, 2).reshape(shards, -1)
            for v in (
                jnp.stack([g_bias_attn, g_bias_out]),
                g_ff_in_bias[None],
                jnp.stack([g_gain_one, g_gain_two]),
                jnp.stack([g_shift_one, g_shift_two]),
            )
        ],
        axis=1,
    ).astype(bf16)
    small_count = small_grads.shape[1]
    depth = model_width // shards
    small_rows = 16 * -(-small_count // (16 * model_width))
    small_grads = jnp.pad(small_grads, ((0, 0), (0, small_rows * model_width - small_count)))
    first_heads, rest_heads, tail = heads_backward(
        d_branch,
        heads_out,
        w_pair,
        inner_width // model_width,
        small_grads.reshape(shards, small_rows, model_width),
        rows,
    )
    d_mixed = [exchange(first_heads)]
    rest_heads, d_mixed[0] = tie(rest_heads, d_mixed[0])
    d_mixed.append(exchange(rest_heads))
    tail = lax.psum_scatter(tail, "fsdp", scatter_dimension=0)
    sums = []
    own = None
    for m in range(micro):
        qkv, lse = sequence[m]
        parts, picks = inputs[m]
        d_x, *own = attention_backward(
            infos[m],
            qkv,
            d_mixed[min(m, 1)],
            max(m - 1, 0),
            lse,
            parts,
            picks,
            w_own,
            own,
            docs,
            shards if m + 1 == micro else 0,
        )
        if m == 0:
            own[0], last, d_mixed[1] = tie(own[0], last, d_mixed[1])
            last_got = from_peer(last, 1)
        elif m == 1:
            own[0], last_got, inside, sums[0] = tie(own[0], last_got, inside, sums[0])
            last = add_sent(last, last_got)
            last_got = from_peer(last, 2)
            inside_got = from_peer(inside, 1)
        elif m == 2:
            own_got = from_core(own[1])
            own[0], last_got, inside_got, sums[1] = tie(
                own[0], last_got, inside_got, sums[1]
            )
            inside = add_sent(inside, inside_got)
            inside_got = from_peer(inside, 2)
        sums.append(exchange(d_x))
    own_sum, *own_sent = core_add(rank[None] // 2, own[0], own_got)
    own_got = tuple(along_chips(v, k + 1) for k, v in enumerate(own_sent))
    own_sum, tail = tie(own_sum, tail)
    tail_got = from_peer(tail, 1)
    own_kept = line_sum(own_sum, own_got)
    pieces = (own_kept,) + tuple(from_peer(own_kept, j) for j in (1, 2, 3))
    own_kept, tail_got = tie(own_kept, tail_got)
    tail = add_sent(tail, tail_got)
    tail_got = from_peer(tail, 2)
    in_grad = d_first + jnp.concatenate(
        [jnp.sum(v.astype(f32), axis=0) for v in sums], axis=0
    )
    in_grad = in_grad.astype(bf16)
    g_in = inside.astype(f32) + inside_got.astype(f32)
    pieces, g_in, in_grad = tie(pieces, g_in, in_grad)
    g_qkv, both = join_columns(me[None], pieces, depth)
    g_qkv, tail_got = tie(g_qkv, tail_got)
    both = both[0].reshape(3, model_width)
    own_shard = lax.axis_index("fsdp") * proj_bias.shape[1]
    both = lax.dynamic_slice_in_dim(both, own_shard, proj_bias.shape[1], 1)
    g_last = last.astype(f32) + last_got.astype(f32)
    tail = tail.astype(f32) + tail_got.astype(f32)
    g_out = tail[: w_attn_out.shape[0]]
    flat = tail[w_attn_out.shape[0] :].reshape(-1)
    narrow = proj_bias.shape[1]
    bias_pair = flat[: 2 * narrow].reshape(2, narrow)
    at = 2 * narrow
    inner_bias_grad = flat[at : at + ff_in_bias.shape[0]]
    at += ff_in_bias.shape[0]
    gain_grad = flat[at : at + 2 * narrow].reshape(2, narrow)
    at += 2 * narrow
    shift_grad = flat[at : at + 2 * narrow].reshape(2, narrow)
    bias_grad = jnp.concatenate([both[0:1], both[2:3], bias_pair], axis=0)
    return (
        result.astype(bf16).reshape(out_grad.shape),
        in_grad.astype(bf16).reshape(hidden_in.shape),
        g_qkv,
        g_out,
        g_in,
        g_last,
        bias_grad,
        inner_bias_grad,
        gain_grad,
        shift_grad,
    )


def solution(mesh):
    plane = mesh.shape["ctx"] == 4 and mesh.shape["fsdp"] == 8
    return jax.shard_map(
        on_plane if plane else on_device,
        mesh=mesh,
        in_specs=(
            P(None, "fsdp", "ctx", None),
            P(None, "fsdp", None),
            P("fsdp", None),
            P("fsdp", None),
            P("fsdp", None),
            P("fsdp", None),
            P(None, "fsdp"),
            P("fsdp"),
            P(None, "fsdp"),
            P(None, "fsdp"),
            P(None, "fsdp", "ctx", None),
        ),
        out_specs=(
            P(None, "fsdp", "ctx", None),
            P(None, "fsdp", "ctx", None),
            P("fsdp", None),
            P("fsdp", None),
            P("fsdp", None),
            P("fsdp", None),
            P(None, "fsdp"),
            P("fsdp"),
            P(None, "fsdp"),
            P(None, "fsdp"),
        ),
        check_vma=False,
    )
```
